32 devices in a mesh: dp: 8 (over y, x, core), head: 4 (over z).
Axes of the slice: x: 2, y: 2, z: 4, core: 2. Of those that a mesh axis runs over, the one named last changes fastest.
Arguments:
- tokens: bfloat16 [16384, 1024], P(('dp', 'head')), may hold values from -6 to 6
- first_values: bfloat16 [16384, 1024], P('dp', 'head'), may hold values from -6 to 6
- mixer_in: float32 [3, 1024, 1024], P(None, 'dp', 'head'), may hold values from -0.1875 to 0.1875
- mixer_out: float32 [1024, 1024], P('head', 'dp'), may hold values from -0.75 to 0.75
- gate_up: float32 [2, 1024, 2816], P(None, 'dp', 'head'), may hold values from -0.1875 to 0.1875
- down_weight: float32 [2816, 1024], P('head', 'dp'), may hold values from -0.109375 to 0.109375
- norm_gains: float32 [2, 1024], P(None, 'dp'), may hold values from 0.5 to 1.5
- lengths: int32 [8], P('dp'), may hold values from 128 to 2048, as said below
- cotangent: bfloat16 [16384, 1024], P(('dp', 'head')), may hold values from -6 to 6
Outputs:
- block_out: bfloat16 [16384, 1024], P(('dp', 'head'))
- tokens_grad: float32 [16384, 1024], P(('dp', 'head'))
- first_grad: float32 [16384, 1024], P('dp', 'head')
- mixer_in_grad: float32 [3, 1024, 1024], P(None, 'dp', 'head')
- mixer_out_grad: float32 [1024, 1024], P('head', 'dp')
- gate_up_grad: float32 [2, 1024, 2816], P(None, 'dp', 'head')
- down_grad: float32 [2816, 1024], P('head', 'dp')
- gains_grad: float32 [2, 1024], P(None, 'dp')
The draws below stay inside these ranges and needn't reach their ends.
Inputs may be any that keep to these rules, and one draw needn't show every extreme that they name: `lengths`: positions from a sequence's length on are padding; some sequence has exactly 2048 real tokens in every draw.
All inputs are finite; a program needn't handle non-finite values.
Results may differ from the reference program's by a relative error of at most 0.013.
The reference program's roundings to bfloat16 on the way count: a program that leaves them out, or rounds other values in their place, can miss the bound.
Values may be sent and summed in bfloat16 or wider, within the bound.
No kernel may reach another device: no remote copies, remote signals or barrier semaphores. Data moves between devices by JAX's collectives and lax.ppermute only.
A program may use at most 128 MiB of HBM per device.

```python
import jax
import jax.numpy as jnp
from jax import lax

D = 1024
HEADS = 16
HDIM = 64
FF = 2816
SEQ = 2048
MIN_LEN = 128
SEQS = 8
TOKENS = 16384


def draw_lengths(key, part):
    levels = (SEQ // MIN_LEN).bit_length() - 1
    key_level, key_extra, key_top = jax.random.split(key, 3)
    level = jax.random.randint(key_level, (SEQS,), 0, levels + 1)
    base = MIN_LEN * jnp.left_shift(jnp.ones((SEQS,), jnp.int32), level.astype(jnp.int32))
    extra = jax.random.randint(key_extra, (SEQS,), 0, base)
    drawn = jnp.minimum(base + extra, SEQ)
    chosen = jax.random.randint(key_top, (), 0, SEQS)
    return jnp.where(jnp.arange(SEQS) == chosen, SEQ, drawn).astype(jnp.int32)


def block_scale(rng, dims, cuts, least, top_value):
    loudness, own = 1.0, jax.random.fold_in(rng, 6)
    for dim, parts in cuts:
        steps = jnp.exp(jax.random.uniform(jax.random.fold_in(own, dim), (parts,), jnp.float32, least / len(cuts), top_value / len(cuts)))
        loudness = loudness * jnp.repeat(steps, dims[dim] // parts).reshape([-1 if axis == dim else 1 for axis in range(len(dims))])
    return loudness


def noise(rng, dims, spread, bound, cuts=(), held_as=jnp.bfloat16):
    factor_of = block_scale(rng, dims, cuts, -0.22, 0.18) if cuts else 1.0
    values = jax.random.normal(rng, dims, jnp.float32) * spread * factor_of
    return jnp.minimum(jnp.maximum(values, -bound), bound).astype(held_as)


def setup_inputs(seed: int = 0) -> dict:
    seeds = jax.random.split(jax.random.key(seed), 10)
    tokens = noise(seeds[0], (TOKENS, D), 1.0, 6.0, ((0, 32),))
    first_values = noise(seeds[1], (TOKENS, D), 1.0, 6.0, ((0, 8), (1, 4)))
    mixer_in = noise(seeds[2], (3, D, D), D ** -0.5, 0.1875, ((1, 8), (2, 4)), jnp.float32)
    mixer_out = noise(seeds[3], (D, D), (D // 16) ** -0.5, 0.75, ((0, 4), (1, 8)), jnp.float32)
    gate_up = noise(seeds[4], (2, D, FF), D ** -0.5, 0.1875, ((1, 8), (2, 4)), jnp.float32)
    down_weight = noise(seeds[5], (FF, D), FF ** -0.5, 0.109375, ((0, 4), (1, 8)), jnp.float32)
    norm_gains = jnp.clip(1.0 + 0.1 * jax.random.normal(seeds[6], (2, D), jnp.float32), 0.5, 1.5)
    lengths = draw_lengths(jax.random.fold_in(seeds[9], 71), 0)
    cotangent = noise(seeds[8], (TOKENS, D), 1.0, 6.0, ((0, 32),))
    return dict(tokens=tokens, first_values=first_values, mixer_in=mixer_in, mixer_out=mixer_out, gate_up=gate_up, down_weight=down_weight, norm_gains=norm_gains, lengths=lengths, cotangent=cotangent)


@jax.custom_vjp
def low(v):
    return lax.optimization_barrier(v.astype(jnp.bfloat16)).astype(jnp.float32)

@jax.custom_vjp
def low_back(v):
    return v

def low_keep(v):
    return (low(v), None)

def low_pass(kept, grad):
    return (grad,)

def back_keep(v):
    return (v, None)

def back_low(kept, grad):
    return (low(grad),)
low.defvjp(low_keep, low_pass)
low_back.defvjp(back_keep, back_low)
epsilon = 1e-05
far_below = -1e+30
rope_base = 10000.0

def rope_tables():
    half = HDIM // 2
    rates = rope_base ** (-jnp.arange(half, dtype=jnp.float32) * 2.0 / HDIM)
    angles = jnp.arange(SEQ, dtype=jnp.float32)[:, None] * rates[None, :]
    return (jnp.cos(angles)[:, None, :], jnp.sin(angles)[:, None, :])

def rotate(field, cosine, sine):
    half = field.shape[-1] // 2
    first = field[..., :half]
    second = field[..., half:]
    return jnp.concatenate([first * cosine - second * sine, second * cosine + first * sine], axis=-1)

def rms(field, gain):
    return field * lax.rsqrt(lax.optimization_barrier(jnp.mean(field * field, axis=-1, keepdims=True)) + epsilon) * gain

def attend(item):
    query, keys, values, valid_row = item
    highest = lax.Precision.HIGHEST
    raw = low_back(jnp.einsum('qhe,khe->hqk', query, keys, precision=highest))
    places = jnp.arange(SEQ)
    allowed = (places[None, :] <= places[:, None]) & (valid_row[None, :] > 0.5)
    scores = jnp.where(allowed[None], raw * HDIM ** (-0.5), far_below)
    probs = low(jax.nn.softmax(scores, axis=-1))
    result = jnp.einsum('hqk,khe->qhe', probs, values, precision=highest)
    return result * valid_row[:, None, None]

def forward(tokens, first_values, mixer_in, mixer_out, gate_up, down_weight, norm_gains, valid):
    highest = lax.Precision.HIGHEST
    mixer_in = low(mixer_in)
    mixer_out = low(mixer_out)
    gate_up = low(gate_up)
    down_weight = low(down_weight)
    norm_gains = low(norm_gains)
    normed_a = low(rms(tokens, norm_gains[0]))
    mixed = low_back(jnp.einsum('td,kdc->ktc', normed_a, mixer_in, precision=highest))
    cosine, sine = rope_tables()
    shape_four = (SEQS, SEQ, HEADS, HDIM)
    query = low(rotate(mixed[0].reshape(shape_four), cosine, sine))
    keys = low(rotate(mixed[1].reshape(shape_four), cosine, sine))
    values = low(0.5 * mixed[2] + 0.5 * first_values).reshape(shape_four)
    attended = lax.map(jax.checkpoint(attend), (query, keys, values, valid))
    attended = low_back(low(attended.reshape(TOKENS, D)))
    branch_a = low_back(jnp.dot(attended, mixer_out, precision=highest))
    hidden_state = tokens + branch_a
    normed_b = low(rms(hidden_state, norm_gains[1]))
    gates = low_back(jnp.einsum('td,kdf->ktf', normed_b, gate_up, precision=highest))
    inner = low(jax.nn.silu(gates[0]) * gates[1])
    branch_b = low_back(jnp.dot(inner, down_weight, precision=highest))
    return hidden_state + branch_b

def reference(tokens, first_values, mixer_in, mixer_out, gate_up, down_weight, norm_gains, lengths, cotangent):
    places = jnp.arange(SEQ).astype(jnp.int32)
    valid = (places[None, :] < lengths[:, None].astype(jnp.int32)).astype(jnp.float32)
    primals = (tokens.astype(jnp.float32), first_values.astype(jnp.float32), mixer_in, mixer_out, gate_up, down_weight, norm_gains)
    result, pullback = jax.vjp(lambda *inputs: forward(*inputs, valid), *primals)
    grads = pullback(cotangent.astype(jnp.float32))
    return (result.astype(jnp.bfloat16), grads[0], grads[1], grads[2], grads[3], grads[4], grads[5], grads[6])
```

```python
import functools

import jax
import jax.numpy as jnp
from jax import lax
from jax.experimental import pallas as pl
from jax.experimental.pallas import tpu as pltpu
from jax.sharding import PartitionSpec as P

HDIM = 64
SEQ = 2048
LANES = 128
GAIN_ROWS = 16

epsilon = 1e-05
far_below = -1e30
rope_base = 10000.0
low = jnp.bfloat16
wide = jnp.float32
VMEM_BYTES = 60 * 1024 * 1024


def dot_nn(a, b):
    return lax.dot_general(a, b, (((1,), (0,)), ((), ())), preferred_element_type=wide)


def dot_nt(a, b):
    return lax.dot_general(a, b, (((1,), (1,)), ((), ())), preferred_element_type=wide)


def dot_tn(a, b):
    return lax.dot_general(a, b, (((0,), (0,)), ((), ())), preferred_element_type=wide)


def rope_tables():
    half = HDIM // 2
    rates = rope_base ** (-jnp.arange(half, dtype=wide) * 2.0 / HDIM)
    angles = jnp.arange(SEQ, dtype=wide)[:, None] * rates[None, :]
    cosine, sine = jnp.cos(angles), jnp.sin(angles)
    pair = LANES // HDIM
    return (
        jnp.concatenate([cosine, cosine] * pair, axis=1),
        jnp.concatenate([-sine, sine] * pair, axis=1),
    )


def swap_halves(field):
    half = HDIM // 2
    lane = lax.broadcasted_iota(jnp.int32, field.shape, 1)
    ahead = pltpu.roll(field, LANES - half, 1)
    behind = pltpu.roll(field, half, 1)
    return jnp.where(lane % HDIM < half, ahead, behind)


def rms_parts(field, gain):
    factor = lax.rsqrt(jnp.mean(field * field, axis=-1, keepdims=True) + epsilon)
    unit = field * factor
    return (unit * gain, unit, factor)


def rms_back(normed_grad, unit, factor, gain):
    scaled = normed_grad * gain
    return factor * (scaled - unit * jnp.mean(scaled * unit, axis=-1, keepdims=True))


def project_kernel(place, x_ref, w_ref, gain_ref, first_ref, cos_ref, sin_ref, q_ref, k_ref, v_ref):
    x = x_ref[0].astype(wide)
    gain = gain_ref[0:1, :].astype(wide)
    normed = rms_parts(x, gain)[0].astype(low)
    cols = q_ref.shape[1]
    cosine, sine = cos_ref[...], sin_ref[...]
    for part, out_ref in ((0, q_ref), (1, k_ref)):
        mixed = dot_nt(normed, w_ref[part * cols : (part + 1) * cols, :])
        for start in range(0, cols, LANES):
            piece = mixed[:, start : start + LANES]
            out_ref[:, start : start + LANES] = (
                piece * cosine + swap_halves(piece) * sine
            ).astype(low)
    mixed = dot_nt(normed, w_ref[2 * cols : 3 * cols, :])
    v_ref[...] = (0.5 * mixed + 0.5 * first_ref[...].astype(wide)).astype(low)


def project(place, x_turned, pack, first_values, cosine, sine):
    count, rows, depth = x_turned.shape
    cols = first_values.shape[1]
    gain_block = pack.shape[0] // GAIN_ROWS - 1
    natural = lambda o, p: ((p[0] + o) % count, 0)
    spec = pltpu.PrefetchScalarGridSpec(
        num_scalar_prefetch=1,
        grid=(count,),
        in_specs=[
            pl.BlockSpec((1, rows, depth), lambda o, p: (o, 0, 0)),
            pl.BlockSpec((3 * cols, depth), lambda o, p: (0, 0)),
            pl.BlockSpec((GAIN_ROWS, depth), lambda o, p: (gain_block, 0)),
            pl.BlockSpec((rows, cols), natural),
            pl.BlockSpec((rows, LANES), natural),
            pl.BlockSpec((rows, LANES), natural),
        ],
        out_specs=[pl.BlockSpec((rows, cols), natural)] * 3,
    )
    return pl.pallas_call(
        project_kernel,
        grid_spec=spec,
        out_shape=[jax.ShapeDtypeStruct((count * rows, cols), low)] * 3,
        compiler_params=pltpu.CompilerParams(vmem_limit_bytes=VMEM_BYTES),
        cost_estimate=pl.CostEstimate(
            flops=2 * count * rows * depth * 3 * cols, bytes_accessed=10 << 20, transcendentals=0
        ),
        name="project",
    )(place, x_turned, pack, pack, first_values, cosine, sine)


BLOCK = 512


def allowed_rows(i, j, length):
    q_at = i * BLOCK + lax.broadcasted_iota(jnp.int32, (BLOCK, BLOCK), 0)
    k_at = j * BLOCK + lax.broadcasted_iota(jnp.int32, (BLOCK, BLOCK), 1)
    return (k_at <= q_at) & (k_at < length)


def attend_kernel(len_ref, q_ref, k_ref, v_ref, out_ref, full_ref, lse_ref, acc_ref, max_ref, sum_ref):
    i = pl.program_id(1)
    length = len_ref[0]
    lane = lax.broadcasted_iota(jnp.int32, (BLOCK, LANES), 1)
    query = q_ref[...] * jnp.asarray(HDIM**-0.5, low)
    blocks = jnp.where(i * BLOCK < length, jnp.minimum(i + 1, pl.cdiv(length, BLOCK)), 0)
    plain = jnp.minimum(blocks, jnp.minimum(i, length // BLOCK))
    valid = i * BLOCK + lax.broadcasted_iota(jnp.int32, (BLOCK, 1), 0) < length
    results = []
    for head in range(LANES // HDIM):
        own = jnp.where(lane // HDIM == head, query, jnp.zeros_like(query))
        max_ref[...] = jnp.full_like(max_ref, far_below)
        sum_ref[...] = jnp.zeros_like(sum_ref)
        acc_ref[...] = jnp.zeros_like(acc_ref)

        def step(j, masked, own=own):
            at = pl.ds(pl.multiple_of(j * BLOCK, BLOCK), BLOCK)
            scores = dot_nt(own, k_ref[at, :])
            if masked:
                scores = jnp.where(allowed_rows(i, j, length), scores, far_below)
            old = max_ref[...]
            peak = jnp.maximum(old, jnp.max(scores, axis=1, keepdims=True))
            powers = jnp.exp(scores - peak[:, 0:1])
            decay = jnp.exp(old - peak)
            max_ref[...] = peak
            sum_ref[...] = sum_ref[...] * decay + jnp.sum(powers, axis=1, keepdims=True)
            acc_ref[...] = acc_ref[...] * decay + dot_nn(powers.astype(low), v_ref[at, :])

        @pl.loop(0, plain)
        def _(j):
            step(j, False)

        @pl.loop(plain, blocks)
        def _(j):
            step(j, True)

        total = jnp.where(valid, sum_ref[...], 1.0)
        results.append(jnp.where(valid, acc_ref[...] / total, 0.0))
        log_total = max_ref[...] + jnp.log(total)
        lse_ref[0, head : head + 1, :] = jnp.transpose(log_total)[0:1, :]
    result = jnp.where(lane < HDIM, results[0], results[1])
    out_ref[...] = result.astype(low)
    full_ref[...] = result


def attend(lengths, query, keys, values):
    rows, cols = query.shape
    pairs = cols // LANES
    block = pl.BlockSpec((BLOCK, LANES), lambda p, i, n: (i, p))
    whole = pl.BlockSpec((rows, LANES), lambda p, i, n: (0, p))
    spec = pltpu.PrefetchScalarGridSpec(
        num_scalar_prefetch=1,
        grid=(pairs, rows // BLOCK),
        in_specs=[block, whole, whole],
        out_specs=[block, block, pl.BlockSpec((1, 8, BLOCK), lambda p, i, n: (p, 0, i))],
        scratch_shapes=[pltpu.VMEM((BLOCK, LANES), wide)] * 3,
    )
    return pl.pallas_call(
        attend_kernel,
        grid_spec=spec,
        out_shape=[
            jax.ShapeDtypeStruct((rows, cols), low),
            jax.ShapeDtypeStruct((rows, cols), wide),
            jax.ShapeDtypeStruct((pairs, 8, rows), wide),
        ],
        compiler_params=pltpu.CompilerParams(vmem_limit_bytes=VMEM_BYTES),
        cost_estimate=pl.CostEstimate(
            flops=4 * rows * rows * cols, bytes_accessed=8 << 20, transcendentals=rows * rows * 2
        ),
        name="attend",
    )(lengths, query, keys, values)


def attend_back_kernel(
    len_ref, q_ref, k_ref, v_ref, grad_ref, full_ref, lse_ref, cos_ref, sin_ref,
    dq_ref, dk_ref, dv_ref, first_ref, dk_acc, dv_acc, dq_acc,
):
    i = pl.program_id(1)
    length = len_ref[0]

    @pl.when(i == 0)
    def _():
        dk_acc[...] = jnp.zeros_like(dk_acc)
        dv_acc[...] = jnp.zeros_like(dv_acc)

    lane = lax.broadcasted_iota(jnp.int32, (BLOCK, LANES), 1)
    query = q_ref[...] * jnp.asarray(HDIM**-0.5, low)
    grad = grad_ref[...]
    blocks = jnp.where(i * BLOCK < length, jnp.minimum(i + 1, pl.cdiv(length, BLOCK)), 0)
    plain = jnp.minimum(blocks, jnp.minimum(i, length // BLOCK))
    products = jnp.transpose(grad.astype(wide) * full_ref[...])
    dq_acc[...] = jnp.zeros_like(dq_acc)
    for head in range(LANES // HDIM):
        mine = lane // HDIM == head
        own = jnp.where(mine, query, jnp.zeros_like(query))
        own_grad = jnp.where(mine, grad, jnp.zeros_like(grad))
        log_total = lse_ref[0, head : head + 1, :]
        offset = jnp.sum(products[head * HDIM : (head + 1) * HDIM, :], axis=0, keepdims=True)

        def step(j, masked, mine=mine, own=own, own_grad=own_grad, log_total=log_total, offset=offset):
            at = pl.ds(pl.multiple_of(j * BLOCK, BLOCK), BLOCK)
            keys = k_ref[at, :]
            scores = dot_nt(keys, own)
            if masked:
                k_at = j * BLOCK + lax.broadcasted_iota(jnp.int32, (BLOCK, BLOCK), 0)
                q_at = i * BLOCK + lax.broadcasted_iota(jnp.int32, (BLOCK, BLOCK), 1)
                allowed = (k_at <= q_at) & (k_at < length)
                scores = jnp.where(allowed, scores, far_below)
            probs = jnp.exp(scores - log_total)
            prob_grad = dot_nt(v_ref[at, :], own_grad)
            dv_acc[at, :] += dot_nn(probs.astype(low), own_grad)
            raw_grad = (probs * (prob_grad - offset)).astype(low)
            dk_acc[at, :] += dot_nn(raw_grad, own)
            dq_acc[...] += dot_tn(raw_grad, jnp.where(mine, keys, jnp.zeros_like(keys)))

        @pl.loop(0, plain)
        def _(j):
            step(j, False)

        @pl.loop(plain, blocks)
        def _(j):
            step(j, True)

    at = pl.ds(pl.multiple_of(i * BLOCK, BLOCK), BLOCK)
    query_grad = dq_acc[...] * HDIM**-0.5
    dq_ref[...] = (
        query_grad * cos_ref[at, :] - swap_halves(query_grad) * sin_ref[at, :]
    ).astype(low)

    @pl.when(i == pl.num_programs(1) - 1)
    def _():
        @pl.loop(0, dk_acc.shape[0] // BLOCK)
        def _(j):
            at = pl.ds(pl.multiple_of(j * BLOCK, BLOCK), BLOCK)
            keys_grad = dk_acc[at, :]
            dk_ref[at, :] = (
                keys_grad * cos_ref[at, :] - swap_halves(keys_grad) * sin_ref[at, :]
            ).astype(low)
            half_grad = 0.5 * dv_acc[at, :]
            first_ref[at, :] = half_grad
            dv_ref[at, :] = half_grad.astype(low)


def attend_back(lengths, query, keys, values, grad, full, lse, cosine, sine):
    rows, cols = query.shape
    pairs = cols // LANES
    block = pl.BlockSpec((BLOCK, LANES), lambda p, i, n: (i, p))
    whole = pl.BlockSpec((rows, LANES), lambda p, i, n: (0, p))
    table = pl.BlockSpec((rows, LANES), lambda p, i, n: (0, 0))
    spec = pltpu.PrefetchScalarGridSpec(
        num_scalar_prefetch=1,
        grid=(pairs, rows // BLOCK),
        in_specs=[
            block, whole, whole, block, block,
            pl.BlockSpec((1, 8, BLOCK), lambda p, i, n: (p, 0, i)),
            table, table,
        ],
        out_specs=[block, whole, whole, whole],
        scratch_shapes=[
            pltpu.VMEM((rows, LANES), wide),
            pltpu.VMEM((rows, LANES), wide),
            pltpu.VMEM((BLOCK, LANES), wide),
        ],
    )
    return pl.pallas_call(
        attend_back_kernel,
        grid_spec=spec,
        out_shape=[jax.ShapeDtypeStruct((rows, cols), low)] * 3
        + [jax.ShapeDtypeStruct((rows, cols), wide)],
        compiler_params=pltpu.CompilerParams(vmem_limit_bytes=VMEM_BYTES),
        cost_estimate=pl.CostEstimate(
            flops=10 * rows * rows * cols, bytes_accessed=12 << 20, transcendentals=rows * rows * 2
        ),
        name="attend_back",
    )(lengths, query, keys, values, grad, full, lse, cosine, sine)


def feed_kernel(x_ref, c_ref, w_ref, out_ref, grad_ref, dw_ref, inner_s, mlp_s):
    step = pl.program_id(0)
    pieces, _, depth3, width = w_ref.shape
    units = depth3 // 3
    tokens = x_ref.shape[0]
    chunk = 256

    @pl.when(step == 0)
    def _():
        out_ref[...] = jnp.zeros_like(out_ref)
        grad_ref[...] = jnp.zeros_like(grad_ref)

    @pl.loop(0, tokens // chunk)
    def _(t):
        at = pl.ds(pl.multiple_of(t * chunk, chunk), chunk)
        gated = jnp.zeros((2 * units, chunk), wide)
        inner_grad = jnp.zeros((units, chunk), wide)
        for c in range(pieces):
            cols = slice(c * width, (c + 1) * width)
            gated += dot_nt(w_ref[c, 0, : 2 * units, :], x_ref[at, cols])
            inner_grad += dot_nt(w_ref[c, 0, 2 * units :, :], c_ref[at, cols])
        gate, up = gated[:units], gated[units:]
        sigmoid = jax.nn.sigmoid(gate)
        silu = gate * sigmoid
        inner = (silu * up).astype(low)
        gate_grad = (inner_grad * up * sigmoid * (1.0 + gate * (1.0 - sigmoid))).astype(low)
        up_grad = (inner_grad * silu).astype(low)
        inner_s[:, at] = inner
        mlp_s[:units, at] = gate_grad
        mlp_s[units:, at] = up_grad
        mlp_grad = jnp.concatenate([gate_grad, up_grad], axis=0)
        for c in range(pieces):
            cols = slice(c * width, (c + 1) * width)
            out_ref[at, cols] += dot_tn(inner, w_ref[c, 0, 2 * units :, :])
            grad_ref[at, cols] += dot_tn(mlp_grad, w_ref[c, 0, : 2 * units, :])

    for c in range(pieces):
        cols = slice(c * width, (c + 1) * width)
        dw_ref[c, 0, : 2 * units, :] = dot_nn(mlp_s[...], x_ref[:, cols]).astype(low)
        dw_ref[c, 0, 2 * units :, :] = dot_nn(inner_s[...], c_ref[:, cols]).astype(low)


def feed(x, cotangent, weights):
    tokens, depth = x.shape
    pieces, parts, rows, width = weights.shape
    units = rows // 3
    fixed = lambda h: (0, 0)
    once = pl.Buffered(1)
    activations = pl.BlockSpec((tokens, depth), fixed, pipeline_mode=once)
    block = pl.BlockSpec((pieces, 1, rows, width), lambda h: (0, h, 0, 0))
    return pl.pallas_call(
        feed_kernel,
        grid=(parts,),
        in_specs=[activations, activations, block],
        out_specs=[activations, activations, block],
        out_shape=[
            jax.ShapeDtypeStruct((tokens, depth), wide),
            jax.ShapeDtypeStruct((tokens, depth), wide),
            jax.ShapeDtypeStruct(weights.shape, low),
        ],
        scratch_shapes=[pltpu.VMEM((units, tokens), low), pltpu.VMEM((2 * units, tokens), low)],
        compiler_params=pltpu.CompilerParams(vmem_limit_bytes=VMEM_BYTES),
        cost_estimate=pl.CostEstimate(
            flops=18 * tokens * depth * units * parts,
            bytes_accessed=30 << 20,
            transcendentals=tokens * units * parts,
        ),
        name="feed",
    )(x, cotangent, weights)


def unproject_kernel(place, x_ref, w_ref, gain_ref, dq_ref, dk_ref, dv_ref, part_ref, dw_ref, gain_grad_ref, acc_ref):
    step = pl.program_id(0)
    cols = dq_ref.shape[1]

    @pl.when(step == 0)
    def _():
        acc_ref[...] = jnp.zeros_like(acc_ref)
        gain_grad_ref[...] = jnp.zeros_like(gain_grad_ref)

    x = x_ref[0].astype(wide)
    normed, unit, _ = rms_parts(x, gain_ref[0:1, :].astype(wide))
    normed = normed.astype(low)
    part = jnp.zeros(x.shape, wide)
    for number, ref in enumerate((dq_ref, dk_ref, dv_ref)):
        rows = slice(number * cols, (number + 1) * cols)
        part += dot_nn(ref[...], w_ref[rows, :])
        acc_ref[rows, :] += dot_tn(ref[...], normed)
    part_ref[...] = part.astype(low)
    gain_grad_ref[0:1, :] += jnp.sum(part * unit, axis=0, keepdims=True)

    @pl.when(step == pl.num_programs(0) - 1)
    def _():
        dw_ref[...] = acc_ref[...].astype(low)


def unproject(place, x_turned, pack, dq, dk, dv):
    count, rows, depth = x_turned.shape
    cols = dq.shape[1]
    gain_block = pack.shape[0] // GAIN_ROWS - 1
    natural = pl.BlockSpec((rows, cols), lambda o, p: ((p[0] + o) % count, 0))
    spec = pltpu.PrefetchScalarGridSpec(
        num_scalar_prefetch=1,
        grid=(count,),
        in_specs=[
            pl.BlockSpec((1, rows, depth), lambda o, p: (o, 0, 0)),
            pl.BlockSpec((3 * cols, depth), lambda o, p: (0, 0)),
            pl.BlockSpec((GAIN_ROWS, depth), lambda o, p: (gain_block, 0)),
            natural, natural, natural,
        ],
        out_specs=[
            pl.BlockSpec((rows, depth), lambda o, p: ((p[0] + o) % count, 0)),
            pl.BlockSpec((3 * cols, depth), lambda o, p: (0, 0)),
            pl.BlockSpec((8, depth), lambda o, p: (0, 0)),
        ],
        scratch_shapes=[pltpu.VMEM((3 * cols, depth), wide)],
    )
    return pl.pallas_call(
        unproject_kernel,
        grid_spec=spec,
        out_shape=[
            jax.ShapeDtypeStruct((count * rows, depth), low),
            jax.ShapeDtypeStruct((3 * cols, depth), low),
            jax.ShapeDtypeStruct((8, depth), wide),
        ],
        compiler_params=pltpu.CompilerParams(vmem_limit_bytes=VMEM_BYTES),
        cost_estimate=pl.CostEstimate(
            flops=4 * count * rows * depth * 3 * cols, bytes_accessed=16 << 20, transcendentals=0
        ),
        name="unproject",
    )(place, x_turned, pack, pack, dq, dk, dv)


def ring_gather(block, place, count):
    rightward = [(k, k + 1) for k in range(count - 1)]
    leftward = [(k + 1, k) for k in range(count - 1)]
    right = left = block
    from_left, from_right = {}, {}
    for hop in range(1, count):
        right = lax.ppermute(right, "head", rightward)
        left = lax.ppermute(left, "head", leftward)
        from_left[hop] = right
        from_right[hop] = left
    slots = [block]
    for ahead in range(1, count):
        inside = place + ahead < count
        slots.append(jnp.where(inside, from_right[ahead], from_left[count - ahead]))
    return jnp.stack(slots)


def ring_scatter(parts, place, count):
    zero = jnp.zeros(parts.shape[1:], parts.dtype)
    right = left = zero
    for hop in range(1, count):
        to_right = jnp.minimum(place + count - hop, count - 1)
        to_left = jnp.maximum(place - count + hop, 0)
        right = right + lax.dynamic_index_in_dim(parts, to_right, 0, keepdims=False)
        left = left + lax.dynamic_index_in_dim(parts, to_left, 0, keepdims=False)
        right = lax.ppermute(right, "head", [(k, k + 1) for k in range(min(hop, count - 1))])
        left = lax.ppermute(
            left, "head", [(k, k - 1) for k in range(count - 1, max(count - 1 - hop, 0), -1)]
        )
    own = lax.dynamic_index_in_dim(parts, place, 0, keepdims=False)
    return own.astype(wide) + right.astype(wide) + left.astype(wide)


def other_core(array):
    return lax.ppermute(array, "core", [(0, 1), (1, 0)])


def shards(
    tokens, first_values, mixer_in, mixer_out, gate_up, down_weight, norm_gains, lengths, cotangent
):
    line = lax.axis_size("head")
    chips = lax.axis_size("chip")
    place = lax.axis_index("head")
    core = lax.axis_index("core")
    rows, depth = tokens.shape
    cols = mixer_in.shape[2]
    width = mixer_in.shape[1]
    units = down_weight.shape[0] // 2
    place_one = place[None].astype(jnp.int32)

    x_turned = ring_gather(tokens, place, line)
    cot_pair = jnp.concatenate([cotangent, other_core(cotangent)], axis=0)

    qkv_rows = mixer_in.astype(low).transpose(0, 2, 1).reshape(3 * cols, width)
    out_rows = lax.all_gather(mixer_out.astype(low), "head", axis=0, tiled=True)
    gain_rows = jnp.pad(norm_gains.astype(low), ((0, GAIN_ROWS - 2), (0, 0)))
    pack = lax.all_gather(
        jnp.concatenate([qkv_rows, out_rows, gain_rows], axis=0),
        ("chip", "core"),
        axis=1,
        tiled=True,
    )
    out_full = pack[3 * cols : 3 * cols + depth]
    gain_second = pack[3 * cols + depth + 1].astype(wide)
    gain_first = pack[3 * cols + depth].astype(wide)

    feed_rows = jnp.concatenate(
        [gate_up.astype(low).transpose(0, 2, 1), down_weight.astype(low)[None]], axis=0
    ).reshape(3, 2, units, width)
    own_half = jnp.where(core == 0, feed_rows[:, 0], feed_rows[:, 1])
    other_half = jnp.where(core == 0, feed_rows[:, 1], feed_rows[:, 0])
    came = other_core(other_half)
    feed_rows = jnp.where(
        core == 0,
        jnp.concatenate([own_half, came], axis=-1),
        jnp.concatenate([came, own_half], axis=-1),
    ).reshape(3 * units, 2 * width)
    feed_full = lax.all_gather(feed_rows, ("chip", "head"), axis=0)
    feed_full = feed_full.reshape(chips, line, 3 * units, 2 * width)
    lined = (2 * width) % LANES == 0
    if not lined:
        feed_full = feed_full.transpose(1, 2, 0, 3).reshape(1, line, 3 * units, depth)

    cosine, sine = rope_tables()
    query, keys, values = project(place_one, x_turned, pack, first_values, cosine, sine)
    attended_heads, attended_wide, log_total = attend(lengths, query, keys, values)
    attended = lax.all_to_all(attended_heads, "head", split_axis=0, concat_axis=1, tiled=True)

    token_rows = tokens.astype(wide)
    hidden_state = token_rows + dot_nn(attended, out_full)
    normed_b, unit_b, factor_b = rms_parts(hidden_state, gain_second)
    normed_b = normed_b.astype(low)
    normed_pair = jnp.concatenate([normed_b, other_core(normed_b)], axis=0)
    branch_pair, normed_b_grad_pair, feed_grad = feed(normed_pair, cot_pair, feed_full)
    branch_b = branch_pair[:rows] + other_core(branch_pair[rows:])
    normed_b_grad = normed_b_grad_pair[:rows] + other_core(normed_b_grad_pair[rows:])
    block_out = (hidden_state + branch_b).astype(low)

    if not lined:
        feed_grad = feed_grad.reshape(line, 3 * units, chips, 2 * width).transpose(2, 0, 1, 3)
    feed_grad = lax.psum_scatter(feed_grad, "chip", scatter_dimension=0)
    feed_grad = lax.psum_scatter(feed_grad, "head", scatter_dimension=0)
    own_cols = jnp.where(core == 0, feed_grad[:, :width], feed_grad[:, width:])
    came = other_core(jnp.where(core == 0, feed_grad[:, width:], feed_grad[:, :width]))
    own_cols = own_cols.reshape(3, 1, units, width)
    came = came.reshape(3, 1, units, width)
    feed_grad = jnp.where(
        core == 0,
        jnp.concatenate([own_cols, came], axis=1),
        jnp.concatenate([came, own_cols], axis=1),
    ).reshape(3, 2 * units, width)
    gate_up_grad = feed_grad[:2].transpose(0, 2, 1).astype(wide)
    down_grad = feed_grad[2].astype(wide)

    state_part = rms_back(normed_b_grad, unit_b, factor_b, gain_second)
    gain_b_grad = jnp.sum(normed_b_grad * unit_b, axis=0)
    state_grad = cotangent.astype(wide) + state_part
    branch_grad = state_grad.astype(low)
    out_grad = dot_tn(attended, branch_grad)
    positions = place * rows + jnp.arange(rows)
    valid = (positions < lengths[0]).astype(wide)
    attended_grad = (valid[:, None] * dot_nt(branch_grad, out_full)).astype(low)
    grad_heads = lax.all_to_all(attended_grad, "head", split_axis=1, concat_axis=0, tiled=True)
    dq, dk, dv, first_grad = attend_back(
        lengths, query, keys, values, grad_heads, attended_wide, log_total, cosine, sine
    )
    part, qkv_grad, gain_a_grad = unproject(place_one, x_turned, pack, dq, dk, dv)
    normed_a_grad = ring_scatter(part.reshape(line, rows, depth), place, line)
    _, unit_a, factor_a = rms_parts(token_rows, gain_first)
    tokens_grad = state_grad + rms_back(normed_a_grad, unit_a, factor_a, gain_first)

    gain_grads = jnp.pad(
        jnp.stack([gain_a_grad[0], gain_b_grad]).astype(low), ((0, GAIN_ROWS - 2), (0, 0))
    )
    grads = jnp.concatenate([qkv_grad, out_grad.astype(low), gain_grads], axis=0)
    grads = lax.psum_scatter(grads, ("chip", "core"), scatter_dimension=1, tiled=True)
    mixer_in_grad = grads[: 3 * cols].reshape(3, cols, width).transpose(0, 2, 1).astype(wide)
    mixer_out_grad = lax.psum_scatter(
        grads[3 * cols : 3 * cols + depth], "head", scatter_dimension=0, tiled=True
    ).astype(wide)
    gains_grad = lax.psum(grads[3 * cols + depth : 3 * cols + depth + 2].astype(wide), "head")
    return (
        block_out,
        tokens_grad,
        first_grad,
        mixer_in_grad,
        mixer_out_grad,
        gate_up_grad,
        down_grad,
        gains_grad,
    )


def solution(mesh):
    groups, line = mesh.shape["dp"], mesh.shape["head"]
    fine = jax.sharding.Mesh(
        mesh.devices.reshape(groups // 2, 2, line), ("chip", "core", "head")
    )
    dp = ("chip", "core")
    return jax.shard_map(
        shards,
        mesh=fine,
        in_specs=(
            P(("chip", "core", "head"), None),
            P(dp, "head"),
            P(None, dp, "head"),
            P("head", dp),
            P(None, dp, "head"),
            P("head", dp),
            P(None, dp),
            P(dp),
            P(("chip", "core", "head"), None),
        ),
        out_specs=(
            P(("chip", "core", "head"), None),
            P(("chip", "core", "head"), None),
            P(dp, "head"),
            P(None, dp, "head"),
            P("head", dp),
            P(None, dp, "head"),
            P("head", dp),
            P(None, dp),
        ),
        check_vma=False,
    )
```

```python
import functools

import jax
import jax.numpy as jnp
from jax import lax
from jax.experimental import pallas as pl
from jax.experimental.pallas import tpu as pltpu
from jax.sharding import PartitionSpec as P

HDIM = 64
SEQ = 2048
LANES = 128
GAIN_ROWS = 16

epsilon = 1e-05
far_below = -1e30
rope_base = 10000.0
low = jnp.bfloat16
wide = jnp.float32
VMEM_BYTES = 60 * 1024 * 1024


def dot_nn(a, b):
    return lax.dot_general(a, b, (((1,), (0,)), ((), ())), preferred_element_type=wide)


def dot_nt(a, b):
    return lax.dot_general(a, b, (((1,), (1,)), ((), ())), preferred_element_type=wide)


def dot_tn(a, b):
    return lax.dot_general(a, b, (((0,), (0,)), ((), ())), preferred_element_type=wide)


def rope_tables():
    half = HDIM // 2
    rates = rope_base ** (-jnp.arange(half, dtype=wide) * 2.0 / HDIM)
    angles = jnp.arange(SEQ, dtype=wide)[:, None] * rates[None, :]
    cosine, sine = jnp.cos(angles), jnp.sin(angles)
    pair = LANES // HDIM
    return (
        jnp.concatenate([cosine, cosine] * pair, axis=1),
        jnp.concatenate([-sine, sine] * pair, axis=1),
    )


def swap_halves(field):
    half = HDIM // 2
    lane = lax.broadcasted_iota(jnp.int32, field.shape, 1)
    ahead = pltpu.roll(field, LANES - half, 1)
    behind = pltpu.roll(field, half, 1)
    return jnp.where(lane % HDIM < half, ahead, behind)


def rms_parts(field, gain):
    factor = lax.rsqrt(jnp.mean(field * field, axis=-1, keepdims=True) + epsilon)
    unit = field * factor
    return (unit * gain, unit, factor)


def rms_back(normed_grad, unit, factor, gain):
    scaled = normed_grad * gain
    return factor * (scaled - unit * jnp.mean(scaled * unit, axis=-1, keepdims=True))


def project_kernel(place, x_ref, w_ref, gain_ref, first_ref, cos_ref, sin_ref, *refs):
    q_ref, k_ref, v_ref, normed_ref = refs[-4:]
    rows, depth = normed_ref.shape
    width = x_ref.shape[1]
    if width == depth:
        width = depth // 4
        blocks = [x_ref[:, start : start + width].astype(wide) for start in range(0, depth, width)]
    else:
        starts = range(0, x_ref.shape[0], rows)
        blocks = [x_ref[start : start + rows, :].astype(wide) for start in starts]
    squares = sum(jnp.sum(block * block, axis=-1, keepdims=True) for block in blocks)
    factor = lax.rsqrt(squares / depth + epsilon)
    for number, block in enumerate(blocks):
        cols = slice(number * width, (number + 1) * width)
        normed_ref[:, cols] = (block * factor * gain_ref[0:1, cols].astype(wide)).astype(low)
    normed = normed_ref[...]
    cosine, sine = cos_ref[...], sin_ref[...]
    for pair in range(q_ref.shape[1] // LANES):
        cols = slice(pair * LANES, (pair + 1) * LANES)
        start = pair * 3 * LANES
        mixed = dot_nt(normed, w_ref[start : start + 3 * LANES, :])
        for part, out_ref in ((0, q_ref), (1, k_ref)):
            piece = mixed[:, part * LANES : (part + 1) * LANES]
            out_ref[:, cols] = (piece * cosine + swap_halves(piece) * sine).astype(low)
        first = first_ref[:, cols].astype(wide)
        v_ref[:, cols] = (0.5 * mixed[:, 2 * LANES :] + 0.5 * first).astype(low)


def project(index, x, pack, first_values, cosine, sine, made):
    total, cols = first_values.shape
    depth = pack.shape[1]
    rows = x.shape[0] * x.shape[1] // depth
    gain_block = pack.shape[0] // GAIN_ROWS - 1
    fixed = lambda i, p: (0, 0)
    natural = lambda width: pl.BlockSpec((rows, width), lambda i, p: (p[0], 0))
    shapes = [cols, cols, cols, depth]
    spec = pltpu.PrefetchScalarGridSpec(
        num_scalar_prefetch=1,
        grid=(1,),
        in_specs=[
            pl.BlockSpec(x.shape, fixed),
            pl.BlockSpec((3 * cols, depth), fixed),
            pl.BlockSpec((GAIN_ROWS, depth), lambda i, p: (gain_block, 0)),
            natural(cols),
            natural(LANES),
            natural(LANES),
        ]
        + [pl.BlockSpec(memory_space=pl.ANY)] * len(made),
        out_specs=[natural(width) for width in shapes],
    )
    return pl.pallas_call(
        project_kernel,
        grid_spec=spec,
        out_shape=[jax.ShapeDtypeStruct((total, width), low) for width in shapes],
        input_output_aliases={7 + number: number for number in range(len(made))},
        compiler_params=pltpu.CompilerParams(vmem_limit_bytes=VMEM_BYTES),
        cost_estimate=pl.CostEstimate(
            flops=2 * rows * depth * 3 * cols, bytes_accessed=5 << 20, transcendentals=0
        ),
        name="project",
    )(index, x, pack, pack, first_values, cosine, sine, *made)


BLOCK = 512


def both_heads(array):
    lane = lax.broadcasted_iota(jnp.int32, array.shape, 1)
    zero = jnp.zeros_like(array)
    return jnp.concatenate(
        [jnp.where(lane < HDIM, array, zero), jnp.where(lane < HDIM, zero, array)], axis=0
    )


def attend_kernel(len_ref, q_ref, k_ref, v_ref, out_ref, full_ref, lse_ref, acc_ref, max_ref, sum_ref):
    i = pl.program_id(0)
    own = both_heads(q_ref[...] * jnp.asarray(HDIM**-0.5, low))
    max_ref[...] = jnp.full_like(max_ref, far_below)
    sum_ref[...] = jnp.zeros_like(sum_ref)
    acc_ref[...] = jnp.zeros_like(acc_ref)

    def step(j, diagonal):
        at = pl.ds(pl.multiple_of(j * BLOCK, BLOCK), BLOCK)
        scores = dot_nt(own, k_ref[at, :])
        if diagonal:
            q_at = lax.broadcasted_iota(jnp.int32, (BLOCK, BLOCK), 0)
            k_at = lax.broadcasted_iota(jnp.int32, (BLOCK, BLOCK), 1)
            allowed = k_at <= q_at
            allowed = jnp.concatenate([allowed, allowed], axis=0)
            scores = jnp.where(allowed, scores, far_below)
        old = max_ref[...]
        peak = jnp.maximum(old, jnp.max(scores, axis=1, keepdims=True))
        decay = jnp.exp(old - peak)
        max_ref[...] = peak
        total = sum_ref[...] * decay
        powers = []
        for start in range(0, BLOCK, LANES):
            power = jnp.exp(scores[:, start : start + LANES] - peak)
            total += power
            powers.append(power.astype(low))
        sum_ref[...] = total
        acc_ref[...] = acc_ref[...] * decay + dot_nn(jnp.concatenate(powers, axis=1), v_ref[at, :])

    @pl.loop(0, i)
    def _(j):
        step(j, False)

    step(i, True)
    total = jnp.sum(sum_ref[...], axis=1, keepdims=True)
    log_total = max_ref[...] + jnp.log(total)
    for head in range(LANES // HDIM):
        rows = slice(head * BLOCK, (head + 1) * BLOCK)
        lse_ref[head : head + 1, :] = jnp.transpose(log_total[rows])[0:1, :]
    result = acc_ref[...] / total
    lane = lax.broadcasted_iota(jnp.int32, (BLOCK, LANES), 1)
    valid = i * BLOCK + lax.broadcasted_iota(jnp.int32, (BLOCK, 1), 0) < len_ref[0]
    result = jnp.where(valid, jnp.where(lane < HDIM, result[:BLOCK], result[BLOCK:]), 0.0)
    out_ref[...] = result.astype(low)
    full_ref[...] = result


def attend(pair, lengths, query, keys, values):
    rows = query.shape[0]
    block = pl.BlockSpec((BLOCK, LANES), lambda i, n: (i, pair))
    whole = pl.BlockSpec((rows, LANES), lambda i, n: (0, pair))
    result = pl.BlockSpec((BLOCK, LANES), lambda i, n: (i, 0))
    spec = pltpu.PrefetchScalarGridSpec(
        num_scalar_prefetch=1,
        grid=(rows // BLOCK,),
        in_specs=[block, whole, whole],
        out_specs=[result, result, pl.BlockSpec((8, BLOCK), lambda i, n: (0, i))],
        scratch_shapes=[pltpu.VMEM((2 * BLOCK, LANES), wide)] * 3,
    )
    return pl.pallas_call(
        attend_kernel,
        grid_spec=spec,
        out_shape=[
            jax.ShapeDtypeStruct((rows, LANES), low),
            jax.ShapeDtypeStruct((rows, LANES), wide),
            jax.ShapeDtypeStruct((8, rows), wide),
        ],
        compiler_params=pltpu.CompilerParams(vmem_limit_bytes=VMEM_BYTES),
        cost_estimate=pl.CostEstimate(
            flops=8 * rows * rows * LANES, bytes_accessed=4 << 20, transcendentals=rows * rows
        ),
        name="attend",
    )(lengths, query, keys, values)


def attend_back_kernel(
    len_ref, q_ref, k_ref, v_ref, grad_ref, full_ref, lse_ref, cos_ref, sin_ref,
    mixed_ref, first_ref, dk_acc, dv_acc, dq_acc, keys_t,
):
    i = pl.program_id(0)
    count = pl.num_programs(0)
    heads = range(LANES // HDIM)

    @pl.when(i == 0)
    def _():
        dk_acc[...] = jnp.zeros_like(dk_acc)
        dv_acc[...] = jnp.zeros_like(dv_acc)
        for start in range(0, k_ref.shape[0], BLOCK):
            keys_t[:, start : start + BLOCK] = jnp.transpose(k_ref[start : start + BLOCK, :])

    grad = grad_ref[...]
    own = both_heads(q_ref[...] * jnp.asarray(HDIM**-0.5, low))
    own_grad = both_heads(grad)
    columns = [slice(head * HDIM, (head + 1) * HDIM) for head in heads]
    products = jnp.transpose(grad.astype(wide) * full_ref[...])
    offset = jnp.concatenate(
        [jnp.sum(products[rows], axis=0, keepdims=True) for rows in columns], axis=1
    )
    log_total = jnp.concatenate([lse_ref[head : head + 1, :] for head in heads], axis=1)
    dq_acc[...] = jnp.zeros_like(dq_acc)

    def step(j, diagonal):
        at = pl.ds(pl.multiple_of(j * BLOCK, BLOCK), BLOCK)
        scores = dot_nt(k_ref[at, :], own)
        if diagonal:
            k_at = lax.broadcasted_iota(jnp.int32, (BLOCK, BLOCK), 0)
            q_at = lax.broadcasted_iota(jnp.int32, (BLOCK, BLOCK), 1)
            allowed = k_at <= q_at
            allowed = jnp.concatenate([allowed, allowed], axis=1)
            scores = jnp.where(allowed, scores, far_below)
        probs = jnp.exp(scores - log_total)
        prob_grad = dot_nt(v_ref[at, :], own_grad)
        dv_acc[at, :] += dot_nn(probs.astype(low), own_grad)
        raw_grad = (probs * (prob_grad - offset)).astype(low)
        dk_acc[at, :] += dot_nn(raw_grad, own)
        for head, rows in zip(heads, columns):
            dq_acc[rows, :] += dot_nn(
                keys_t[rows, at], raw_grad[:, head * BLOCK : (head + 1) * BLOCK]
            )

    @pl.loop(0, i)
    def _(j):
        step(j, False)

    step(i, True)
    at = pl.ds(pl.multiple_of(i * BLOCK, BLOCK), BLOCK)
    query_grad = jnp.transpose(dq_acc[...]) * HDIM**-0.5
    mixed_ref[at, :LANES] = (
        query_grad * cos_ref[at, :] - swap_halves(query_grad) * sin_ref[at, :]
    ).astype(low)

    @pl.when(i == count - 1)
    def _():
        @pl.loop(0, count)
        def _(j):
            at = pl.ds(pl.multiple_of(j * BLOCK, BLOCK), BLOCK)
            keys_grad = dk_acc[at, :]
            mixed_ref[at, LANES : 2 * LANES] = (
                keys_grad * cos_ref[at, :] - swap_halves(keys_grad) * sin_ref[at, :]
            ).astype(low)
            half_grad = 0.5 * dv_acc[at, :]
            first_ref[at, :] = half_grad
            mixed_ref[at, 2 * LANES :] = half_grad.astype(low)


def attend_back(pair, lengths, query, keys, values, grad, full, lse, cosine, sine):
    rows = query.shape[0]
    block = pl.BlockSpec((BLOCK, LANES), lambda i, n: (i, pair))
    whole = pl.BlockSpec((rows, LANES), lambda i, n: (0, pair))
    given = pl.BlockSpec((BLOCK, LANES), lambda i, n: (i, 0))
    fixed = lambda i, n: (0, 0)
    table = pl.BlockSpec((rows, LANES), fixed)
    spec = pltpu.PrefetchScalarGridSpec(
        num_scalar_prefetch=1,
        grid=(rows // BLOCK,),
        in_specs=[
            block, whole, whole, given, given,
            pl.BlockSpec((8, BLOCK), lambda i, n: (0, i)),
            table, table,
        ],
        out_specs=[pl.BlockSpec((rows, 3 * LANES), fixed), pl.BlockSpec((rows, LANES), fixed)],
        scratch_shapes=[
            pltpu.VMEM((rows, LANES), wide),
            pltpu.VMEM((rows, LANES), wide),
            pltpu.VMEM((LANES, BLOCK), wide),
            pltpu.VMEM((LANES, rows), low),
        ],
    )
    return pl.pallas_call(
        attend_back_kernel,
        grid_spec=spec,
        out_shape=[
            jax.ShapeDtypeStruct((rows, 3 * LANES), low),
            jax.ShapeDtypeStruct((rows, LANES), wide),
        ],
        compiler_params=pltpu.CompilerParams(vmem_limit_bytes=VMEM_BYTES),
        cost_estimate=pl.CostEstimate(
            flops=20 * rows * rows * LANES, bytes_accessed=6 << 20, transcendentals=rows * rows
        ),
        name="attend_back",
    )(lengths, query, keys, values, grad, full, lse, cosine, sine)


def feed_kernel(order, which, *refs):
    given, (x_own, x_other, c_own, c_other) = refs[:-17], refs[-17:-13]
    outs, grads, dgate_ref, ddown_ref = refs[-13:-11], refs[-11:-9], refs[-9], refs[-8]
    weights, x_ref, c_ref, inner_s, mlp_s, weight_sems, row_sems = refs[-7:]
    step = pl.program_id(0)
    parts, depth3, depth = weights.shape
    pieces = len(given) // parts
    width = depth // pieces
    units = depth3 // 3
    rows = x_own.shape[0]
    skipped = given[0].shape[0] - depth3
    chunk = min(512, rows)
    sides = (slice(0, rows), slice(rows, 2 * rows))
    fetches = [
        [
            pltpu.make_async_copy(
                given[number * pieces + c].at[skipped:, :],
                weights.at[number, :, pl.ds(pl.multiple_of(which[c] * width, LANES), width)],
                weight_sems.at[number, c],
            )
            for c in range(pieces)
        ]
        for number in range(parts)
    ]
    loads = [
        pltpu.make_async_copy(source, target.at[side, :], row_sems.at[number])
        for number, (source, target, side) in enumerate(
            zip((x_own, x_other, c_own, c_other), (x_ref, x_ref, c_ref, c_ref), sides * 2)
        )
    ]

    @pl.when(step == 0)
    def _():
        for fetch in fetches[0]:
            fetch.start()
        for load in loads:
            load.start()
        for fetch in sum(fetches[1:], []):
            fetch.start()
        for ref in (*outs, *grads):
            ref[...] = jnp.zeros_like(ref)
        for load in loads:
            load.wait()

    for number in range(parts):

        @pl.when(step == number)
        def _(number=number):
            for fetch in fetches[number]:
                fetch.wait()

    w_ref = weights.at[step]
    for half, (out_ref, grad_ref) in enumerate(zip(outs, grads)):

        @pl.loop(0, rows // chunk)
        def _(t, half=half, out_ref=out_ref, grad_ref=grad_ref):
            at = pl.ds(pl.multiple_of(t * chunk, chunk), chunk)
            along = pl.ds(pl.multiple_of(half * rows + t * chunk, chunk), chunk)
            gated = dot_nt(w_ref[: 2 * units, :], x_ref[along, :])
            inner_grad = dot_nt(w_ref[2 * units :, :], c_ref[along, :])
            gate, up = gated[:units], gated[units:]
            sigmoid = jax.nn.sigmoid(gate)
            silu = gate * sigmoid
            inner = (silu * up).astype(low)
            gate_grad = (inner_grad * up * sigmoid * (1.0 + gate * (1.0 - sigmoid))).astype(low)
            up_grad = (inner_grad * silu).astype(low)
            inner_s[:, along] = inner
            mlp_s[:units, along] = gate_grad
            mlp_s[units:, along] = up_grad
            mlp_grad = jnp.concatenate([gate_grad, up_grad], axis=0)
            out_ref[at, :] += dot_tn(inner, w_ref[2 * units :, :])
            grad_ref[at, :] += dot_tn(mlp_grad, w_ref[: 2 * units, :])

    for c in range(pieces):
        cols = slice(c * width, (c + 1) * width)
        dgate_ref[c, 0, skipped:, :] = dot_nn(mlp_s[...], x_ref[:, cols]).astype(low)
        ddown_ref[c, 0] = dot_nn(inner_s[...], c_ref[:, cols]).astype(low)


def feed(order, which, slots, units, x_own, x_other, c_own, c_other):
    rows, depth = x_own.shape
    parts, pieces, width = len(slots), len(slots[0]), slots[0][0].shape[1]
    gates = slots[0][0].shape[0] - units
    anywhere = pl.BlockSpec(memory_space=pl.ANY)
    activations = pl.BlockSpec((rows, depth), lambda h, o, c: (0, 0), pipeline_mode=pl.Buffered(1))
    block = lambda height: pl.BlockSpec((pieces, 1, height, width), lambda h, o, c: (0, o[h], 0, 0))
    spec = pltpu.PrefetchScalarGridSpec(
        num_scalar_prefetch=2,
        grid=(parts,),
        in_specs=[anywhere] * (parts * pieces + 4),
        out_specs=[activations] * 4 + [block(gates), block(units)],
        scratch_shapes=[
            pltpu.VMEM((parts, 3 * units, depth), low),
            pltpu.VMEM((2 * rows, depth), low),
            pltpu.VMEM((2 * rows, depth), low),
            pltpu.VMEM((units, 2 * rows), low),
            pltpu.VMEM((2 * units, 2 * rows), low),
            pltpu.SemaphoreType.DMA((parts, pieces)),
            pltpu.SemaphoreType.DMA((4,)),
        ],
    )
    return pl.pallas_call(
        feed_kernel,
        grid_spec=spec,
        out_shape=[jax.ShapeDtypeStruct((rows, depth), wide)] * 4
        + [
            jax.ShapeDtypeStruct((pieces, parts, gates, width), low),
            jax.ShapeDtypeStruct((pieces, parts, units, width), low),
        ],
        compiler_params=pltpu.CompilerParams(vmem_limit_bytes=VMEM_BYTES),
        cost_estimate=pl.CostEstimate(
            flops=36 * rows * depth * units * parts,
            bytes_accessed=30 << 20,
            transcendentals=2 * rows * units * parts,
        ),
        name="feed",
    )(order, which, *sum(slots, []), x_own, x_other, c_own, c_other)


def collect_kernel(order, which, *refs):
    out_ref = refs[-1]
    height, width = refs[0].shape
    pieces = out_ref.shape[1] // width
    for number, ref in enumerate(refs[:-1]):
        part, piece = divmod(number, pieces)
        rows = pl.ds(pl.multiple_of(order[part] * height, height), height)
        out_ref[rows, pl.ds(pl.multiple_of(which[piece] * width, LANES), width)] = ref[...]


def collect(order, which, slots, height):
    parts, pieces, width = len(slots), len(slots[0]), slots[0][0].shape[1]
    spec = pltpu.PrefetchScalarGridSpec(
        num_scalar_prefetch=2,
        grid=(1,),
        in_specs=[pl.BlockSpec((height, width), lambda i, o, c: (0, 0))] * (parts * pieces),
        out_specs=pl.BlockSpec((parts * height, pieces * width), lambda i, o, c: (0, 0)),
    )
    return pl.pallas_call(
        collect_kernel,
        grid_spec=spec,
        out_shape=jax.ShapeDtypeStruct((parts * height, pieces * width), low),
        compiler_params=pltpu.CompilerParams(vmem_limit_bytes=VMEM_BYTES),
        cost_estimate=pl.CostEstimate(flops=0, bytes_accessed=2 << 20, transcendentals=0),
        name="collect",
    )(order, which, *sum(slots, []))


def line_up_kernel(order, *refs):
    out_ref = refs[-1]
    height, width = refs[0].shape
    pairs = out_ref.shape[0] // height // (len(refs) - 1)
    each = width // pairs
    for number, ref in enumerate(refs[:-1]):
        for pair in range(pairs):
            start = (order[number] * pairs + pair) * height
            rows = pl.ds(pl.multiple_of(start, height), height)
            out_ref[rows, :] = ref[:, pair * each : (pair + 1) * each]


def line_up(order, arrived, pairs):
    height, width = arrived[0].shape
    shape = (len(arrived) * pairs * height, width // pairs)
    spec = pltpu.PrefetchScalarGridSpec(
        num_scalar_prefetch=1,
        grid=(1,),
        in_specs=[pl.BlockSpec((height, width), lambda i, o: (0, 0))] * len(arrived),
        out_specs=pl.BlockSpec(shape, lambda i, o: (0, 0)),
    )
    return pl.pallas_call(
        line_up_kernel,
        grid_spec=spec,
        out_shape=jax.ShapeDtypeStruct(shape, low),
        compiler_params=pltpu.CompilerParams(vmem_limit_bytes=VMEM_BYTES),
        cost_estimate=pl.CostEstimate(flops=0, bytes_accessed=2 << 20, transcendentals=0),
        name="line_up",
    )(order, *arrived)


def unproject_kernel(normed_ref, *refs):
    mixed_refs, (dw_ref, acc_ref) = refs[:-2], refs[-2:]
    step = pl.program_id(0)

    @pl.when(step == 0)
    def _():
        acc_ref[...] = jnp.zeros_like(acc_ref)

    height = mixed_refs[0].shape[1]
    for number, ref in enumerate(mixed_refs):
        acc_ref[number * height : (number + 1) * height, :] += dot_tn(ref[...], normed_ref[...])

    @pl.when(step == pl.num_programs(0) - 1)
    def _():
        dw_ref[...] = acc_ref[...].astype(low)


def unproject(normed, mixed_grads):
    tokens, depth = normed.shape
    rows = 512
    height = mixed_grads[0].shape[1]
    total = height * len(mixed_grads)
    block = lambda width: pl.BlockSpec((rows, width), lambda o: (o, 0))
    return pl.pallas_call(
        unproject_kernel,
        grid=(tokens // rows,),
        in_specs=[block(depth)] + [block(height)] * len(mixed_grads),
        out_specs=pl.BlockSpec((total, depth), lambda o: (0, 0)),
        scratch_shapes=[pltpu.VMEM((total, depth), wide)],
        out_shape=jax.ShapeDtypeStruct((total, depth), low),
        compiler_params=pltpu.CompilerParams(vmem_limit_bytes=VMEM_BYTES),
        cost_estimate=pl.CostEstimate(
            flops=2 * tokens * depth * total, bytes_accessed=9 << 20, transcendentals=0
        ),
        name="unproject",
    )(normed, *mixed_grads)


def arrival_order(place):
    ways = jnp.where(place < 2, 1, -1)
    far = jnp.where(place % 2 == 0, 3, 0)
    return jnp.stack([place, place + ways, place + 2 * ways, far]).astype(jnp.int32)


def gather_all(tokens, weights, end, place, chips, use, then):
    near = place < 2
    rows, depth = tokens.shape
    width = weights.shape[1]
    cut = rows * depth // width

    def hop(ends):
        return (
            lax.ppermute(ends[0], "head", [(0, 1), (1, 2), (2, 3)]),
            lax.ppermute(ends[1], "head", [(1, 0), (2, 1), (3, 2)]),
        )

    def nearest(hops):
        return jnp.where(near, hops[-1][1], hops[-1][0])

    def farthest(hops):
        return jnp.where(
            place % 3 == 0, nearest(hops), jnp.where(near, hops[0][0], hops[0][1])
        )

    def in_blocks(tokens):
        return jnp.moveaxis(tokens.reshape(rows, -1, width), 1, 0).reshape(cut, width)

    def plane(slot):
        if chips != 4:
            return [lax.all_gather(slot[:end], "chip", axis=1, tiled=True)]
        return [slot[:end]] + [
            lax.ppermute(slot[:end], "chip", [(c, c ^ away) for c in range(chips)])
            for away in range(1, chips)
        ]

    barrier = lax.optimization_barrier
    slots, planes = [weights], []
    token_hops, weight_hops = [], []
    ends = barrier(hop((tokens, tokens)))
    first_block = nearest([ends])
    token_hops.append(tuple(in_blocks(end) for end in ends))

    ends = hop(tuple(jnp.concatenate([end, weights]) for end in token_hops[0]))
    planes.append(plane(weights))
    used = use(0, tokens, None)
    ends, planes, used = barrier((ends, planes, used))
    token_hops.append(tuple(end[:cut] for end in ends))
    weight_hops.append(tuple(end[cut:] for end in ends))
    slots.append(nearest(weight_hops))
    second_block = nearest(token_hops)

    ends = hop(ends)
    planes.append(plane(slots[1]))
    used = use(1, first_block, used)
    used = use(2, second_block, used)
    ends, planes, used = barrier((ends, planes, used))
    token_hops.append(tuple(end[:cut] for end in ends))
    weight_hops.append(tuple(end[cut:] for end in ends))
    slots.append(nearest(weight_hops))
    used = use(3, farthest(token_hops), used)

    ends = hop(weight_hops[-1])
    planes.append(plane(slots[2]))
    made, used = then(0, used)
    ends, planes, made, used = barrier((ends, planes, made, used))
    weight_hops.append(ends)
    slots.append(farthest(weight_hops))
    planes.append(plane(slots[3]))
    more, used = then(1, used)
    planes, more = barrier((planes, more))
    return planes, [slot[end:] for slot in slots], used, [made, more]


def exchange(pieces):
    return lax.all_to_all(pieces, "head", split_axis=0, concat_axis=0)


def exchange_turned(pieces, place):
    count = pieces.shape[0]
    came = []
    for j in range(count):
        piece = lax.dynamic_index_in_dim(pieces, (place + j) % count, 0, keepdims=False)
        came.append(
            lax.ppermute(piece, "head", [(k, (k + j) % count) for k in range(count)]) if j else piece
        )
    return came


def to_line(piece, count):
    return exchange(jnp.broadcast_to(piece[None], (count, *piece.shape)))


def other_core(array):
    return lax.ppermute(array, "core", [(0, 1), (1, 0)])


def by_core(core, own, came, axis):
    first = jnp.where(core == 0, own, came)
    second = jnp.where(core == 0, came, own)
    return jnp.concatenate([first, second], axis=axis)


def shards(
    tokens, first_values, mixer_in, mixer_out, gate_up, down_weight, norm_gains, lengths, cotangent
):
    line = lax.axis_size("head")
    chips = lax.axis_size("chip")
    place = lax.axis_index("head")
    core = lax.axis_index("core")
    rows, depth = tokens.shape
    cols = mixer_in.shape[2]
    width = mixer_in.shape[1]
    units = down_weight.shape[0] // 2
    pairs = cols // LANES
    after = lax.optimization_barrier

    def halves(array, axis):
        first, second = jnp.split(array, 2, axis=axis)
        return jnp.where(core == 0, first, second), jnp.where(core == 0, second, first)

    def chip_scatter(grad):
        grad = grad.reshape(*grad.shape[:-1], chips, 2 * width)
        return lax.psum_scatter(jnp.moveaxis(grad, -2, 0), "chip", scatter_dimension=0)

    def before(given, *results):
        return after((given, *results))[0]

    qkv_low = mixer_in.astype(low)
    gain_low = norm_gains.astype(low)
    gain_rows = jnp.pad(gain_low, ((0, GAIN_ROWS - 2), (0, 0)))
    qkv_rows = qkv_low.reshape(3, width, pairs, LANES).transpose(2, 0, 3, 1)
    qkv_rows = qkv_rows.reshape(3 * cols, width)
    pack = lax.all_gather(
        jnp.concatenate([qkv_rows, gain_rows], axis=0), ("chip", "core"), axis=1, tiled=True
    )
    gain_first = pack[3 * cols].astype(wide)
    gain_second = pack[3 * cols + 1].astype(wide)

    gates_low = gate_up.astype(low)
    feed_rows = jnp.concatenate(
        [gates_low.transpose(0, 2, 1), down_weight.astype(low)[None]], axis=0
    ).reshape(3, 2, units, width)
    out_low = mixer_out.astype(low).reshape(2, cols // 2, width)

    def half_rows(which):
        return jnp.concatenate([out_low[which], feed_rows[:, which].reshape(3 * units, width)])

    first_rows, second_rows = half_rows(0), half_rows(1)
    own_rows = jnp.where(core == 0, first_rows, second_rows)
    other_rows = jnp.where(core == 0, second_rows, first_rows)
    own_rows = by_core(core, own_rows, other_core(other_rows), -1)
    end = own_rows.shape[0]
    qkv_sides = jnp.concatenate(jnp.split(qkv_rows, pairs), axis=-1)
    weights = jnp.concatenate([own_rows, qkv_sides])

    order = arrival_order(place)
    place_one = place[None].astype(jnp.int32)
    chip = lax.axis_index("chip")
    which = (chip ^ jnp.arange(4) if chips == 4 else jnp.zeros(1)).astype(jnp.int32)
    cosine, sine = rope_tables()

    def use(number, x, made):
        index = order[number : number + 1]
        return project(index, x, pack, first_values, cosine, sine, made or [])

    def then(pair, made):
        return attend(pair, lengths, *made[:3]), made

    planes, qkv_line, made, attended_parts = gather_all(
        tokens, weights, end, place, chips, use, then
    )
    query, keys, values, normed_a = made
    cot_other = other_core(cotangent)
    out_half = collect(order, which, planes, cols // 2).reshape(line, 1, cols // 2, depth)
    out_heads = by_core(core, out_half, other_core(out_half), 1)
    out_full = out_heads.reshape(depth, depth)
    lined = chips == 4
    attended_pieces = [exchange(part[0].reshape(line, rows, LANES)) for part in attended_parts]
    attended_wide = [part[1] for part in attended_parts]
    log_total = [part[2] for part in attended_parts]
    attended = jnp.stack(attended_pieces, axis=1).transpose(2, 0, 1, 3).reshape(rows, depth)

    qkv_line = line_up(order, qkv_line, pairs)
    qkv_full = lax.all_gather(qkv_line, ("chip", "core"), axis=1, tiled=True)
    qkv_full = qkv_full.reshape(line, pairs, 3 * LANES, depth)

    token_rows = tokens.astype(wide)
    hidden_state = token_rows + dot_nn(attended, out_full)
    normed_b, unit_b, factor_b = rms_parts(hidden_state, gain_second)
    normed_b = before(normed_b.astype(low), qkv_full)
    branch_own, branch_other, grad_own, grad_other, gate_grad, down_grad = feed(
        order, which, planes, units, normed_b, other_core(normed_b), cotangent, cot_other
    )
    normed_b_grad = grad_own + other_core(grad_other)
    branch_b = branch_own + other_core(branch_other)
    block_out = (hidden_state + branch_b).astype(low)

    state_part = rms_back(normed_b_grad, unit_b, factor_b, gain_second)
    state_grad = cotangent.astype(wide) + state_part
    branch_grad = state_grad.astype(low)

    def spread(grad):
        if not lined:
            grad = grad.reshape(line, -1, chips, 2 * width).transpose(2, 0, 1, 3)
        return grad

    down_sum = lax.psum_scatter(spread(down_grad), "chip", scatter_dimension=0)
    positions = place * rows + jnp.arange(rows)
    valid = (positions < lengths[0]).astype(wide)[None, :, None]
    outs = out_full.reshape(line, pairs, LANES, depth)
    asked = [
        (valid * jnp.einsum("td,zcd->ztc", branch_grad, outs[:, pair], preferred_element_type=wide)).astype(low)
        for pair in range(pairs)
    ]

    def back(pair, came):
        return attend_back(
            pair, lengths, query, keys, values, came.reshape(line * rows, LANES),
            attended_wide[pair], log_total[pair], cosine, sine,
        )

    came = exchange(asked[0])
    out_grad = dot_tn(attended, branch_grad).astype(low).reshape(line, cols, depth)
    kept, given = halves(out_grad, 1)
    out_grad = (kept.astype(wide) + other_core(given).astype(wide)).astype(low)
    out_grad = jnp.moveaxis(out_grad.reshape(line, cols // 2, chips, 2 * width), 2, 0)
    gate_grad = spread(gate_grad).at[:, :, : cols // 2].set(out_grad)
    came, gate_grad, asked, down_sum = after((came, gate_grad, asked, down_sum))

    gate_sum = lax.psum_scatter(gate_grad, "chip", scatter_dimension=0)
    mixed_first = back(0, came)
    came = exchange(asked[1])
    down_came = exchange_turned(down_sum, place)
    came, mixed_first, down_came = after((came, mixed_first, down_came))

    mixed_second = back(1, came)
    mixed_rows = exchange(mixed_first[0].reshape(line, rows, 3 * LANES))
    mixed_rows, mixed_second, gate_sum = after((mixed_rows, mixed_second, gate_sum))

    came = exchange(mixed_second[0].reshape(line, rows, 3 * LANES))
    gate_came = exchange_turned(gate_sum, place)
    qkv_grad = unproject(normed_a, [mixed_first[0], mixed_second[0]])
    kept, given = halves(qkv_grad, 0)
    qkv_grad = (kept.astype(wide) + other_core(given).astype(wide)).astype(low)
    qkv_sum = chip_scatter(qkv_grad)
    normed_a_grad = jnp.einsum(
        "ztc,zcd->td", mixed_rows, qkv_full[:, 0], preferred_element_type=wide
    )
    normed_a_grad, came, gate_came, qkv_sum = after((normed_a_grad, came, gate_came, qkv_sum))
    normed_a_grad += jnp.einsum("ztc,zcd->td", came, qkv_full[:, 1], preferred_element_type=wide)
    first_grad = jnp.concatenate([mixed_first[1], mixed_second[1]], axis=1)

    def settle(grad):
        kept, given = halves(grad, -1)
        return by_core(core, kept[..., None, :, :], other_core(given)[..., None, :, :], -3)

    gate_sum = sum(piece.astype(wide) for piece in gate_came)
    down_sum = sum(piece.astype(wide) for piece in down_came)
    mixer_out_grad = settle(gate_sum[: cols // 2]).reshape(cols, width)
    gate_sum = settle(gate_sum[cols // 2 :].reshape(2, units, 2 * width)).reshape(2, 2 * units, width)
    down_grad = settle(down_sum).reshape(2 * units, width)
    qkv_sum = settle(qkv_sum.astype(wide)).reshape(pairs, 3, LANES, width)
    gate_up_grad = gate_sum.transpose(0, 2, 1)
    mixer_in_grad = qkv_sum.transpose(1, 3, 0, 2).reshape(3, width, cols)

    _, unit_a, factor_a = rms_parts(token_rows, gain_first)
    tokens_grad = state_grad + rms_back(normed_a_grad, unit_a, factor_a, gain_first)

    gain_wide = gain_low.astype(wide)
    gain_parts = jnp.stack(
        [
            jnp.sum(qkv_low.astype(wide) * mixer_in_grad, axis=(0, 2)),
            jnp.sum(gates_low.astype(wide) * gate_up_grad, axis=(0, 2)),
        ]
    )
    gains_grad = jnp.sum(to_line(gain_parts / gain_wide, line), axis=0)
    return (
        block_out,
        tokens_grad,
        first_grad,
        mixer_in_grad,
        mixer_out_grad,
        gate_up_grad,
        down_grad,
        gains_grad,
    )


def solution(mesh):
    groups, line = mesh.shape["dp"], mesh.shape["head"]
    fine = jax.sharding.Mesh(
        mesh.devices.reshape(groups // 2, 2, line), ("chip", "core", "head")
    )
    dp = ("chip", "core")
    return jax.shard_map(
        shards,
        mesh=fine,
        in_specs=(
            P(("chip", "core", "head"), None),
            P(dp, "head"),
            P(None, dp, "head"),
            P("head", dp),
            P(None, dp, "head"),
            P("head", dp),
            P(None, dp),
            P(dp),
            P(("chip", "core", "head"), None),
        ),
        out_specs=(
            P(("chip", "core", "head"), None),
            P(("chip", "core", "head"), None),
            P(dp, "head"),
            P(None, dp, "head"),
            P("head", dp),
            P(None, dp, "head"),
            P("head", dp),
            P(None, dp),
        ),
        check_vma=False,
    )
```

```python
import functools

import jax
import jax.numpy as jnp
from jax import lax
from jax.experimental import pallas as pl
from jax.experimental.pallas import tpu as pltpu
from jax.sharding import PartitionSpec as P

HDIM = 64
SEQ = 2048
LANES = 128
GAIN_ROWS = 16

epsilon = 1e-05
far_below = -1e30
rope_base = 10000.0
low = jnp.bfloat16
wide = jnp.float32
VMEM_BYTES = 60 * 1024 * 1024
FINISH_FLOPS = 1 << 38


def dot_nn(a, b):
    return lax.dot_general(a, b, (((1,), (0,)), ((), ())), preferred_element_type=wide)


def dot_nt(a, b):
    return lax.dot_general(a, b, (((1,), (1,)), ((), ())), preferred_element_type=wide)


def dot_tn(a, b):
    return lax.dot_general(a, b, (((0,), (0,)), ((), ())), preferred_element_type=wide)


def rope_tables():
    half = HDIM // 2
    rates = rope_base ** (-jnp.arange(half, dtype=wide) * 2.0 / HDIM)
    angles = jnp.arange(SEQ, dtype=wide)[:, None] * rates[None, :]
    cosine, sine = jnp.cos(angles), jnp.sin(angles)
    pair = LANES // HDIM
    return (
        jnp.concatenate([cosine, cosine] * pair, axis=1),
        jnp.concatenate([-sine, sine] * pair, axis=1),
    )


def swap_halves(field):
    half = HDIM // 2
    lane = lax.broadcasted_iota(jnp.int32, field.shape, 1)
    ahead = pltpu.roll(field, LANES - half, 1)
    behind = pltpu.roll(field, half, 1)
    return jnp.where(lane % HDIM < half, ahead, behind)


def rms_parts(field, gain):
    factor = lax.rsqrt(jnp.mean(field * field, axis=-1, keepdims=True) + epsilon)
    unit = field * factor
    return (unit * gain, unit, factor)


def rms_back(normed_grad, unit, factor, gain):
    scaled = normed_grad * gain
    return factor * (scaled - unit * jnp.mean(scaled * unit, axis=-1, keepdims=True))


def project_kernel(place, x_ref, w_ref, gain_ref, first_ref, cos_ref, sin_ref, *refs):
    q_ref, k_ref, v_ref, normed_ref = refs[-4:]
    rows, depth = normed_ref.shape
    width = x_ref.shape[1]
    if width == depth:
        width = depth // 4
        blocks = [x_ref[:, start : start + width].astype(wide) for start in range(0, depth, width)]
    else:
        starts = range(0, x_ref.shape[0], rows)
        blocks = [x_ref[start : start + rows, :].astype(wide) for start in starts]
    squares = sum(jnp.sum(block * block, axis=-1, keepdims=True) for block in blocks)
    factor = lax.rsqrt(squares / depth + epsilon)
    for number, block in enumerate(blocks):
        cols = slice(number * width, (number + 1) * width)
        normed_ref[:, cols] = (block * factor * gain_ref[0:1, cols].astype(wide)).astype(low)
    normed = normed_ref[...]
    cosine, sine = cos_ref[...], sin_ref[...]
    for pair in range(q_ref.shape[1] // LANES):
        cols = slice(pair * LANES, (pair + 1) * LANES)
        start = pair * 3 * LANES
        mixed = dot_nt(normed, w_ref[start : start + 3 * LANES, :])
        for part, out_ref in ((0, q_ref), (1, k_ref)):
            piece = mixed[:, part * LANES : (part + 1) * LANES]
            out_ref[:, cols] = (piece * cosine + swap_halves(piece) * sine).astype(low)
        first = first_ref[:, cols].astype(wide)
        v_ref[:, cols] = (0.5 * mixed[:, 2 * LANES :] + 0.5 * first).astype(low)


def project(index, x, pack, first_values, cosine, sine, made):
    total, cols = first_values.shape
    depth = pack.shape[1]
    rows = x.shape[0] * x.shape[1] // depth
    gain_block = pack.shape[0] // GAIN_ROWS - 1
    fixed = lambda i, p: (0, 0)
    natural = lambda width: pl.BlockSpec((rows, width), lambda i, p: (p[0], 0))
    shapes = [cols, cols, cols, depth]
    spec = pltpu.PrefetchScalarGridSpec(
        num_scalar_prefetch=1,
        grid=(1,),
        in_specs=[
            pl.BlockSpec(x.shape, fixed),
            pl.BlockSpec((3 * cols, depth), fixed),
            pl.BlockSpec((GAIN_ROWS, depth), lambda i, p: (gain_block, 0)),
            natural(cols),
            natural(LANES),
            natural(LANES),
        ]
        + [pl.BlockSpec(memory_space=pl.ANY)] * len(made),
        out_specs=[natural(width) for width in shapes],
    )
    return pl.pallas_call(
        project_kernel,
        grid_spec=spec,
        out_shape=[jax.ShapeDtypeStruct((total, width), low) for width in shapes],
        input_output_aliases={7 + number: number for number in range(len(made))},
        compiler_params=pltpu.CompilerParams(vmem_limit_bytes=VMEM_BYTES),
        cost_estimate=pl.CostEstimate(
            flops=2 * rows * depth * 3 * cols, bytes_accessed=5 << 20, transcendentals=0
        ),
        name="project",
    )(index, x, pack, pack, first_values, cosine, sine, *made)


BLOCK = 512


def both_heads(array):
    lane = lax.broadcasted_iota(jnp.int32, array.shape, 1)
    zero = jnp.zeros_like(array)
    return jnp.concatenate(
        [jnp.where(lane < HDIM, array, zero), jnp.where(lane < HDIM, zero, array)], axis=0
    )


def attend_kernel(len_ref, q_ref, k_ref, v_ref, out_ref, full_ref, lse_ref, acc_ref, max_ref, sum_ref):
    i = pl.program_id(0)
    own = both_heads(q_ref[...] * jnp.asarray(HDIM**-0.5, low))
    max_ref[...] = jnp.full_like(max_ref, far_below)
    sum_ref[...] = jnp.zeros_like(sum_ref)
    acc_ref[...] = jnp.zeros_like(acc_ref)

    def step(j, diagonal):
        at = pl.ds(pl.multiple_of(j * BLOCK, BLOCK), BLOCK)
        scores = dot_nt(own, k_ref[at, :])
        if diagonal:
            q_at = lax.broadcasted_iota(jnp.int32, (BLOCK, BLOCK), 0)
            k_at = lax.broadcasted_iota(jnp.int32, (BLOCK, BLOCK), 1)
            allowed = k_at <= q_at
            allowed = jnp.concatenate([allowed, allowed], axis=0)
            scores = jnp.where(allowed, scores, far_below)
        old = max_ref[...]
        peak = jnp.maximum(old, jnp.max(scores, axis=1, keepdims=True))
        decay = jnp.exp(old - peak)
        max_ref[...] = peak
        total = sum_ref[...] * decay
        powers = []
        for start in range(0, BLOCK, LANES):
            power = jnp.exp(scores[:, start : start + LANES] - peak)
            total += power
            powers.append(power.astype(low))
        sum_ref[...] = total
        acc_ref[...] = acc_ref[...] * decay + dot_nn(jnp.concatenate(powers, axis=1), v_ref[at, :])

    @pl.loop(0, i)
    def _(j):
        step(j, False)

    step(i, True)
    total = jnp.sum(sum_ref[...], axis=1, keepdims=True)
    log_total = max_ref[...] + jnp.log(total)
    for head in range(LANES // HDIM):
        rows = slice(head * BLOCK, (head + 1) * BLOCK)
        lse_ref[head : head + 1, :] = jnp.transpose(log_total[rows])[0:1, :]
    result = acc_ref[...] / total
    lane = lax.broadcasted_iota(jnp.int32, (BLOCK, LANES), 1)
    valid = i * BLOCK + lax.broadcasted_iota(jnp.int32, (BLOCK, 1), 0) < len_ref[0]
    result = jnp.where(valid, jnp.where(lane < HDIM, result[:BLOCK], result[BLOCK:]), 0.0)
    out_ref[...] = result.astype(low)
    full_ref[...] = result


def attend(pair, lengths, query, keys, values):
    rows = query.shape[0]
    block = pl.BlockSpec((BLOCK, LANES), lambda i, n: (i, pair))
    whole = pl.BlockSpec((rows, LANES), lambda i, n: (0, pair))
    result = pl.BlockSpec((BLOCK, LANES), lambda i, n: (i, 0))
    spec = pltpu.PrefetchScalarGridSpec(
        num_scalar_prefetch=1,
        grid=(rows // BLOCK,),
        in_specs=[block, whole, whole],
        out_specs=[result, result, pl.BlockSpec((8, BLOCK), lambda i, n: (0, i))],
        scratch_shapes=[pltpu.VMEM((2 * BLOCK, LANES), wide)] * 3,
    )
    return pl.pallas_call(
        attend_kernel,
        grid_spec=spec,
        out_shape=[
            jax.ShapeDtypeStruct((rows, LANES), low),
            jax.ShapeDtypeStruct((rows, LANES), wide),
            jax.ShapeDtypeStruct((8, rows), wide),
        ],
        compiler_params=pltpu.CompilerParams(vmem_limit_bytes=VMEM_BYTES),
        cost_estimate=pl.CostEstimate(
            flops=8 * rows * rows * LANES, bytes_accessed=4 << 20, transcendentals=rows * rows
        ),
        name="attend",
    )(lengths, query, keys, values)


def attend_back_kernel(
    len_ref, q_ref, k_ref, v_ref, grad_ref, full_ref, lse_ref, cos_ref, sin_ref,
    mixed_ref, first_ref, dk_acc, dv_acc, dq_acc, keys_t,
):
    i = pl.program_id(0)
    count = pl.num_programs(0)
    heads = range(LANES // HDIM)

    @pl.when(i == 0)
    def _():
        dk_acc[...] = jnp.zeros_like(dk_acc)
        dv_acc[...] = jnp.zeros_like(dv_acc)
        for start in range(0, k_ref.shape[0], BLOCK):
            keys_t[:, start : start + BLOCK] = jnp.transpose(k_ref[start : start + BLOCK, :])

    grad = grad_ref[...]
    own = both_heads(q_ref[...] * jnp.asarray(HDIM**-0.5, low))
    own_grad = both_heads(grad)
    columns = [slice(head * HDIM, (head + 1) * HDIM) for head in heads]
    products = jnp.transpose(grad.astype(wide) * full_ref[...])
    offset = jnp.concatenate(
        [jnp.sum(products[rows], axis=0, keepdims=True) for rows in columns], axis=1
    )
    log_total = jnp.concatenate([lse_ref[head : head + 1, :] for head in heads], axis=1)
    dq_acc[...] = jnp.zeros_like(dq_acc)

    def step(j, diagonal):
        at = pl.ds(pl.multiple_of(j * BLOCK, BLOCK), BLOCK)
        scores = dot_nt(k_ref[at, :], own)
        if diagonal:
            k_at = lax.broadcasted_iota(jnp.int32, (BLOCK, BLOCK), 0)
            q_at = lax.broadcasted_iota(jnp.int32, (BLOCK, BLOCK), 1)
            allowed = k_at <= q_at
            allowed = jnp.concatenate([allowed, allowed], axis=1)
            scores = jnp.where(allowed, scores, far_below)
        probs = jnp.exp(scores - log_total)
        prob_grad = dot_nt(v_ref[at, :], own_grad)
        dv_acc[at, :] += dot_nn(probs.astype(low), own_grad)
        raw_grad = (probs * (prob_grad - offset)).astype(low)
        dk_acc[at, :] += dot_nn(raw_grad, own)
        for head, rows in zip(heads, columns):
            dq_acc[rows, :] += dot_nn(
                keys_t[rows, at], raw_grad[:, head * BLOCK : (head + 1) * BLOCK]
            )

    @pl.loop(0, i)
    def _(j):
        step(j, False)

    step(i, True)
    at = pl.ds(pl.multiple_of(i * BLOCK, BLOCK), BLOCK)
    query_grad = jnp.transpose(dq_acc[...]) * HDIM**-0.5
    mixed_ref[at, :LANES] = (
        query_grad * cos_ref[at, :] - swap_halves(query_grad) * sin_ref[at, :]
    ).astype(low)

    @pl.when(i == count - 1)
    def _():
        @pl.loop(0, count)
        def _(j):
            at = pl.ds(pl.multiple_of(j * BLOCK, BLOCK), BLOCK)
            keys_grad = dk_acc[at, :]
            mixed_ref[at, LANES : 2 * LANES] = (
                keys_grad * cos_ref[at, :] - swap_halves(keys_grad) * sin_ref[at, :]
            ).astype(low)
            half_grad = 0.5 * dv_acc[at, :]
            first_ref[at, :] = half_grad
            mixed_ref[at, 2 * LANES :] = half_grad.astype(low)


def attend_back(pair, lengths, query, keys, values, grad, full, lse, cosine, sine):
    rows = query.shape[0]
    block = pl.BlockSpec((BLOCK, LANES), lambda i, n: (i, pair))
    whole = pl.BlockSpec((rows, LANES), lambda i, n: (0, pair))
    given = pl.BlockSpec((BLOCK, LANES), lambda i, n: (i, 0))
    fixed = lambda i, n: (0, 0)
    table = pl.BlockSpec((rows, LANES), fixed)
    spec = pltpu.PrefetchScalarGridSpec(
        num_scalar_prefetch=1,
        grid=(rows // BLOCK,),
        in_specs=[
            block, whole, whole, given, given,
            pl.BlockSpec((8, BLOCK), lambda i, n: (0, i)),
            table, table,
        ],
        out_specs=[pl.BlockSpec((rows, 3 * LANES), fixed), pl.BlockSpec((rows, LANES), fixed)],
        scratch_shapes=[
            pltpu.VMEM((rows, LANES), wide),
            pltpu.VMEM((rows, LANES), wide),
            pltpu.VMEM((LANES, BLOCK), wide),
            pltpu.VMEM((LANES, rows), low),
        ],
    )
    return pl.pallas_call(
        attend_back_kernel,
        grid_spec=spec,
        out_shape=[
            jax.ShapeDtypeStruct((rows, 3 * LANES), low),
            jax.ShapeDtypeStruct((rows, LANES), wide),
        ],
        compiler_params=pltpu.CompilerParams(vmem_limit_bytes=VMEM_BYTES),
        cost_estimate=pl.CostEstimate(
            flops=20 * rows * rows * LANES, bytes_accessed=6 << 20, transcendentals=rows * rows
        ),
        name="attend_back",
    )(lengths, query, keys, values, grad, full, lse, cosine, sine)


def feed_kernel(order, which, *refs):
    given, (x_own, x_other, c_own, c_other) = refs[:-17], refs[-17:-13]
    outs, grads, dgate_ref, ddown_ref = refs[-13:-11], refs[-11:-9], refs[-9], refs[-8]
    weights, x_ref, c_ref, inner_s, mlp_s, weight_sems, row_sems = refs[-7:]
    step = pl.program_id(0)
    parts, depth3, depth = weights.shape
    pieces = len(given) // parts
    width = depth // pieces
    units = depth3 // 3
    rows = x_own.shape[0]
    skipped = given[0].shape[0] - depth3
    chunk = min(512, rows)
    sides = (slice(0, rows), slice(rows, 2 * rows))
    fetches = [
        [
            pltpu.make_async_copy(
                given[number * pieces + c].at[skipped:, :],
                weights.at[number, :, pl.ds(pl.multiple_of(which[c] * width, LANES), width)],
                weight_sems.at[number, c],
            )
            for c in range(pieces)
        ]
        for number in range(parts)
    ]
    loads = [
        pltpu.make_async_copy(source, target.at[side, :], row_sems.at[number])
        for number, (source, target, side) in enumerate(
            zip((x_own, x_other, c_own, c_other), (x_ref, x_ref, c_ref, c_ref), sides * 2)
        )
    ]

    @pl.when(step == 0)
    def _():
        for fetch in fetches[0]:
            fetch.start()
        for load in loads:
            load.start()
        for fetch in sum(fetches[1:], []):
            fetch.start()
        for ref in (*outs, *grads):
            ref[...] = jnp.zeros_like(ref)
        for load in loads:
            load.wait()

    for number in range(parts):

        @pl.when(step == number)
        def _(number=number):
            for fetch in fetches[number]:
                fetch.wait()

    w_ref = weights.at[step]
    for half, (out_ref, grad_ref) in enumerate(zip(outs, grads)):

        @pl.loop(0, rows // chunk)
        def _(t, half=half, out_ref=out_ref, grad_ref=grad_ref):
            at = pl.ds(pl.multiple_of(t * chunk, chunk), chunk)
            along = pl.ds(pl.multiple_of(half * rows + t * chunk, chunk), chunk)
            gated = dot_nt(w_ref[: 2 * units, :], x_ref[along, :])
            inner_grad = dot_nt(w_ref[2 * units :, :], c_ref[along, :])
            gate, up = gated[:units], gated[units:]
            sigmoid = jax.nn.sigmoid(gate)
            silu = gate * sigmoid
            inner = (silu * up).astype(low)
            gate_grad = (inner_grad * up * sigmoid * (1.0 + gate * (1.0 - sigmoid))).astype(low)
            up_grad = (inner_grad * silu).astype(low)
            inner_s[:, along] = inner
            mlp_s[:units, along] = gate_grad
            mlp_s[units:, along] = up_grad
            mlp_grad = jnp.concatenate([gate_grad, up_grad], axis=0)
            out_ref[at, :] += dot_tn(inner, w_ref[2 * units :, :])
            grad_ref[at, :] += dot_tn(mlp_grad, w_ref[: 2 * units, :])

    for c in range(pieces):
        cols = slice(c * width, (c + 1) * width)
        dgate_ref[c, 0, skipped:, :] = dot_nn(mlp_s[...], x_ref[:, cols]).astype(low)
        ddown_ref[c, 0] = dot_nn(inner_s[...], c_ref[:, cols]).astype(low)


def feed(order, which, slots, units, x_own, x_other, c_own, c_other):
    rows, depth = x_own.shape
    parts, pieces, width = len(slots), len(slots[0]), slots[0][0].shape[1]
    gates = slots[0][0].shape[0] - units
    anywhere = pl.BlockSpec(memory_space=pl.ANY)
    activations = pl.BlockSpec((rows, depth), lambda h, o, c: (0, 0), pipeline_mode=pl.Buffered(1))
    block = lambda height: pl.BlockSpec((pieces, 1, height, width), lambda h, o, c: (0, o[h], 0, 0))
    spec = pltpu.PrefetchScalarGridSpec(
        num_scalar_prefetch=2,
        grid=(parts,),
        in_specs=[anywhere] * (parts * pieces + 4),
        out_specs=[activations] * 4 + [block(gates), block(units)],
        scratch_shapes=[
            pltpu.VMEM((parts, 3 * units, depth), low),
            pltpu.VMEM((2 * rows, depth), low),
            pltpu.VMEM((2 * rows, depth), low),
            pltpu.VMEM((units, 2 * rows), low),
            pltpu.VMEM((2 * units, 2 * rows), low),
            pltpu.SemaphoreType.DMA((parts, pieces)),
            pltpu.SemaphoreType.DMA((4,)),
        ],
    )
    return pl.pallas_call(
        feed_kernel,
        grid_spec=spec,
        out_shape=[jax.ShapeDtypeStruct((rows, depth), wide)] * 4
        + [
            jax.ShapeDtypeStruct((pieces, parts, gates, width), low),
            jax.ShapeDtypeStruct((pieces, parts, units, width), low),
        ],
        compiler_params=pltpu.CompilerParams(vmem_limit_bytes=VMEM_BYTES),
        cost_estimate=pl.CostEstimate(
            flops=36 * rows * depth * units * parts,
            bytes_accessed=30 << 20,
            transcendentals=2 * rows * units * parts,
        ),
        name="feed",
    )(order, which, *sum(slots, []), x_own, x_other, c_own, c_other)


def collect_kernel(order, which, *refs):
    out_ref = refs[-1]
    height, width = refs[0].shape
    pieces = out_ref.shape[1] // width
    for number, ref in enumerate(refs[:-1]):
        part, piece = divmod(number, pieces)
        rows = pl.ds(pl.multiple_of(order[part] * height, height), height)
        out_ref[rows, pl.ds(pl.multiple_of(which[piece] * width, LANES), width)] = ref[...]


def collect(order, which, slots, height):
    parts, pieces, width = len(slots), len(slots[0]), slots[0][0].shape[1]
    spec = pltpu.PrefetchScalarGridSpec(
        num_scalar_prefetch=2,
        grid=(1,),
        in_specs=[pl.BlockSpec((height, width), lambda i, o, c: (0, 0))] * (parts * pieces),
        out_specs=pl.BlockSpec((parts * height, pieces * width), lambda i, o, c: (0, 0)),
    )
    return pl.pallas_call(
        collect_kernel,
        grid_spec=spec,
        out_shape=jax.ShapeDtypeStruct((parts * height, pieces * width), low),
        compiler_params=pltpu.CompilerParams(vmem_limit_bytes=VMEM_BYTES),
        cost_estimate=pl.CostEstimate(flops=0, bytes_accessed=2 << 20, transcendentals=0),
        name="collect",
    )(order, which, *sum(slots, []))


def join_kernel(right_ref, left_ref, w_ref, *outs):
    rows, depth = right_ref.shape
    width = w_ref.shape[1]
    cut = rows * depth // width
    for ref, out_ref in zip((right_ref, left_ref), outs):
        for number in range(depth // width):
            cols = slice(number * width, (number + 1) * width)
            out_ref[number * rows : (number + 1) * rows, :] = ref[:, cols]
        out_ref[cut:, :] = w_ref[...]


def join(right, left, weights):
    rows, depth = right.shape
    height, width = weights.shape
    shape = jax.ShapeDtypeStruct((rows * depth // width + height, width), low)
    return pl.pallas_call(
        join_kernel,
        out_shape=[shape] * 2,
        compiler_params=pltpu.CompilerParams(vmem_limit_bytes=VMEM_BYTES),
        cost_estimate=pl.CostEstimate(flops=0, bytes_accessed=7 << 20, transcendentals=0),
        name="join",
    )(right, left, weights)


def line_up_kernel(order, *refs):
    out_ref = refs[-1]
    height, width = refs[0].shape
    pairs = out_ref.shape[0] // height // (len(refs) - 1)
    each = width // pairs
    for number, ref in enumerate(refs[:-1]):
        for pair in range(pairs):
            start = (order[number] * pairs + pair) * height
            rows = pl.ds(pl.multiple_of(start, height), height)
            out_ref[rows, :] = ref[:, pair * each : (pair + 1) * each]


def line_up(order, arrived, pairs):
    height, width = arrived[0].shape
    shape = (len(arrived) * pairs * height, width // pairs)
    spec = pltpu.PrefetchScalarGridSpec(
        num_scalar_prefetch=1,
        grid=(1,),
        in_specs=[pl.BlockSpec((height, width), lambda i, o: (0, 0))] * len(arrived),
        out_specs=pl.BlockSpec(shape, lambda i, o: (0, 0)),
    )
    return pl.pallas_call(
        line_up_kernel,
        grid_spec=spec,
        out_shape=jax.ShapeDtypeStruct(shape, low),
        compiler_params=pltpu.CompilerParams(vmem_limit_bytes=VMEM_BYTES),
        cost_estimate=pl.CostEstimate(flops=0, bytes_accessed=2 << 20, transcendentals=0),
        name="line_up",
    )(order, *arrived)


def turn_kernel(facts, own_ref, came_ref, state_ref, c_ref, gain_ref, w_ref, grad_ref, low_ref, *asked):
    normed_grad = own_ref[...] + came_ref[...]
    gain = gain_ref[1:2, :].astype(wide)
    _, unit, factor = rms_parts(state_ref[...], gain)
    state_grad = c_ref[...].astype(wide) + rms_back(normed_grad, unit, factor, gain)
    branch_grad = state_grad.astype(low)
    grad_ref[...] = state_grad
    low_ref[...] = branch_grad
    chunk = own_ref.shape[0]
    start = facts[1] * chunk * pl.num_programs(0) + pl.program_id(0) * chunk
    valid = start + lax.broadcasted_iota(jnp.int32, (chunk, 1), 0) < facts[0]
    heads_grad = jnp.where(valid, dot_nt(branch_grad, w_ref[...]), 0.0).astype(low)
    line = asked[0].shape[0]
    for z in range(line):
        for pair, ref in enumerate(asked):
            column = (z * len(asked) + pair) * LANES
            ref[z] = heads_grad[:, column : column + LANES]


def turn(facts, own, came, hidden_state, cotangent, pack, out_full, line, pairs):
    rows, depth = own.shape
    chunk = rows // 2
    gain_block = pack.shape[0] // GAIN_ROWS - 1
    block = pl.BlockSpec((chunk, depth), lambda i, f: (i, 0))
    piece = pl.BlockSpec((line, chunk, LANES), lambda i, f: (0, i, 0))
    spec = pltpu.PrefetchScalarGridSpec(
        num_scalar_prefetch=1,
        grid=(rows // chunk,),
        in_specs=[
            block, block, block, block,
            pl.BlockSpec((GAIN_ROWS, depth), lambda i, f: (gain_block, 0)),
            pl.BlockSpec((depth, depth), lambda i, f: (0, 0)),
        ],
        out_specs=[block, block] + [piece] * pairs,
    )
    return pl.pallas_call(
        turn_kernel,
        grid_spec=spec,
        out_shape=[
            jax.ShapeDtypeStruct((rows, depth), wide),
            jax.ShapeDtypeStruct((rows, depth), low),
        ]
        + [jax.ShapeDtypeStruct((line, rows, LANES), low)] * pairs,
        compiler_params=pltpu.CompilerParams(vmem_limit_bytes=VMEM_BYTES),
        cost_estimate=pl.CostEstimate(
            flops=2 * rows * depth * depth, bytes_accessed=13 << 20, transcendentals=0
        ),
        name="turn",
    )(facts, own, came, hidden_state, cotangent, pack, out_full)


def unproject_kernel(normed_ref, *refs):
    mixed_refs, (dw_ref, acc_ref) = refs[:-2], refs[-2:]
    step = pl.program_id(0)

    @pl.when(step == 0)
    def _():
        acc_ref[...] = jnp.zeros_like(acc_ref)

    height = mixed_refs[0].shape[1]
    for number, ref in enumerate(mixed_refs):
        acc_ref[number * height : (number + 1) * height, :] += dot_tn(ref[...], normed_ref[...])

    @pl.when(step == pl.num_programs(0) - 1)
    def _():
        dw_ref[...] = acc_ref[...].astype(low)


def unproject(normed, mixed_grads):
    tokens, depth = normed.shape
    rows = 512
    height = mixed_grads[0].shape[1]
    total = height * len(mixed_grads)
    block = lambda width: pl.BlockSpec((rows, width), lambda o: (o, 0))
    return pl.pallas_call(
        unproject_kernel,
        grid=(tokens // rows,),
        in_specs=[block(depth)] + [block(height)] * len(mixed_grads),
        out_specs=pl.BlockSpec((total, depth), lambda o: (0, 0)),
        scratch_shapes=[pltpu.VMEM((total, depth), wide)],
        out_shape=jax.ShapeDtypeStruct((total, depth), low),
        compiler_params=pltpu.CompilerParams(vmem_limit_bytes=VMEM_BYTES),
        cost_estimate=pl.CostEstimate(flops=0, bytes_accessed=0, transcendentals=0),
        name="unproject",
    )(normed, *mixed_grads)


def finish_kernel(came_ref, w_ref, part_ref, x_ref, gain_ref, state_ref, out_ref):
    normed_grad = part_ref[...]
    for number in range(came_ref.shape[0]):
        normed_grad += dot_nn(came_ref[number], w_ref[number, 0])
    gain = gain_ref[0:1, :].astype(wide)
    _, unit, factor = rms_parts(x_ref[...].astype(wide), gain)
    out_ref[...] = state_ref[...] + rms_back(normed_grad, unit, factor, gain)


def finish(came, qkv_full, part, tokens, pack, state_grad):
    line, rows, height = came.shape
    pairs, depth = qkv_full.shape[1], qkv_full.shape[3]
    gain_block = pack.shape[0] // GAIN_ROWS - 1
    chunk = rows // 2
    block = pl.BlockSpec((chunk, depth), lambda i: (i, 0))
    return pl.pallas_call(
        finish_kernel,
        grid=(rows // chunk,),
        in_specs=[
            pl.BlockSpec((line, chunk, height), lambda i: (0, i, 0)),
            pl.BlockSpec((line, 1, height, depth), lambda i: (0, pairs - 1, 0, 0)),
            block,
            block,
            pl.BlockSpec((GAIN_ROWS, depth), lambda i: (gain_block, 0)),
            block,
        ],
        out_specs=block,
        out_shape=jax.ShapeDtypeStruct((rows, depth), wide),
        compiler_params=pltpu.CompilerParams(vmem_limit_bytes=VMEM_BYTES),
        cost_estimate=pl.CostEstimate(
            flops=FINISH_FLOPS, bytes_accessed=10 << 20, transcendentals=0
        ),
        name="finish",
    )(came, qkv_full, part, tokens, pack, state_grad)


def arrival_order(place):
    ways = jnp.where(place < 2, 1, -1)
    far = jnp.where(place % 2 == 0, 3, 0)
    return jnp.stack([place, place + ways, place + 2 * ways, far]).astype(jnp.int32)


def gather_all(tokens, weights, end, place, chips, use, then, send):
    near = place < 2
    rows, depth = tokens.shape
    width = weights.shape[1]
    cut = rows * depth // width

    def hop(ends):
        return (
            lax.ppermute(ends[0], "head", [(0, 1), (1, 2), (2, 3)]),
            lax.ppermute(ends[1], "head", [(1, 0), (2, 1), (3, 2)]),
        )

    def nearest(hops):
        return jnp.where(near, hops[-1][1], hops[-1][0])

    def farthest(hops):
        return jnp.where(
            place % 3 == 0, nearest(hops), jnp.where(near, hops[0][0], hops[0][1])
        )

    def plane(slot):
        if chips != 4:
            return [lax.all_gather(slot[:end], "chip", axis=1, tiled=True)]
        return [slot[:end]] + [
            lax.ppermute(slot[:end], "chip", [(c, c ^ away) for c in range(chips)])
            for away in range(1, chips)
        ]

    barrier = lax.optimization_barrier
    slots, planes = [weights], []
    token_hops, weight_hops = [], []
    ends = barrier(hop((tokens, tokens)))
    first_block = nearest([ends])
    ends = tuple(join(*ends, weights))
    token_hops.append(tuple(end[:cut] for end in ends))

    ends = hop(ends)
    planes.append(plane(weights))
    used = use(0, tokens, None)
    ends, planes, used = barrier((ends, planes, used))
    token_hops.append(tuple(end[:cut] for end in ends))
    weight_hops.append(tuple(end[cut:] for end in ends))
    slots.append(nearest(weight_hops))
    second_block = nearest(token_hops)

    ends = hop(ends)
    planes.append(plane(slots[1]))
    used = use(1, first_block, used)
    used = use(2, second_block, used)
    ends, planes, used = barrier((ends, planes, used))
    token_hops.append(tuple(end[:cut] for end in ends))
    weight_hops.append(tuple(end[cut:] for end in ends))
    slots.append(nearest(weight_hops))
    used = use(3, farthest(token_hops), used)

    ends = hop(weight_hops[-1])
    planes.append(plane(slots[2]))
    made, used = then(0, used)
    ends, planes, made, used = barrier((ends, planes, made, used))
    sent = [send(made[0])]
    weight_hops.append(ends)
    slots.append(farthest(weight_hops))
    planes.append(plane(slots[3]))
    more, used = then(1, used)
    planes, more, sent = barrier((planes, more, sent))
    sent.append(send(more[0]))
    return planes, slots, used, [made, more], sent


def exchange(pieces):
    return lax.all_to_all(pieces, "head", split_axis=0, concat_axis=0)


def exchange_turned(pieces, place):
    count = pieces.shape[0]
    came = []
    for j in range(count):
        piece = lax.dynamic_index_in_dim(pieces, (place + j) % count, 0, keepdims=False)
        came.append(
            lax.ppermute(piece, "head", [(k, (k + j) % count) for k in range(count)]) if j else piece
        )
    return came


def other_core(array):
    return lax.ppermute(array, "core", [(0, 1), (1, 0)])


def by_core(core, own, came, axis):
    first = jnp.where(core == 0, own, came)
    second = jnp.where(core == 0, came, own)
    return jnp.concatenate([first, second], axis=axis)


def shards(
    tokens, first_values, mixer_in, mixer_out, gate_up, down_weight, norm_gains, lengths, cotangent
):
    line = lax.axis_size("head")
    chips = lax.axis_size("chip")
    place = lax.axis_index("head")
    core = lax.axis_index("core")
    rows, depth = tokens.shape
    cols = mixer_in.shape[2]
    width = mixer_in.shape[1]
    units = down_weight.shape[0] // 2
    pairs = cols // LANES
    after = lax.optimization_barrier

    def halves(array, axis):
        first, second = jnp.split(array, 2, axis=axis)
        return jnp.where(core == 0, first, second), jnp.where(core == 0, second, first)

    def chip_scatter(grad):
        grad = grad.reshape(*grad.shape[:-1], chips, 2 * width)
        return lax.psum_scatter(jnp.moveaxis(grad, -2, 0), "chip", scatter_dimension=0)

    def before(given, *results):
        return after((given, *results))[0]

    qkv_low = mixer_in.astype(low)
    gain_low = norm_gains.astype(low)
    gain_rows = jnp.pad(gain_low, ((0, GAIN_ROWS - 2), (0, 0)))
    qkv_rows = qkv_low.reshape(3, width, pairs, LANES).transpose(2, 0, 3, 1)
    qkv_rows = qkv_rows.reshape(3 * cols, width)
    pack = lax.all_gather(
        jnp.concatenate([qkv_rows, gain_rows], axis=0), ("chip", "core"), axis=1, tiled=True
    )
    gain_second = pack[3 * cols + 1].astype(wide)

    gates_low = gate_up.astype(low)
    feed_rows = jnp.concatenate(
        [gates_low.transpose(0, 2, 1), down_weight.astype(low)[None]], axis=0
    ).reshape(3, 2, units, width)
    out_low = mixer_out.astype(low).reshape(2, cols // 2, width)

    def half_rows(which):
        return jnp.concatenate([out_low[which], feed_rows[:, which].reshape(3 * units, width)])

    first_rows, second_rows = half_rows(0), half_rows(1)
    own_rows = jnp.where(core == 0, first_rows, second_rows)
    other_rows = jnp.where(core == 0, second_rows, first_rows)
    own_rows = by_core(core, own_rows, other_core(other_rows), -1)
    end = own_rows.shape[0]
    qkv_sides = jnp.concatenate(jnp.split(qkv_rows, pairs), axis=-1)
    weights = jnp.concatenate([own_rows, qkv_sides])

    order = arrival_order(place)
    place_one = place[None].astype(jnp.int32)
    chip = lax.axis_index("chip")
    which = (chip ^ jnp.arange(4) if chips == 4 else jnp.zeros(1)).astype(jnp.int32)
    cosine, sine = rope_tables()

    def use(number, x, made):
        index = order[number : number + 1]
        return project(index, x, pack, first_values, cosine, sine, made or [])

    def then(pair, made):
        return attend(pair, lengths, *made[:3]), made

    def send(result):
        return exchange(result.reshape(line, rows, LANES))

    planes, slots, made, attended_parts, attended_pieces = gather_all(
        tokens, weights, end, place, chips, use, then, send
    )
    query, keys, values, normed_a = made
    cot_other = other_core(cotangent)
    out_half = collect(order, which, planes, cols // 2).reshape(line, 1, cols // 2, depth)
    qkv_sides, out_half = after(([slot[end:] for slot in slots], out_half))
    out_heads = by_core(core, out_half, other_core(out_half), 1)
    out_full = out_heads.reshape(depth, depth)
    lined = chips == 4
    attended_wide = [part[1] for part in attended_parts]
    log_total = [part[2] for part in attended_parts]
    attended = jnp.stack(attended_pieces, axis=1).transpose(2, 0, 1, 3).reshape(rows, depth)

    qkv_line = line_up(order, qkv_sides, pairs)
    qkv_full = lax.all_gather(qkv_line, ("chip", "core"), axis=1, tiled=True)
    qkv_full = qkv_full.reshape(line, pairs, 3 * LANES, depth)

    token_rows = tokens.astype(wide)
    hidden_state = token_rows + dot_nn(attended, out_full)
    normed_b = rms_parts(hidden_state, gain_second)[0].astype(low)
    branch_own, branch_other, grad_own, grad_other, gate_grad, down_grad = feed(
        order, which, planes, units, normed_b, other_core(normed_b), cotangent, cot_other
    )
    facts = jnp.concatenate([lengths, place_one])
    state_grad, branch_grad, *asked = turn(
        facts, grad_own, before(other_core(grad_other), qkv_full), hidden_state, cotangent, pack,
        out_full, line, pairs,
    )
    branch_b = branch_own + other_core(branch_other)
    block_out = (hidden_state + branch_b).astype(low)

    def settle(grad):
        kept, given = halves(grad, -1)
        return by_core(core, kept[..., None, :, :], other_core(given)[..., None, :, :], -3)

    def plane_sum(grad):
        if chips != 4:
            return chip_scatter(grad).astype(wide)
        pieces = [
            lax.dynamic_slice_in_dim(grad, (chip ^ away) * 2 * width, 2 * width, 1)
            for away in range(chips)
        ]
        moved = [
            lax.ppermute(pieces[away], "chip", [(c, c ^ away) for c in range(chips)])
            for away in range(1, chips)
        ]
        return sum(piece.astype(wide) for piece in [pieces[0]] + moved)

    def spread(grad):
        if not lined:
            grad = grad.reshape(line, -1, chips, 2 * width).transpose(2, 0, 1, 3)
        return grad

    down_sum = lax.psum_scatter(spread(down_grad), "chip", scatter_dimension=0)
    def back(pair, came):
        return attend_back(
            pair, lengths, query, keys, values, came.reshape(line * rows, LANES),
            attended_wide[pair], log_total[pair], cosine, sine,
        )

    came = exchange(asked[0])
    out_grad = dot_tn(attended, branch_grad).astype(low).reshape(line, cols, depth)
    kept, given = halves(out_grad, 1)
    out_grad = (kept.astype(wide) + other_core(given).astype(wide)).astype(low)
    out_grad = jnp.moveaxis(out_grad.reshape(line, cols // 2, chips, 2 * width), 2, 0)
    gate_grad = spread(gate_grad).at[:, :, : cols // 2].set(out_grad)
    came, gate_grad, asked, down_sum, block_out = after(
        (came, gate_grad, asked, down_sum, block_out)
    )

    gate_sum = lax.psum_scatter(gate_grad, "chip", scatter_dimension=0)
    mixed_first = back(0, came)
    came = exchange(asked[1])
    down_came = exchange_turned(down_sum, place)
    came, mixed_first, down_came = after((came, mixed_first, down_came))

    mixed_second = back(1, came)
    mixed_rows = exchange(mixed_first[0].reshape(line, rows, 3 * LANES))
    mixed_rows, mixed_second = after((mixed_rows, mixed_second))

    came = exchange(mixed_second[0].reshape(line, rows, 3 * LANES))
    gate_came = exchange_turned(after(gate_sum), place)
    qkv_grad = unproject(normed_a, [mixed_first[0], mixed_second[0]])
    kept, given = halves(qkv_grad, 0)
    qkv_grad = (kept.astype(wide) + other_core(given).astype(wide)).astype(low)
    came, gate_came, qkv_grad = after((came, gate_came, qkv_grad))

    qkv_sum = settle(plane_sum(qkv_grad)).reshape(pairs, 3, LANES, width)
    mixer_in_grad = qkv_sum.transpose(1, 3, 0, 2).reshape(3, width, cols)
    normed_a_grad = jnp.einsum(
        "ztc,zcd->td", mixed_rows, qkv_full[:, 0], preferred_element_type=wide
    )
    tokens_grad = finish(came, qkv_full, normed_a_grad, tokens, pack, state_grad)
    down_sum = sum(piece.astype(wide) for piece in down_came)
    down_grad = settle(down_sum).reshape(2 * units, width)
    weights_sum = sum(piece.astype(wide) for piece in gate_came)
    mixer_out_grad = settle(weights_sum[: cols // 2]).reshape(cols, width)
    gate_up_grad = settle(weights_sum[cols // 2 :].reshape(2, units, 2 * width))
    gate_up_grad = gate_up_grad.reshape(2, 2 * units, width).transpose(0, 2, 1)

    gain_parts = jnp.stack(
        [
            jnp.sum(qkv_low.astype(wide) * mixer_in_grad, axis=(0, 2)),
            jnp.sum(gates_low.astype(wide) * gate_up_grad, axis=(0, 2)),
        ]
    )
    gains_grad = sum(exchange_turned(jnp.broadcast_to(gain_parts, (line, 2, width)), place))
    gains_grad = gains_grad / gain_low.astype(wide)
    first_grad = jnp.concatenate([mixed_first[1], mixed_second[1]], axis=1)
    return (
        block_out,
        tokens_grad,
        first_grad,
        mixer_in_grad,
        mixer_out_grad,
        gate_up_grad,
        down_grad,
        gains_grad,
    )


def solution(mesh):
    groups, line = mesh.shape["dp"], mesh.shape["head"]
    fine = jax.sharding.Mesh(
        mesh.devices.reshape(groups // 2, 2, line), ("chip", "core", "head")
    )
    dp = ("chip", "core")
    return jax.shard_map(
        shards,
        mesh=fine,
        in_specs=(
            P(("chip", "core", "head"), None),
            P(dp, "head"),
            P(None, dp, "head"),
            P("head", dp),
            P(None, dp, "head"),
            P("head", dp),
            P(None, dp),
            P(dp),
            P(("chip", "core", "head"), None),
        ),
        out_specs=(
            P(("chip", "core", "head"), None),
            P(("chip", "core", "head"), None),
            P(dp, "head"),
            P(None, dp, "head"),
            P("head", dp),
            P(None, dp, "head"),
            P("head", dp),
            P(None, dp),
        ),
        check_vma=False,
    )
```

```python
import functools

import jax
import jax.numpy as jnp
from jax import lax
from jax.experimental import pallas as pl
from jax.experimental.pallas import tpu as pltpu
from jax.sharding import PartitionSpec as P

HDIM = 64
SEQ = 2048
LANES = 128
GAIN_ROWS = 16

epsilon = 1e-05
far_below = -1e30
rope_base = 10000.0
low = jnp.bfloat16
wide = jnp.float32
VMEM_BYTES = 60 * 1024 * 1024
FINISH_FLOPS = 1 << 38


def dot_nn(a, b):
    return lax.dot_general(a, b, (((1,), (0,)), ((), ())), preferred_element_type=wide)


def dot_nt(a, b):
    return lax.dot_general(a, b, (((1,), (1,)), ((), ())), preferred_element_type=wide)


def dot_tn(a, b):
    return lax.dot_general(a, b, (((0,), (0,)), ((), ())), preferred_element_type=wide)


def rope_tables():
    half = HDIM // 2
    rates = rope_base ** (-jnp.arange(half, dtype=wide) * 2.0 / HDIM)
    angles = jnp.arange(SEQ, dtype=wide)[:, None] * rates[None, :]
    cosine, sine = jnp.cos(angles), jnp.sin(angles)
    pair = LANES // HDIM
    return (
        jnp.concatenate([cosine, cosine] * pair, axis=1),
        jnp.concatenate([-sine, sine] * pair, axis=1),
    )


def swap_halves(field):
    half = HDIM // 2
    lane = lax.broadcasted_iota(jnp.int32, field.shape, 1)
    ahead = pltpu.roll(field, LANES - half, 1)
    behind = pltpu.roll(field, half, 1)
    return jnp.where(lane % HDIM < half, ahead, behind)


def rms_parts(field, gain):
    factor = lax.rsqrt(jnp.mean(field * field, axis=-1, keepdims=True) + epsilon)
    unit = field * factor
    return (unit * gain, unit, factor)


def rms_back(normed_grad, unit, factor, gain):
    scaled = normed_grad * gain
    return factor * (scaled - unit * jnp.mean(scaled * unit, axis=-1, keepdims=True))


def project_kernel(place, x_ref, w_ref, gain_ref, first_ref, cos_ref, sin_ref, *refs):
    q_ref, k_ref, v_ref, normed_ref = refs[-4:]
    rows, depth = normed_ref.shape
    width = x_ref.shape[1]
    if width == depth:
        width = depth // 4
        blocks = [x_ref[:, start : start + width].astype(wide) for start in range(0, depth, width)]
    else:
        starts = range(0, x_ref.shape[0], rows)
        blocks = [x_ref[start : start + rows, :].astype(wide) for start in starts]
    squares = sum(jnp.sum(block * block, axis=-1, keepdims=True) for block in blocks)
    factor = lax.rsqrt(squares / depth + epsilon)
    for number, block in enumerate(blocks):
        cols = slice(number * width, (number + 1) * width)
        normed_ref[:, cols] = (block * factor * gain_ref[0:1, cols].astype(wide)).astype(low)
    normed = normed_ref[...]
    cosine, sine = cos_ref[...], sin_ref[...]
    for pair in range(q_ref.shape[1] // LANES):
        cols = slice(pair * LANES, (pair + 1) * LANES)
        start = pair * 3 * LANES
        mixed = dot_nt(normed, w_ref[start : start + 3 * LANES, :])
        for part, out_ref in ((0, q_ref), (1, k_ref)):
            piece = mixed[:, part * LANES : (part + 1) * LANES]
            out_ref[:, cols] = (piece * cosine + swap_halves(piece) * sine).astype(low)
        first = first_ref[:, cols].astype(wide)
        v_ref[:, cols] = (0.5 * mixed[:, 2 * LANES :] + 0.5 * first).astype(low)


def project(index, x, pack, first_values, cosine, sine, made):
    total, cols = first_values.shape
    depth = pack.shape[1]
    rows = x.shape[0] * x.shape[1] // depth
    gain_block = pack.shape[0] // GAIN_ROWS - 1
    fixed = lambda i, p: (0, 0)
    natural = lambda width: pl.BlockSpec((rows, width), lambda i, p: (p[0], 0))
    shapes = [cols, cols, cols, depth]
    spec = pltpu.PrefetchScalarGridSpec(
        num_scalar_prefetch=1,
        grid=(1,),
        in_specs=[
            pl.BlockSpec(x.shape, fixed),
            pl.BlockSpec((3 * cols, depth), fixed),
            pl.BlockSpec((GAIN_ROWS, depth), lambda i, p: (gain_block, 0)),
            natural(cols),
            natural(LANES),
            natural(LANES),
        ]
        + [pl.BlockSpec(memory_space=pl.ANY)] * len(made),
        out_specs=[natural(width) for width in shapes],
    )
    return pl.pallas_call(
        project_kernel,
        grid_spec=spec,
        out_shape=[jax.ShapeDtypeStruct((total, width), low) for width in shapes],
        input_output_aliases={7 + number: number for number in range(len(made))},
        compiler_params=pltpu.CompilerParams(vmem_limit_bytes=VMEM_BYTES),
        cost_estimate=pl.CostEstimate(
            flops=2 * rows * depth * 3 * cols, bytes_accessed=5 << 20, transcendentals=0
        ),
        name="project",
    )(index, x, pack, pack, first_values, cosine, sine, *made)


BLOCK = 512


def both_heads(array):
    lane = lax.broadcasted_iota(jnp.int32, array.shape, 1)
    zero = jnp.zeros_like(array)
    return jnp.concatenate(
        [jnp.where(lane < HDIM, array, zero), jnp.where(lane < HDIM, zero, array)], axis=0
    )


def attend_kernel(len_ref, q_ref, k_ref, v_ref, out_ref, full_ref, lse_ref, acc_ref, max_ref, sum_ref):
    i = pl.program_id(0)
    own = both_heads(q_ref[...] * jnp.asarray(HDIM**-0.5, low))
    max_ref[...] = jnp.full_like(max_ref, far_below)
    sum_ref[...] = jnp.zeros_like(sum_ref)
    acc_ref[...] = jnp.zeros_like(acc_ref)

    def step(j, diagonal):
        at = pl.ds(pl.multiple_of(j * BLOCK, BLOCK), BLOCK)
        scores = dot_nt(own, k_ref[at, :])
        if diagonal:
            q_at = lax.broadcasted_iota(jnp.int32, (BLOCK, BLOCK), 0)
            k_at = lax.broadcasted_iota(jnp.int32, (BLOCK, BLOCK), 1)
            allowed = k_at <= q_at
            allowed = jnp.concatenate([allowed, allowed], axis=0)
            scores = jnp.where(allowed, scores, far_below)
        old = max_ref[...]
        peak = jnp.maximum(old, jnp.max(scores, axis=1, keepdims=True))
        decay = jnp.exp(old - peak)
        max_ref[...] = peak
        total = sum_ref[...] * decay
        powers = []
        for start in range(0, BLOCK, LANES):
            power = jnp.exp(scores[:, start : start + LANES] - peak)
            total += power
            powers.append(power.astype(low))
        sum_ref[...] = total
        acc_ref[...] = acc_ref[...] * decay + dot_nn(jnp.concatenate(powers, axis=1), v_ref[at, :])

    @pl.loop(0, i)
    def _(j):
        step(j, False)

    step(i, True)
    total = jnp.sum(sum_ref[...], axis=1, keepdims=True)
    log_total = max_ref[...] + jnp.log(total)
    for head in range(LANES // HDIM):
        rows = slice(head * BLOCK, (head + 1) * BLOCK)
        lse_ref[head : head + 1, :] = jnp.transpose(log_total[rows])[0:1, :]
    result = acc_ref[...] / total
    lane = lax.broadcasted_iota(jnp.int32, (BLOCK, LANES), 1)
    valid = i * BLOCK + lax.broadcasted_iota(jnp.int32, (BLOCK, 1), 0) < len_ref[0]
    result = jnp.where(valid, jnp.where(lane < HDIM, result[:BLOCK], result[BLOCK:]), 0.0)
    out_ref[...] = result.astype(low)
    full_ref[...] = result


def attend(pair, lengths, query, keys, values):
    rows = query.shape[0]
    block = pl.BlockSpec((BLOCK, LANES), lambda i, n: (i, pair))
    whole = pl.BlockSpec((rows, LANES), lambda i, n: (0, pair))
    result = pl.BlockSpec((BLOCK, LANES), lambda i, n: (i, 0))
    spec = pltpu.PrefetchScalarGridSpec(
        num_scalar_prefetch=1,
        grid=(rows // BLOCK,),
        in_specs=[block, whole, whole],
        out_specs=[result, result, pl.BlockSpec((8, BLOCK), lambda i, n: (0, i))],
        scratch_shapes=[pltpu.VMEM((2 * BLOCK, LANES), wide)] * 3,
    )
    return pl.pallas_call(
        attend_kernel,
        grid_spec=spec,
        out_shape=[
            jax.ShapeDtypeStruct((rows, LANES), low),
            jax.ShapeDtypeStruct((rows, LANES), wide),
            jax.ShapeDtypeStruct((8, rows), wide),
        ],
        compiler_params=pltpu.CompilerParams(vmem_limit_bytes=VMEM_BYTES),
        cost_estimate=pl.CostEstimate(
            flops=8 * rows * rows * LANES, bytes_accessed=4 << 20, transcendentals=rows * rows
        ),
        name="attend",
    )(lengths, query, keys, values)


def attend_back_kernel(
    len_ref, q_ref, k_ref, v_ref, grad_ref, full_ref, lse_ref, cos_ref, sin_ref,
    mixed_ref, first_ref, dk_acc, dv_acc, dq_acc, keys_t,
):
    i = pl.program_id(0)
    count = pl.num_programs(0)
    heads = range(LANES // HDIM)

    @pl.when(i == 0)
    def _():
        dk_acc[...] = jnp.zeros_like(dk_acc)
        dv_acc[...] = jnp.zeros_like(dv_acc)
        for start in range(0, k_ref.shape[0], BLOCK):
            keys_t[:, start : start + BLOCK] = jnp.transpose(k_ref[start : start + BLOCK, :])

    grad = grad_ref[...]
    own = both_heads(q_ref[...] * jnp.asarray(HDIM**-0.5, low))
    own_grad = both_heads(grad)
    columns = [slice(head * HDIM, (head + 1) * HDIM) for head in heads]
    products = jnp.transpose(grad.astype(wide) * full_ref[...])
    offset = jnp.concatenate(
        [jnp.sum(products[rows], axis=0, keepdims=True) for rows in columns], axis=1
    )
    log_total = jnp.concatenate([lse_ref[head : head + 1, :] for head in heads], axis=1)
    dq_acc[...] = jnp.zeros_like(dq_acc)

    def step(j, diagonal):
        at = pl.ds(pl.multiple_of(j * BLOCK, BLOCK), BLOCK)
        scores = dot_nt(k_ref[at, :], own)
        if diagonal:
            k_at = lax.broadcasted_iota(jnp.int32, (BLOCK, BLOCK), 0)
            q_at = lax.broadcasted_iota(jnp.int32, (BLOCK, BLOCK), 1)
            allowed = k_at <= q_at
            allowed = jnp.concatenate([allowed, allowed], axis=1)
            scores = jnp.where(allowed, scores, far_below)
        probs = jnp.exp(scores - log_total)
        prob_grad = dot_nt(v_ref[at, :], own_grad)
        dv_acc[at, :] += dot_nn(probs.astype(low), own_grad)
        raw_grad = (probs * (prob_grad - offset)).astype(low)
        dk_acc[at, :] += dot_nn(raw_grad, own)
        for head, rows in zip(heads, columns):
            dq_acc[rows, :] += dot_nn(
                keys_t[rows, at], raw_grad[:, head * BLOCK : (head + 1) * BLOCK]
            )

    @pl.loop(0, i)
    def _(j):
        step(j, False)

    step(i, True)
    at = pl.ds(pl.multiple_of(i * BLOCK, BLOCK), BLOCK)
    query_grad = jnp.transpose(dq_acc[...]) * HDIM**-0.5
    mixed_ref[at, :LANES] = (
        query_grad * cos_ref[at, :] - swap_halves(query_grad) * sin_ref[at, :]
    ).astype(low)

    @pl.when(i == count - 1)
    def _():
        @pl.loop(0, count)
        def _(j):
            at = pl.ds(pl.multiple_of(j * BLOCK, BLOCK), BLOCK)
            keys_grad = dk_acc[at, :]
            mixed_ref[at, LANES : 2 * LANES] = (
                keys_grad * cos_ref[at, :] - swap_halves(keys_grad) * sin_ref[at, :]
            ).astype(low)
            half_grad = 0.5 * dv_acc[at, :]
            first_ref[at, :] = half_grad
            mixed_ref[at, 2 * LANES :] = half_grad.astype(low)


def attend_back(pair, lengths, query, keys, values, grad, full, lse, cosine, sine):
    rows = query.shape[0]
    block = pl.BlockSpec((BLOCK, LANES), lambda i, n: (i, pair))
    whole = pl.BlockSpec((rows, LANES), lambda i, n: (0, pair))
    given = pl.BlockSpec((BLOCK, LANES), lambda i, n: (i, 0))
    fixed = lambda i, n: (0, 0)
    table = pl.BlockSpec((rows, LANES), fixed)
    spec = pltpu.PrefetchScalarGridSpec(
        num_scalar_prefetch=1,
        grid=(rows // BLOCK,),
        in_specs=[
            block, whole, whole, given, given,
            pl.BlockSpec((8, BLOCK), lambda i, n: (0, i)),
            table, table,
        ],
        out_specs=[pl.BlockSpec((rows, 3 * LANES), fixed), pl.BlockSpec((rows, LANES), fixed)],
        scratch_shapes=[
            pltpu.VMEM((rows, LANES), wide),
            pltpu.VMEM((rows, LANES), wide),
            pltpu.VMEM((LANES, BLOCK), wide),
            pltpu.VMEM((LANES, rows), low),
        ],
    )
    return pl.pallas_call(
        attend_back_kernel,
        grid_spec=spec,
        out_shape=[
            jax.ShapeDtypeStruct((rows, 3 * LANES), low),
            jax.ShapeDtypeStruct((rows, LANES), wide),
        ],
        compiler_params=pltpu.CompilerParams(vmem_limit_bytes=VMEM_BYTES),
        cost_estimate=pl.CostEstimate(
            flops=20 * rows * rows * LANES, bytes_accessed=6 << 20, transcendentals=rows * rows
        ),
        name="attend_back",
    )(lengths, query, keys, values, grad, full, lse, cosine, sine)


def feed_kernel(order, which, *refs):
    given, (x_own, x_other, c_own, c_other) = refs[:-17], refs[-17:-13]
    outs, grads, dgate_ref, ddown_ref = refs[-13:-11], refs[-11:-9], refs[-9], refs[-8]
    weights, x_ref, c_ref, inner_s, mlp_s, weight_sems, row_sems = refs[-7:]
    step = pl.program_id(0)
    parts, depth3, depth = weights.shape
    pieces = len(given) // parts
    width = depth // pieces
    units = depth3 // 3
    rows = x_own.shape[0]
    skipped = given[0].shape[0] - depth3
    chunk = min(512, rows)
    sides = (slice(0, rows), slice(rows, 2 * rows))
    fetches = [
        [
            pltpu.make_async_copy(
                given[number * pieces + c].at[skipped:, :],
                weights.at[number, :, pl.ds(pl.multiple_of(which[c] * width, LANES), width)],
                weight_sems.at[number, c],
            )
            for c in range(pieces)
        ]
        for number in range(parts)
    ]
    loads = [
        pltpu.make_async_copy(source, target.at[side, :], row_sems.at[number])
        for number, (source, target, side) in enumerate(
            zip((x_own, x_other, c_own, c_other), (x_ref, x_ref, c_ref, c_ref), sides * 2)
        )
    ]

    @pl.when(step == 0)
    def _():
        for fetch in fetches[0]:
            fetch.start()
        for load in loads:
            load.start()
        for fetch in sum(fetches[1:], []):
            fetch.start()
        for ref in (*outs, *grads):
            ref[...] = jnp.zeros_like(ref)
        for load in loads:
            load.wait()

    for number in range(parts):

        @pl.when(step == number)
        def _(number=number):
            for fetch in fetches[number]:
                fetch.wait()

    w_ref = weights.at[step]
    for half, (out_ref, grad_ref) in enumerate(zip(outs, grads)):

        @pl.loop(0, rows // chunk)
        def _(t, half=half, out_ref=out_ref, grad_ref=grad_ref):
            at = pl.ds(pl.multiple_of(t * chunk, chunk), chunk)
            along = pl.ds(pl.multiple_of(half * rows + t * chunk, chunk), chunk)
            gated = dot_nt(w_ref[: 2 * units, :], x_ref[along, :])
            inner_grad = dot_nt(w_ref[2 * units :, :], c_ref[along, :])
            gate, up = gated[:units], gated[units:]
            sigmoid = jax.nn.sigmoid(gate)
            silu = gate * sigmoid
            inner = (silu * up).astype(low)
            gate_grad = (inner_grad * up * sigmoid * (1.0 + gate * (1.0 - sigmoid))).astype(low)
            up_grad = (inner_grad * silu).astype(low)
            inner_s[:, along] = inner
            mlp_s[:units, along] = gate_grad
            mlp_s[units:, along] = up_grad
            mlp_grad = jnp.concatenate([gate_grad, up_grad], axis=0)
            out_ref[at, :] += dot_tn(inner, w_ref[2 * units :, :])
            grad_ref[at, :] += dot_tn(mlp_grad, w_ref[: 2 * units, :])

    for c in range(pieces):
        cols = slice(c * width, (c + 1) * width)
        dgate_ref[c, 0, skipped:, :] = dot_nn(mlp_s[...], x_ref[:, cols]).astype(low)
        ddown_ref[c, 0] = dot_nn(inner_s[...], c_ref[:, cols]).astype(low)


def feed(order, which, slots, units, x_own, x_other, c_own, c_other):
    rows, depth = x_own.shape
    parts, pieces, width = len(slots), len(slots[0]), slots[0][0].shape[1]
    gates = slots[0][0].shape[0] - units
    anywhere = pl.BlockSpec(memory_space=pl.ANY)
    activations = pl.BlockSpec((rows, depth), lambda h, o, c: (0, 0), pipeline_mode=pl.Buffered(1))
    block = lambda height: pl.BlockSpec((pieces, 1, height, width), lambda h, o, c: (0, o[h], 0, 0))
    spec = pltpu.PrefetchScalarGridSpec(
        num_scalar_prefetch=2,
        grid=(parts,),
        in_specs=[anywhere] * (parts * pieces + 4),
        out_specs=[activations] * 4 + [block(gates), block(units)],
        scratch_shapes=[
            pltpu.VMEM((parts, 3 * units, depth), low),
            pltpu.VMEM((2 * rows, depth), low),
            pltpu.VMEM((2 * rows, depth), low),
            pltpu.VMEM((units, 2 * rows), low),
            pltpu.VMEM((2 * units, 2 * rows), low),
            pltpu.SemaphoreType.DMA((parts, pieces)),
            pltpu.SemaphoreType.DMA((4,)),
        ],
    )
    return pl.pallas_call(
        feed_kernel,
        grid_spec=spec,
        out_shape=[jax.ShapeDtypeStruct((rows, depth), wide)] * 4
        + [
            jax.ShapeDtypeStruct((pieces, parts, gates, width), low),
            jax.ShapeDtypeStruct((pieces, parts, units, width), low),
        ],
        compiler_params=pltpu.CompilerParams(vmem_limit_bytes=VMEM_BYTES),
        cost_estimate=pl.CostEstimate(
            flops=36 * rows * depth * units * parts,
            bytes_accessed=30 << 20,
            transcendentals=2 * rows * units * parts,
        ),
        name="feed",
    )(order, which, *sum(slots, []), x_own, x_other, c_own, c_other)


def collect_kernel(order, which, *refs):
    out_ref = refs[-1]
    height, width = refs[0].shape
    pieces = out_ref.shape[1] // width
    for number, ref in enumerate(refs[:-1]):
        part, piece = divmod(number, pieces)
        rows = pl.ds(pl.multiple_of(order[part] * height, height), height)
        out_ref[rows, pl.ds(pl.multiple_of(which[piece] * width, LANES), width)] = ref[...]


def collect(order, which, slots, height):
    parts, pieces, width = len(slots), len(slots[0]), slots[0][0].shape[1]
    spec = pltpu.PrefetchScalarGridSpec(
        num_scalar_prefetch=2,
        grid=(1,),
        in_specs=[pl.BlockSpec((height, width), lambda i, o, c: (0, 0))] * (parts * pieces),
        out_specs=pl.BlockSpec((parts * height, pieces * width), lambda i, o, c: (0, 0)),
    )
    return pl.pallas_call(
        collect_kernel,
        grid_spec=spec,
        out_shape=jax.ShapeDtypeStruct((parts * height, pieces * width), low),
        compiler_params=pltpu.CompilerParams(vmem_limit_bytes=VMEM_BYTES),
        cost_estimate=pl.CostEstimate(flops=0, bytes_accessed=2 << 20, transcendentals=0),
        name="collect",
    )(order, which, *sum(slots, []))


def join_kernel(right_ref, left_ref, w_ref, *outs):
    rows, depth = right_ref.shape
    width = w_ref.shape[1]
    cut = rows * depth // width
    for ref, out_ref in zip((right_ref, left_ref), outs):
        for number in range(depth // width):
            cols = slice(number * width, (number + 1) * width)
            out_ref[number * rows : (number + 1) * rows, :] = ref[:, cols]
        out_ref[cut:, :] = w_ref[...]


def join(right, left, weights):
    rows, depth = right.shape
    height, width = weights.shape
    shape = jax.ShapeDtypeStruct((rows * depth // width + height, width), low)
    return pl.pallas_call(
        join_kernel,
        out_shape=[shape] * 2,
        compiler_params=pltpu.CompilerParams(vmem_limit_bytes=VMEM_BYTES),
        cost_estimate=pl.CostEstimate(flops=0, bytes_accessed=7 << 20, transcendentals=0),
        name="join",
    )(right, left, weights)


def line_up_kernel(order, *refs):
    out_ref = refs[-1]
    height, width = refs[0].shape
    pairs = out_ref.shape[0] // height // (len(refs) - 1)
    each = width // pairs
    for number, ref in enumerate(refs[:-1]):
        for pair in range(pairs):
            start = (order[number] * pairs + pair) * height
            rows = pl.ds(pl.multiple_of(start, height), height)
            out_ref[rows, :] = ref[:, pair * each : (pair + 1) * each]


def line_up(order, arrived, pairs):
    height, width = arrived[0].shape
    shape = (len(arrived) * pairs * height, width // pairs)
    spec = pltpu.PrefetchScalarGridSpec(
        num_scalar_prefetch=1,
        grid=(1,),
        in_specs=[pl.BlockSpec((height, width), lambda i, o: (0, 0))] * len(arrived),
        out_specs=pl.BlockSpec(shape, lambda i, o: (0, 0)),
    )
    return pl.pallas_call(
        line_up_kernel,
        grid_spec=spec,
        out_shape=jax.ShapeDtypeStruct(shape, low),
        compiler_params=pltpu.CompilerParams(vmem_limit_bytes=VMEM_BYTES),
        cost_estimate=pl.CostEstimate(flops=0, bytes_accessed=2 << 20, transcendentals=0),
        name="line_up",
    )(order, *arrived)


def turn_kernel(facts, own_ref, came_ref, state_ref, c_ref, gain_ref, w_ref, grad_ref, low_ref, *asked):
    normed_grad = own_ref[...] + came_ref[...]
    gain = gain_ref[1:2, :].astype(wide)
    _, unit, factor = rms_parts(state_ref[...], gain)
    state_grad = c_ref[...].astype(wide) + rms_back(normed_grad, unit, factor, gain)
    branch_grad = state_grad.astype(low)
    grad_ref[...] = state_grad
    low_ref[...] = branch_grad
    chunk = own_ref.shape[0]
    start = facts[1] * chunk * pl.num_programs(0) + pl.program_id(0) * chunk
    valid = start + lax.broadcasted_iota(jnp.int32, (chunk, 1), 0) < facts[0]
    heads_grad = jnp.where(valid, dot_nt(branch_grad, w_ref[...]), 0.0).astype(low)
    line = asked[0].shape[0]
    for z in range(line):
        for pair, ref in enumerate(asked):
            column = (z * len(asked) + pair) * LANES
            ref[z] = heads_grad[:, column : column + LANES]


def turn(facts, own, came, hidden_state, cotangent, pack, out_full, line, pairs):
    rows, depth = own.shape
    chunk = rows // 2
    gain_block = pack.shape[0] // GAIN_ROWS - 1
    block = pl.BlockSpec((chunk, depth), lambda i, f: (i, 0))
    piece = pl.BlockSpec((line, chunk, LANES), lambda i, f: (0, i, 0))
    spec = pltpu.PrefetchScalarGridSpec(
        num_scalar_prefetch=1,
        grid=(rows // chunk,),
        in_specs=[
            block, block, block, block,
            pl.BlockSpec((GAIN_ROWS, depth), lambda i, f: (gain_block, 0)),
            pl.BlockSpec((depth, depth), lambda i, f: (0, 0)),
        ],
        out_specs=[block, block] + [piece] * pairs,
    )
    return pl.pallas_call(
        turn_kernel,
        grid_spec=spec,
        out_shape=[
            jax.ShapeDtypeStruct((rows, depth), wide),
            jax.ShapeDtypeStruct((rows, depth), low),
        ]
        + [jax.ShapeDtypeStruct((line, rows, LANES), low)] * pairs,
        compiler_params=pltpu.CompilerParams(vmem_limit_bytes=VMEM_BYTES),
        cost_estimate=pl.CostEstimate(
            flops=2 * rows * depth * depth, bytes_accessed=13 << 20, transcendentals=0
        ),
        name="turn",
    )(facts, own, came, hidden_state, cotangent, pack, out_full)


def outer_kernel(core, first_ref, second_ref, grad_ref, kept_ref, given_ref):
    grad = grad_ref[...]
    first = dot_tn(first_ref[0], grad).astype(low)
    second = dot_tn(second_ref[0], grad).astype(low)
    lower = core[0] == 0
    kept_ref[0] = jnp.where(lower, first, second)
    given_ref[0] = jnp.where(lower, second, first)


def outer(core, attended_pieces, branch_grad):
    line, rows, width = attended_pieces[0].shape
    depth = branch_grad.shape[1]
    piece = pl.BlockSpec((1, rows, width), lambda z, c: (z, 0, 0))
    out = pl.BlockSpec((1, width, depth), lambda z, c: (z, 0, 0))
    spec = pltpu.PrefetchScalarGridSpec(
        num_scalar_prefetch=1,
        grid=(line,),
        in_specs=[piece, piece, pl.BlockSpec((rows, depth), lambda z, c: (0, 0))],
        out_specs=[out, out],
    )
    return pl.pallas_call(
        outer_kernel,
        grid_spec=spec,
        out_shape=[jax.ShapeDtypeStruct((line, width, depth), low)] * 2,
        compiler_params=pltpu.CompilerParams(vmem_limit_bytes=VMEM_BYTES),
        cost_estimate=pl.CostEstimate(
            flops=4 * line * rows * width * depth, bytes_accessed=4 << 20, transcendentals=0
        ),
        name="outer",
    )(core, *attended_pieces, branch_grad)


def unproject_kernel(normed_ref, *refs):
    mixed_refs, (dw_ref, acc_ref) = refs[:-2], refs[-2:]
    step = pl.program_id(0)

    @pl.when(step == 0)
    def _():
        acc_ref[...] = jnp.zeros_like(acc_ref)

    height = mixed_refs[0].shape[1]
    for number, ref in enumerate(mixed_refs):
        acc_ref[number * height : (number + 1) * height, :] += dot_tn(ref[...], normed_ref[...])

    @pl.when(step == pl.num_programs(0) - 1)
    def _():
        dw_ref[...] = acc_ref[...].astype(low)


def unproject(normed, mixed_grads):
    tokens, depth = normed.shape
    rows = 512
    height = mixed_grads[0].shape[1]
    total = height * len(mixed_grads)
    block = lambda width: pl.BlockSpec((rows, width), lambda o: (o, 0))
    return pl.pallas_call(
        unproject_kernel,
        grid=(tokens // rows,),
        in_specs=[block(depth)] + [block(height)] * len(mixed_grads),
        out_specs=pl.BlockSpec((total, depth), lambda o: (0, 0)),
        scratch_shapes=[pltpu.VMEM((total, depth), wide)],
        out_shape=jax.ShapeDtypeStruct((total, depth), low),
        compiler_params=pltpu.CompilerParams(vmem_limit_bytes=VMEM_BYTES),
        cost_estimate=pl.CostEstimate(flops=0, bytes_accessed=0, transcendentals=0),
        name="unproject",
    )(normed, *mixed_grads)


def finish_kernel(came_ref, w_ref, part_ref, x_ref, gain_ref, state_ref, out_ref):
    normed_grad = part_ref[...]
    for number in range(came_ref.shape[0]):
        normed_grad += dot_nn(came_ref[number], w_ref[number, 0])
    gain = gain_ref[0:1, :].astype(wide)
    _, unit, factor = rms_parts(x_ref[...].astype(wide), gain)
    out_ref[...] = state_ref[...] + rms_back(normed_grad, unit, factor, gain)


def finish(came, qkv_full, part, tokens, pack, state_grad):
    line, rows, height = came.shape
    pairs, depth = qkv_full.shape[1], qkv_full.shape[3]
    gain_block = pack.shape[0] // GAIN_ROWS - 1
    chunk = rows // 2
    block = pl.BlockSpec((chunk, depth), lambda i: (i, 0))
    return pl.pallas_call(
        finish_kernel,
        grid=(rows // chunk,),
        in_specs=[
            pl.BlockSpec((line, chunk, height), lambda i: (0, i, 0)),
            pl.BlockSpec((line, 1, height, depth), lambda i: (0, pairs - 1, 0, 0)),
            block,
            block,
            pl.BlockSpec((GAIN_ROWS, depth), lambda i: (gain_block, 0)),
            block,
        ],
        out_specs=block,
        out_shape=jax.ShapeDtypeStruct((rows, depth), wide),
        compiler_params=pltpu.CompilerParams(vmem_limit_bytes=VMEM_BYTES),
        cost_estimate=pl.CostEstimate(
            flops=FINISH_FLOPS, bytes_accessed=10 << 20, transcendentals=0
        ),
        name="finish",
    )(came, qkv_full, part, tokens, pack, state_grad)


def arrival_order(place):
    ways = jnp.where(place < 2, 1, -1)
    far = jnp.where(place % 2 == 0, 3, 0)
    return jnp.stack([place, place + ways, place + 2 * ways, far]).astype(jnp.int32)


def gather_all(tokens, weights, end, place, chips, use, then, send):
    near = place < 2
    rows, depth = tokens.shape
    width = weights.shape[1]
    cut = rows * depth // width

    def hop(ends):
        return (
            lax.ppermute(ends[0], "head", [(0, 1), (1, 2), (2, 3)]),
            lax.ppermute(ends[1], "head", [(1, 0), (2, 1), (3, 2)]),
        )

    def nearest(hops):
        return jnp.where(near, hops[-1][1], hops[-1][0])

    def farthest(hops):
        return jnp.where(
            place % 3 == 0, nearest(hops), jnp.where(near, hops[0][0], hops[0][1])
        )

    def plane(slot):
        if chips != 4:
            return [lax.all_gather(slot[:end], "chip", axis=1, tiled=True)]
        return [slot[:end]] + [
            lax.ppermute(slot[:end], "chip", [(c, c ^ away) for c in range(chips)])
            for away in range(1, chips)
        ]

    barrier = lax.optimization_barrier
    slots, planes = [weights], []
    token_hops, weight_hops = [], []
    ends = barrier(hop((tokens, tokens)))
    first_block = nearest([ends])
    ends = tuple(join(*ends, weights))
    token_hops.append(tuple(end[:cut] for end in ends))

    ends = hop(ends)
    planes.append(plane(weights))
    used = use(0, tokens, None)
    ends, planes, used = barrier((ends, planes, used))
    token_hops.append(tuple(end[:cut] for end in ends))
    weight_hops.append(tuple(end[cut:] for end in ends))
    slots.append(nearest(weight_hops))
    second_block = nearest(token_hops)

    ends = hop(ends)
    planes.append(plane(slots[1]))
    used = use(1, first_block, used)
    used = use(2, second_block, used)
    ends, planes, used = barrier((ends, planes, used))
    token_hops.append(tuple(end[:cut] for end in ends))
    weight_hops.append(tuple(end[cut:] for end in ends))
    slots.append(nearest(weight_hops))
    used = use(3, farthest(token_hops), used)

    ends = hop(weight_hops[-1])
    planes.append(plane(slots[2]))
    made, used = then(0, used)
    ends, planes, made, used = barrier((ends, planes, made, used))
    sent = [send(made[0])]
    weight_hops.append(ends)
    slots.append(farthest(weight_hops))
    planes.append(plane(slots[3]))
    more, used = then(1, used)
    later = more[0]
    planes, more, sent = barrier((planes, more, sent))
    sent.append(send(barrier((later, sent[0]))[0]))
    planes, sent = barrier((planes, sent))
    return planes, slots, used, [made, more], sent


def exchange(pieces):
    return lax.all_to_all(pieces, "head", split_axis=0, concat_axis=0)


def exchange_turned(pieces, place):
    count = pieces.shape[0]
    came = []
    for j in range(count):
        piece = lax.dynamic_index_in_dim(pieces, (place + j) % count, 0, keepdims=False)
        came.append(
            lax.ppermute(piece, "head", [(k, (k + j) % count) for k in range(count)]) if j else piece
        )
    return came


def other_core(array):
    return lax.ppermute(array, "core", [(0, 1), (1, 0)])


def by_core(core, own, came, axis):
    first = jnp.where(core == 0, own, came)
    second = jnp.where(core == 0, came, own)
    return jnp.concatenate([first, second], axis=axis)


def shards(
    tokens, first_values, mixer_in, mixer_out, gate_up, down_weight, norm_gains, lengths, cotangent
):
    line = lax.axis_size("head")
    chips = lax.axis_size("chip")
    place = lax.axis_index("head")
    core = lax.axis_index("core")
    rows, depth = tokens.shape
    cols = mixer_in.shape[2]
    width = mixer_in.shape[1]
    units = down_weight.shape[0] // 2
    pairs = cols // LANES
    after = lax.optimization_barrier

    def halves(array, axis):
        first, second = jnp.split(array, 2, axis=axis)
        return jnp.where(core == 0, first, second), jnp.where(core == 0, second, first)

    def chip_scatter(grad):
        grad = grad.reshape(*grad.shape[:-1], chips, 2 * width)
        return lax.psum_scatter(jnp.moveaxis(grad, -2, 0), "chip", scatter_dimension=0)

    def before(given, *results):
        return after((given, *results))[0]

    qkv_low = mixer_in.astype(low)
    gain_low = norm_gains.astype(low)
    gain_rows = jnp.pad(gain_low, ((0, GAIN_ROWS - 2), (0, 0)))
    qkv_rows = qkv_low.reshape(3, width, pairs, LANES).transpose(2, 0, 3, 1)
    qkv_rows = qkv_rows.reshape(3 * cols, width)
    pack = lax.all_gather(
        jnp.concatenate([qkv_rows, gain_rows], axis=0), ("chip", "core"), axis=1, tiled=True
    )
    gain_second = pack[3 * cols + 1].astype(wide)

    gates_low = gate_up.astype(low)
    feed_rows = jnp.concatenate(
        [gates_low.transpose(0, 2, 1), down_weight.astype(low)[None]], axis=0
    ).reshape(3, 2, units, width)
    out_low = mixer_out.astype(low).reshape(2, cols // 2, width)

    def half_rows(which):
        return jnp.concatenate([out_low[which], feed_rows[:, which].reshape(3 * units, width)])

    first_rows, second_rows = half_rows(0), half_rows(1)
    own_rows = jnp.where(core == 0, first_rows, second_rows)
    other_rows = jnp.where(core == 0, second_rows, first_rows)
    own_rows = by_core(core, own_rows, other_core(other_rows), -1)
    end = own_rows.shape[0]
    qkv_sides = jnp.concatenate(jnp.split(qkv_rows, pairs), axis=-1)
    weights = jnp.concatenate([own_rows, qkv_sides])

    order = arrival_order(place)
    place_one = place[None].astype(jnp.int32)
    chip = lax.axis_index("chip")
    which = (chip ^ jnp.arange(4) if chips == 4 else jnp.zeros(1)).astype(jnp.int32)
    cosine, sine = rope_tables()

    def use(number, x, made):
        index = order[number : number + 1]
        return project(index, x, pack, first_values, cosine, sine, made or [])

    def then(pair, made):
        return attend(pair, lengths, *made[:3]), made

    def send(result):
        return exchange(result.reshape(line, rows, LANES))

    planes, slots, made, attended_parts, attended_pieces = gather_all(
        tokens, weights, end, place, chips, use, then, send
    )
    query, keys, values, normed_a = made
    cot_other = other_core(cotangent)
    out_half = collect(order, which, planes, cols // 2).reshape(line, 1, cols // 2, depth)
    qkv_sides, out_half = after(([slot[end:] for slot in slots], out_half))
    out_heads = by_core(core, out_half, other_core(out_half), 1)
    out_full = out_heads.reshape(depth, depth)
    lined = chips == 4
    attended_wide = [part[1] for part in attended_parts]
    log_total = [part[2] for part in attended_parts]
    attended = jnp.stack(attended_pieces, axis=1).transpose(2, 0, 1, 3).reshape(rows, depth)

    qkv_line = line_up(order, qkv_sides, pairs)
    qkv_full = lax.all_gather(qkv_line, ("chip", "core"), axis=1, tiled=True)
    qkv_full = qkv_full.reshape(line, pairs, 3 * LANES, depth)

    token_rows = tokens.astype(wide)
    hidden_state = token_rows + dot_nn(attended, out_full)
    normed_b = rms_parts(hidden_state, gain_second)[0].astype(low)
    branch_own, branch_other, grad_own, grad_other, gate_grad, down_grad = feed(
        order, which, planes, units, normed_b, other_core(normed_b), cotangent, cot_other
    )
    facts = jnp.concatenate([lengths, place_one])
    state_grad, branch_grad, *asked = turn(
        facts, grad_own, before(other_core(grad_other), qkv_full), hidden_state, cotangent, pack,
        out_full, line, pairs,
    )
    branch_b = branch_own + other_core(branch_other)
    block_out = (hidden_state + branch_b).astype(low)

    def settle(grad):
        kept, given = halves(grad, -1)
        return by_core(core, kept[..., None, :, :], other_core(given)[..., None, :, :], -3)

    def plane_sum(grad):
        if chips != 4:
            return chip_scatter(grad).astype(wide)
        pieces = [
            lax.dynamic_slice_in_dim(grad, (chip ^ away) * 2 * width, 2 * width, 1)
            for away in range(chips)
        ]
        moved = [
            lax.ppermute(pieces[away], "chip", [(c, c ^ away) for c in range(chips)])
            for away in range(1, chips)
        ]
        return sum(piece.astype(wide) for piece in [pieces[0]] + moved)

    def spread(grad):
        if not lined:
            grad = grad.reshape(line, -1, chips, 2 * width).transpose(2, 0, 1, 3)
        return grad

    down_sum = lax.psum_scatter(spread(down_grad), "chip", scatter_dimension=0)
    def back(pair, came):
        return attend_back(
            pair, lengths, query, keys, values, came.reshape(line * rows, LANES),
            attended_wide[pair], log_total[pair], cosine, sine,
        )

    came = exchange(asked[0])
    kept, given = outer(core[None].astype(jnp.int32), attended_pieces, branch_grad)
    out_grad = (kept.astype(wide) + other_core(given).astype(wide)).astype(low)
    out_grad = jnp.moveaxis(out_grad.reshape(line, cols // 2, chips, 2 * width), 2, 0)
    gate_grad = spread(gate_grad).at[:, :, : cols // 2].set(out_grad)
    came, gate_grad, asked, down_sum, block_out = after(
        (came, gate_grad, asked, down_sum, block_out)
    )

    gate_sum = lax.psum_scatter(gate_grad, "chip", scatter_dimension=0)
    mixed_first = back(0, came)
    came = exchange(asked[1])
    down_came = exchange_turned(down_sum, place)
    came, mixed_first, down_came = after((came, mixed_first, down_came))

    mixed_second = back(1, came)
    mixed_rows = exchange(mixed_first[0].reshape(line, rows, 3 * LANES))
    mixed_rows, mixed_second = after((mixed_rows, mixed_second))

    came = exchange(mixed_second[0].reshape(line, rows, 3 * LANES))
    gate_came = exchange_turned(after(gate_sum), place)
    qkv_grad = unproject(normed_a, [mixed_first[0], mixed_second[0]])
    kept, given = halves(qkv_grad, 0)
    qkv_grad = (kept.astype(wide) + other_core(given).astype(wide)).astype(low)
    came, gate_came, qkv_grad = after((came, gate_came, qkv_grad))

    qkv_sum = settle(plane_sum(qkv_grad)).reshape(pairs, 3, LANES, width)
    mixer_in_grad = qkv_sum.transpose(1, 3, 0, 2).reshape(3, width, cols)
    normed_a_grad = jnp.einsum(
        "ztc,zcd->td", mixed_rows, qkv_full[:, 0], preferred_element_type=wide
    )
    tokens_grad = finish(came, qkv_full, normed_a_grad, tokens, pack, state_grad)
    down_sum = sum(piece.astype(wide) for piece in down_came)
    down_grad = settle(down_sum).reshape(2 * units, width)
    weights_sum = sum(piece.astype(wide) for piece in gate_came)
    mixer_out_grad = settle(weights_sum[: cols // 2]).reshape(cols, width)
    gate_up_grad = settle(weights_sum[cols // 2 :].reshape(2, units, 2 * width))
    gate_up_grad = gate_up_grad.reshape(2, 2 * units, width).transpose(0, 2, 1)

    gain_parts = jnp.stack(
        [
            jnp.sum(qkv_low.astype(wide) * mixer_in_grad, axis=(0, 2)),
            jnp.sum(gates_low.astype(wide) * gate_up_grad, axis=(0, 2)),
        ]
    )
    gains_grad = sum(exchange_turned(jnp.broadcast_to(gain_parts, (line, 2, width)), place))
    gains_grad = gains_grad / gain_low.astype(wide)
    first_grad = jnp.concatenate([mixed_first[1], mixed_second[1]], axis=1)
    return (
        block_out,
        tokens_grad,
        first_grad,
        mixer_in_grad,
        mixer_out_grad,
        gate_up_grad,
        down_grad,
        gains_grad,
    )


def solution(mesh):
    groups, line = mesh.shape["dp"], mesh.shape["head"]
    fine = jax.sharding.Mesh(
        mesh.devices.reshape(groups // 2, 2, line), ("chip", "core", "head")
    )
    dp = ("chip", "core")
    return jax.shard_map(
        shards,
        mesh=fine,
        in_specs=(
            P(("chip", "core", "head"), None),
            P(dp, "head"),
            P(None, dp, "head"),
            P("head", dp),
            P(None, dp, "head"),
            P("head", dp),
            P(None, dp),
            P(dp),
            P(("chip", "core", "head"), None),
        ),
        out_specs=(
            P(("chip", "core", "head"), None),
            P(("chip", "core", "head"), None),
            P(dp, "head"),
            P(None, dp, "head"),
            P("head", dp),
            P(None, dp, "head"),
            P("head", dp),
            P(None, dp),
        ),
        check_vma=False,
    )
```

```python
import functools

import jax
import jax.numpy as jnp
from jax import lax
from jax.experimental import pallas as pl
from jax.experimental.pallas import tpu as pltpu
from jax.sharding import PartitionSpec as P

HDIM = 64
SEQ = 2048
LANES = 128
GAIN_ROWS = 16

epsilon = 1e-05
far_below = -1e30
rope_base = 10000.0
low = jnp.bfloat16
wide = jnp.float32
VMEM_BYTES = 60 * 1024 * 1024


def dot_nn(a, b):
    return lax.dot_general(a, b, (((1,), (0,)), ((), ())), preferred_element_type=wide)


def dot_nt(a, b):
    return lax.dot_general(a, b, (((1,), (1,)), ((), ())), preferred_element_type=wide)


def dot_tn(a, b):
    return lax.dot_general(a, b, (((0,), (0,)), ((), ())), preferred_element_type=wide)


def rope_tables():
    half = HDIM // 2
    rates = rope_base ** (-jnp.arange(half, dtype=wide) * 2.0 / HDIM)
    angles = jnp.arange(SEQ, dtype=wide)[:, None] * rates[None, :]
    cosine, sine = jnp.cos(angles), jnp.sin(angles)
    pair = LANES // HDIM
    return (
        jnp.concatenate([cosine, cosine] * pair, axis=1),
        jnp.concatenate([-sine, sine] * pair, axis=1),
    )


def swap_halves(field):
    half = HDIM // 2
    lane = lax.broadcasted_iota(jnp.int32, field.shape, 1)
    ahead = pltpu.roll(field, LANES - half, 1)
    behind = pltpu.roll(field, half, 1)
    return jnp.where(lane % HDIM < half, ahead, behind)


def rms_parts(field, gain):
    factor = lax.rsqrt(jnp.mean(field * field, axis=-1, keepdims=True) + epsilon)
    unit = field * factor
    return (unit * gain, unit, factor)


def rms_back(normed_grad, unit, factor, gain):
    scaled = normed_grad * gain
    return factor * (scaled - unit * jnp.mean(scaled * unit, axis=-1, keepdims=True))


def project_kernel(place, x_ref, w_ref, gain_ref, first_ref, cos_ref, sin_ref, *refs):
    q_ref, k_ref, v_ref, normed_ref = refs[-4:]
    rows, depth = normed_ref.shape
    width = x_ref.shape[1]
    if width == depth:
        width = depth // 4
        blocks = [x_ref[:, start : start + width].astype(wide) for start in range(0, depth, width)]
    else:
        starts = range(0, x_ref.shape[0], rows)
        blocks = [x_ref[start : start + rows, :].astype(wide) for start in starts]
    squares = sum(jnp.sum(block * block, axis=-1, keepdims=True) for block in blocks)
    factor = lax.rsqrt(squares / depth + epsilon)
    for number, block in enumerate(blocks):
        cols = slice(number * width, (number + 1) * width)
        normed_ref[:, cols] = (block * factor * gain_ref[0:1, cols].astype(wide)).astype(low)
    normed = normed_ref[...]
    cosine, sine = cos_ref[...], sin_ref[...]
    for pair in range(q_ref.shape[1] // LANES):
        cols = slice(pair * LANES, (pair + 1) * LANES)
        start = pair * 3 * LANES
        mixed = dot_nt(normed, w_ref[start : start + 3 * LANES, :])
        for part, out_ref in ((0, q_ref), (1, k_ref)):
            piece = mixed[:, part * LANES : (part + 1) * LANES]
            out_ref[:, cols] = (piece * cosine + swap_halves(piece) * sine).astype(low)
        first = first_ref[:, cols].astype(wide)
        v_ref[:, cols] = (0.5 * mixed[:, 2 * LANES :] + 0.5 * first).astype(low)


def project(index, x, pack, first_values, cosine, sine, made):
    total, cols = first_values.shape
    depth = pack.shape[1]
    rows = x.shape[0] * x.shape[1] // depth
    gain_block = pack.shape[0] // GAIN_ROWS - 1
    fixed = lambda i, p: (0, 0)
    natural = lambda width: pl.BlockSpec((rows, width), lambda i, p: (p[0], 0))
    shapes = [cols, cols, cols, depth]
    spec = pltpu.PrefetchScalarGridSpec(
        num_scalar_prefetch=1,
        grid=(1,),
        in_specs=[
            pl.BlockSpec(x.shape, fixed),
            pl.BlockSpec((3 * cols, depth), fixed),
            pl.BlockSpec((GAIN_ROWS, depth), lambda i, p: (gain_block, 0)),
            natural(cols),
            natural(LANES),
            natural(LANES),
        ]
        + [pl.BlockSpec(memory_space=pl.ANY)] * len(made),
        out_specs=[natural(width) for width in shapes],
    )
    return pl.pallas_call(
        project_kernel,
        grid_spec=spec,
        out_shape=[jax.ShapeDtypeStruct((total, width), low) for width in shapes],
        input_output_aliases={7 + number: number for number in range(len(made))},
        compiler_params=pltpu.CompilerParams(vmem_limit_bytes=VMEM_BYTES),
        cost_estimate=pl.CostEstimate(
            flops=2 * rows * depth * 3 * cols, bytes_accessed=5 << 20, transcendentals=0
        ),
        name="project",
    )(index, x, pack, pack, first_values, cosine, sine, *made)


BLOCK = 512


def both_heads(array):
    lane = lax.broadcasted_iota(jnp.int32, array.shape, 1)
    zero = jnp.zeros_like(array)
    return jnp.concatenate(
        [jnp.where(lane < HDIM, array, zero), jnp.where(lane < HDIM, zero, array)], axis=0
    )


def attend_kernel(len_ref, q_ref, k_ref, v_ref, out_ref, full_ref, lse_ref, acc_ref, max_ref, sum_ref):
    i = pl.program_id(0)
    own = both_heads(q_ref[...] * jnp.asarray(HDIM**-0.5, low))
    max_ref[...] = jnp.full_like(max_ref, far_below)
    sum_ref[...] = jnp.zeros_like(sum_ref)
    acc_ref[...] = jnp.zeros_like(acc_ref)

    def step(j, diagonal):
        at = pl.ds(pl.multiple_of(j * BLOCK, BLOCK), BLOCK)
        scores = dot_nt(own, k_ref[at, :])
        if diagonal:
            q_at = lax.broadcasted_iota(jnp.int32, (BLOCK, BLOCK), 0)
            k_at = lax.broadcasted_iota(jnp.int32, (BLOCK, BLOCK), 1)
            allowed = k_at <= q_at
            allowed = jnp.concatenate([allowed, allowed], axis=0)
            scores = jnp.where(allowed, scores, far_below)
        old = max_ref[...]
        peak = jnp.maximum(old, jnp.max(scores, axis=1, keepdims=True))
        decay = jnp.exp(old - peak)
        max_ref[...] = peak
        total = sum_ref[...] * decay
        powers = []
        for start in range(0, BLOCK, LANES):
            power = jnp.exp(scores[:, start : start + LANES] - peak)
            total += power
            powers.append(power.astype(low))
        sum_ref[...] = total
        acc_ref[...] = acc_ref[...] * decay + dot_nn(jnp.concatenate(powers, axis=1), v_ref[at, :])

    @pl.loop(0, i)
    def _(j):
        step(j, False)

    step(i, True)
    total = jnp.sum(sum_ref[...], axis=1, keepdims=True)
    log_total = max_ref[...] + jnp.log(total)
    for head in range(LANES // HDIM):
        rows = slice(head * BLOCK, (head + 1) * BLOCK)
        lse_ref[head : head + 1, :] = jnp.transpose(log_total[rows])[0:1, :]
    result = acc_ref[...] / total
    lane = lax.broadcasted_iota(jnp.int32, (BLOCK, LANES), 1)
    valid = i * BLOCK + lax.broadcasted_iota(jnp.int32, (BLOCK, 1), 0) < len_ref[0]
    result = jnp.where(valid, jnp.where(lane < HDIM, result[:BLOCK], result[BLOCK:]), 0.0)
    out_ref[...] = result.astype(low)
    full_ref[...] = result


def attend(pair, lengths, query, keys, values):
    rows = query.shape[0]
    block = pl.BlockSpec((BLOCK, LANES), lambda i, n: (i, pair))
    whole = pl.BlockSpec((rows, LANES), lambda i, n: (0, pair))
    result = pl.BlockSpec((BLOCK, LANES), lambda i, n: (i, 0))
    spec = pltpu.PrefetchScalarGridSpec(
        num_scalar_prefetch=1,
        grid=(rows // BLOCK,),
        in_specs=[block, whole, whole],
        out_specs=[result, result, pl.BlockSpec((8, BLOCK), lambda i, n: (0, i))],
        scratch_shapes=[pltpu.VMEM((2 * BLOCK, LANES), wide)] * 3,
    )
    return pl.pallas_call(
        attend_kernel,
        grid_spec=spec,
        out_shape=[
            jax.ShapeDtypeStruct((rows, LANES), low),
            jax.ShapeDtypeStruct((rows, LANES), wide),
            jax.ShapeDtypeStruct((8, rows), wide),
        ],
        compiler_params=pltpu.CompilerParams(vmem_limit_bytes=VMEM_BYTES),
        cost_estimate=pl.CostEstimate(
            flops=8 * rows * rows * LANES, bytes_accessed=4 << 20, transcendentals=rows * rows
        ),
        name="attend",
    )(lengths, query, keys, values)


def attend_back_kernel(
    len_ref, q_ref, k_ref, v_ref, grad_ref, full_ref, lse_ref, cos_ref, sin_ref,
    mixed_ref, first_ref, dk_acc, dv_acc, dq_acc, keys_t,
):
    i = pl.program_id(0)
    count = pl.num_programs(0)
    heads = range(LANES // HDIM)

    @pl.when(i == 0)
    def _():
        dk_acc[...] = jnp.zeros_like(dk_acc)
        dv_acc[...] = jnp.zeros_like(dv_acc)
        for start in range(0, k_ref.shape[0], BLOCK):
            keys_t[:, start : start + BLOCK] = jnp.transpose(k_ref[start : start + BLOCK, :])

    grad = grad_ref[...]
    own = both_heads(q_ref[...] * jnp.asarray(HDIM**-0.5, low))
    own_grad = both_heads(grad)
    columns = [slice(head * HDIM, (head + 1) * HDIM) for head in heads]
    products = jnp.transpose(grad.astype(wide) * full_ref[...])
    offset = jnp.concatenate(
        [jnp.sum(products[rows], axis=0, keepdims=True) for rows in columns], axis=1
    )
    log_total = jnp.concatenate([lse_ref[head : head + 1, :] for head in heads], axis=1)
    dq_acc[...] = jnp.zeros_like(dq_acc)

    def step(j, diagonal):
        at = pl.ds(pl.multiple_of(j * BLOCK, BLOCK), BLOCK)
        scores = dot_nt(k_ref[at, :], own)
        if diagonal:
            k_at = lax.broadcasted_iota(jnp.int32, (BLOCK, BLOCK), 0)
            q_at = lax.broadcasted_iota(jnp.int32, (BLOCK, BLOCK), 1)
            allowed = k_at <= q_at
            allowed = jnp.concatenate([allowed, allowed], axis=1)
            scores = jnp.where(allowed, scores, far_below)
        probs = jnp.exp(scores - log_total)
        prob_grad = dot_nt(v_ref[at, :], own_grad)
        dv_acc[at, :] += dot_nn(probs.astype(low), own_grad)
        raw_grad = (probs * (prob_grad - offset)).astype(low)
        dk_acc[at, :] += dot_nn(raw_grad, own)
        for head, rows in zip(heads, columns):
            dq_acc[rows, :] += dot_nn(
                keys_t[rows, at], raw_grad[:, head * BLOCK : (head + 1) * BLOCK]
            )

    @pl.loop(0, i)
    def _(j):
        step(j, False)

    step(i, True)
    at = pl.ds(pl.multiple_of(i * BLOCK, BLOCK), BLOCK)
    query_grad = jnp.transpose(dq_acc[...]) * HDIM**-0.5
    mixed_ref[at, :LANES] = (
        query_grad * cos_ref[at, :] - swap_halves(query_grad) * sin_ref[at, :]
    ).astype(low)

    @pl.when(i == count - 1)
    def _():
        @pl.loop(0, count)
        def _(j):
            at = pl.ds(pl.multiple_of(j * BLOCK, BLOCK), BLOCK)
            keys_grad = dk_acc[at, :]
            mixed_ref[at, LANES : 2 * LANES] = (
                keys_grad * cos_ref[at, :] - swap_halves(keys_grad) * sin_ref[at, :]
            ).astype(low)
            half_grad = 0.5 * dv_acc[at, :]
            first_ref[at, :] = half_grad
            mixed_ref[at, 2 * LANES :] = half_grad.astype(low)


def attend_back(pair, lengths, query, keys, values, grad, full, lse, cosine, sine):
    rows = query.shape[0]
    block = pl.BlockSpec((BLOCK, LANES), lambda i, n: (i, pair))
    whole = pl.BlockSpec((rows, LANES), lambda i, n: (0, pair))
    given = pl.BlockSpec((BLOCK, LANES), lambda i, n: (i, 0))
    fixed = lambda i, n: (0, 0)
    table = pl.BlockSpec((rows, LANES), fixed)
    spec = pltpu.PrefetchScalarGridSpec(
        num_scalar_prefetch=1,
        grid=(rows // BLOCK,),
        in_specs=[
            block, whole, whole, given, given,
            pl.BlockSpec((8, BLOCK), lambda i, n: (0, i)),
            table, table,
        ],
        out_specs=[pl.BlockSpec((rows, 3 * LANES), fixed), pl.BlockSpec((rows, LANES), fixed)],
        scratch_shapes=[
            pltpu.VMEM((rows, LANES), wide),
            pltpu.VMEM((rows, LANES), wide),
            pltpu.VMEM((LANES, BLOCK), wide),
            pltpu.VMEM((LANES, rows), low),
        ],
    )
    return pl.pallas_call(
        attend_back_kernel,
        grid_spec=spec,
        out_shape=[
            jax.ShapeDtypeStruct((rows, 3 * LANES), low),
            jax.ShapeDtypeStruct((rows, LANES), wide),
        ],
        compiler_params=pltpu.CompilerParams(vmem_limit_bytes=VMEM_BYTES),
        cost_estimate=pl.CostEstimate(
            flops=20 * rows * rows * LANES, bytes_accessed=6 << 20, transcendentals=rows * rows
        ),
        name="attend_back",
    )(lengths, query, keys, values, grad, full, lse, cosine, sine)


def feed_kernel(order, which, *refs):
    given, (x_own, x_other, c_own, c_other) = refs[:-17], refs[-17:-13]
    outs, grads, dgate_ref, ddown_ref = refs[-13:-11], refs[-11:-9], refs[-9], refs[-8]
    weights, x_ref, c_ref, inner_s, mlp_s, weight_sems, row_sems = refs[-7:]
    step = pl.program_id(0)
    parts, depth3, depth = weights.shape
    pieces = len(given) // parts
    width = depth // pieces
    units = depth3 // 3
    rows = x_own.shape[0]
    skipped = given[0].shape[0] - depth3
    chunk = min(512, rows)
    sides = (slice(0, rows), slice(rows, 2 * rows))
    fetches = [
        [
            pltpu.make_async_copy(
                given[number * pieces + c].at[skipped:, :],
                weights.at[number, :, pl.ds(pl.multiple_of(which[c] * width, LANES), width)],
                weight_sems.at[number, c],
            )
            for c in range(pieces)
        ]
        for number in range(parts)
    ]
    loads = [
        pltpu.make_async_copy(source, target.at[side, :], row_sems.at[number])
        for number, (source, target, side) in enumerate(
            zip((x_own, x_other, c_own, c_other), (x_ref, x_ref, c_ref, c_ref), sides * 2)
        )
    ]

    @pl.when(step == 0)
    def _():
        for fetch in fetches[0]:
            fetch.start()
        for load in loads:
            load.start()
        for fetch in sum(fetches[1:], []):
            fetch.start()
        for ref in (*outs, *grads):
            ref[...] = jnp.zeros_like(ref)
        for load in loads:
            load.wait()

    for number in range(parts):

        @pl.when(step == number)
        def _(number=number):
            for fetch in fetches[number]:
                fetch.wait()

    w_ref = weights.at[step]
    for half, (out_ref, grad_ref) in enumerate(zip(outs, grads)):

        @pl.loop(0, rows // chunk)
        def _(t, half=half, out_ref=out_ref, grad_ref=grad_ref):
            at = pl.ds(pl.multiple_of(t * chunk, chunk), chunk)
            along = pl.ds(pl.multiple_of(half * rows + t * chunk, chunk), chunk)
            gated = dot_nt(w_ref[: 2 * units, :], x_ref[along, :])
            inner_grad = dot_nt(w_ref[2 * units :, :], c_ref[along, :])
            gate, up = gated[:units], gated[units:]
            sigmoid = jax.nn.sigmoid(gate)
            silu = gate * sigmoid
            inner = (silu * up).astype(low)
            gate_grad = (inner_grad * up * sigmoid * (1.0 + gate * (1.0 - sigmoid))).astype(low)
            up_grad = (inner_grad * silu).astype(low)
            inner_s[:, along] = inner
            mlp_s[:units, along] = gate_grad
            mlp_s[units:, along] = up_grad
            mlp_grad = jnp.concatenate([gate_grad, up_grad], axis=0)
            out_ref[at, :] += dot_tn(inner, w_ref[2 * units :, :])
            grad_ref[at, :] += dot_tn(mlp_grad, w_ref[: 2 * units, :])

    for c in range(pieces):
        cols = slice(c * width, (c + 1) * width)
        dgate_ref[c, 0, skipped:, :] = dot_nn(mlp_s[...], x_ref[:, cols]).astype(low)
        ddown_ref[c, 0] = dot_nn(inner_s[...], c_ref[:, cols]).astype(low)


def feed(order, which, slots, units, x_own, x_other, c_own, c_other):
    rows, depth = x_own.shape
    parts, pieces, width = len(slots), len(slots[0]), slots[0][0].shape[1]
    gates = slots[0][0].shape[0] - units
    anywhere = pl.BlockSpec(memory_space=pl.ANY)
    activations = pl.BlockSpec((rows, depth), lambda h, o, c: (0, 0), pipeline_mode=pl.Buffered(1))
    block = lambda height: pl.BlockSpec((pieces, 1, height, width), lambda h, o, c: (0, o[h], 0, 0))
    spec = pltpu.PrefetchScalarGridSpec(
        num_scalar_prefetch=2,
        grid=(parts,),
        in_specs=[anywhere] * (parts * pieces + 4),
        out_specs=[activations] * 4 + [block(gates), block(units)],
        scratch_shapes=[
            pltpu.VMEM((parts, 3 * units, depth), low),
            pltpu.VMEM((2 * rows, depth), low),
            pltpu.VMEM((2 * rows, depth), low),
            pltpu.VMEM((units, 2 * rows), low),
            pltpu.VMEM((2 * units, 2 * rows), low),
            pltpu.SemaphoreType.DMA((parts, pieces)),
            pltpu.SemaphoreType.DMA((4,)),
        ],
    )
    return pl.pallas_call(
        feed_kernel,
        grid_spec=spec,
        out_shape=[jax.ShapeDtypeStruct((rows, depth), wide)] * 4
        + [
            jax.ShapeDtypeStruct((pieces, parts, gates, width), low),
            jax.ShapeDtypeStruct((pieces, parts, units, width), low),
        ],
        compiler_params=pltpu.CompilerParams(vmem_limit_bytes=VMEM_BYTES),
        cost_estimate=pl.CostEstimate(
            flops=36 * rows * depth * units * parts,
            bytes_accessed=30 << 20,
            transcendentals=2 * rows * units * parts,
        ),
        name="feed",
    )(order, which, *sum(slots, []), x_own, x_other, c_own, c_other)


def collect_kernel(order, which, *refs):
    out_ref = refs[-1]
    height, width = refs[0].shape
    pieces = out_ref.shape[1] // width
    for number, ref in enumerate(refs[:-1]):
        part, piece = divmod(number, pieces)
        rows = pl.ds(pl.multiple_of(order[part] * height, height), height)
        out_ref[rows, pl.ds(pl.multiple_of(which[piece] * width, LANES), width)] = ref[...]


def collect(order, which, slots, height):
    parts, pieces, width = len(slots), len(slots[0]), slots[0][0].shape[1]
    spec = pltpu.PrefetchScalarGridSpec(
        num_scalar_prefetch=2,
        grid=(1,),
        in_specs=[pl.BlockSpec((height, width), lambda i, o, c: (0, 0))] * (parts * pieces),
        out_specs=pl.BlockSpec((parts * height, pieces * width), lambda i, o, c: (0, 0)),
    )
    return pl.pallas_call(
        collect_kernel,
        grid_spec=spec,
        out_shape=jax.ShapeDtypeStruct((parts * height, pieces * width), low),
        compiler_params=pltpu.CompilerParams(vmem_limit_bytes=VMEM_BYTES),
        cost_estimate=pl.CostEstimate(flops=0, bytes_accessed=2 << 20, transcendentals=0),
        name="collect",
    )(order, which, *sum(slots, []))


def join_kernel(right_ref, left_ref, w_ref, *outs):
    rows, depth = right_ref.shape
    width = w_ref.shape[1]
    cut = rows * depth // width
    for ref, out_ref in zip((right_ref, left_ref), outs):
        for number in range(depth // width):
            cols = slice(number * width, (number + 1) * width)
            out_ref[number * rows : (number + 1) * rows, :] = ref[:, cols]
        out_ref[cut:, :] = w_ref[...]


def join(right, left, weights):
    rows, depth = right.shape
    height, width = weights.shape
    shape = jax.ShapeDtypeStruct((rows * depth // width + height, width), low)
    return pl.pallas_call(
        join_kernel,
        out_shape=[shape] * 2,
        compiler_params=pltpu.CompilerParams(vmem_limit_bytes=VMEM_BYTES),
        cost_estimate=pl.CostEstimate(flops=0, bytes_accessed=7 << 20, transcendentals=0),
        name="join",
    )(right, left, weights)


def line_up_kernel(order, *refs):
    out_ref = refs[-1]
    height, width = refs[0].shape
    pairs = out_ref.shape[0] // height // (len(refs) - 1)
    each = width // pairs
    for number, ref in enumerate(refs[:-1]):
        for pair in range(pairs):
            start = (order[number] * pairs + pair) * height
            rows = pl.ds(pl.multiple_of(start, height), height)
            out_ref[rows, :] = ref[:, pair * each : (pair + 1) * each]


def line_up(order, arrived, pairs):
    height, width = arrived[0].shape
    shape = (len(arrived) * pairs * height, width // pairs)
    spec = pltpu.PrefetchScalarGridSpec(
        num_scalar_prefetch=1,
        grid=(1,),
        in_specs=[pl.BlockSpec((height, width), lambda i, o: (0, 0))] * len(arrived),
        out_specs=pl.BlockSpec(shape, lambda i, o: (0, 0)),
    )
    return pl.pallas_call(
        line_up_kernel,
        grid_spec=spec,
        out_shape=jax.ShapeDtypeStruct(shape, low),
        compiler_params=pltpu.CompilerParams(vmem_limit_bytes=VMEM_BYTES),
        cost_estimate=pl.CostEstimate(flops=0, bytes_accessed=2 << 20, transcendentals=0),
        name="line_up",
    )(order, *arrived)


def turn_kernel(facts, own_ref, came_ref, state_ref, c_ref, gain_ref, w_ref, grad_ref, low_ref, *asked):
    normed_grad = own_ref[...] + came_ref[...]
    gain = gain_ref[1:2, :].astype(wide)
    _, unit, factor = rms_parts(state_ref[...], gain)
    state_grad = c_ref[...].astype(wide) + rms_back(normed_grad, unit, factor, gain)
    branch_grad = state_grad.astype(low)
    grad_ref[...] = state_grad
    low_ref[...] = branch_grad
    chunk = own_ref.shape[0]
    start = facts[1] * chunk * pl.num_programs(0) + pl.program_id(0) * chunk
    valid = start + lax.broadcasted_iota(jnp.int32, (chunk, 1), 0) < facts[0]
    heads_grad = jnp.where(valid, dot_nt(branch_grad, w_ref[...]), 0.0).astype(low)
    line = asked[0].shape[0]
    for z in range(line):
        for pair, ref in enumerate(asked):
            column = (z * len(asked) + pair) * LANES
            ref[z] = heads_grad[:, column : column + LANES]


def turn(facts, own, came, hidden_state, cotangent, pack, out_full, line, pairs):
    rows, depth = own.shape
    chunk = rows // 2
    gain_block = pack.shape[0] // GAIN_ROWS - 1
    block = pl.BlockSpec((chunk, depth), lambda i, f: (i, 0))
    piece = pl.BlockSpec((line, chunk, LANES), lambda i, f: (0, i, 0))
    spec = pltpu.PrefetchScalarGridSpec(
        num_scalar_prefetch=1,
        grid=(rows // chunk,),
        in_specs=[
            block, block, block, block,
            pl.BlockSpec((GAIN_ROWS, depth), lambda i, f: (gain_block, 0)),
            pl.BlockSpec((depth, depth), lambda i, f: (0, 0)),
        ],
        out_specs=[block, block] + [piece] * pairs,
    )
    return pl.pallas_call(
        turn_kernel,
        grid_spec=spec,
        out_shape=[
            jax.ShapeDtypeStruct((rows, depth), wide),
            jax.ShapeDtypeStruct((rows, depth), low),
        ]
        + [jax.ShapeDtypeStruct((line, rows, LANES), low)] * pairs,
        compiler_params=pltpu.CompilerParams(vmem_limit_bytes=VMEM_BYTES),
        cost_estimate=pl.CostEstimate(
            flops=2 * rows * depth * depth, bytes_accessed=13 << 20, transcendentals=0
        ),
        name="turn",
    )(facts, own, came, hidden_state, cotangent, pack, out_full)


def outer_kernel(core, first_ref, second_ref, grad_ref, kept_ref, given_ref):
    grad = grad_ref[...]
    first = dot_tn(first_ref[0], grad).astype(low)
    second = dot_tn(second_ref[0], grad).astype(low)
    lower = core[0] == 0
    kept_ref[0] = jnp.where(lower, first, second)
    given_ref[0] = jnp.where(lower, second, first)


def outer(core, attended_pieces, branch_grad):
    line, rows, width = attended_pieces[0].shape
    depth = branch_grad.shape[1]
    piece = pl.BlockSpec((1, rows, width), lambda z, c: (z, 0, 0))
    out = pl.BlockSpec((1, width, depth), lambda z, c: (z, 0, 0))
    spec = pltpu.PrefetchScalarGridSpec(
        num_scalar_prefetch=1,
        grid=(line,),
        in_specs=[piece, piece, pl.BlockSpec((rows, depth), lambda z, c: (0, 0))],
        out_specs=[out, out],
    )
    return pl.pallas_call(
        outer_kernel,
        grid_spec=spec,
        out_shape=[jax.ShapeDtypeStruct((line, width, depth), low)] * 2,
        compiler_params=pltpu.CompilerParams(vmem_limit_bytes=VMEM_BYTES),
        cost_estimate=pl.CostEstimate(flops=0, bytes_accessed=0, transcendentals=0),
        name="outer",
    )(core, *attended_pieces, branch_grad)


def unproject_kernel(normed_ref, *refs):
    mixed_refs, (dw_ref, acc_ref) = refs[:-2], refs[-2:]
    step = pl.program_id(0)

    @pl.when(step == 0)
    def _():
        acc_ref[...] = jnp.zeros_like(acc_ref)

    height = mixed_refs[0].shape[1]
    for number, ref in enumerate(mixed_refs):
        acc_ref[number * height : (number + 1) * height, :] += dot_tn(ref[...], normed_ref[...])

    @pl.when(step == pl.num_programs(0) - 1)
    def _():
        dw_ref[...] = acc_ref[...].astype(low)


def unproject(normed, mixed_grads):
    tokens, depth = normed.shape
    rows = 512
    height = mixed_grads[0].shape[1]
    total = height * len(mixed_grads)
    block = lambda width: pl.BlockSpec((rows, width), lambda o: (o, 0))
    return pl.pallas_call(
        unproject_kernel,
        grid=(tokens // rows,),
        in_specs=[block(depth)] + [block(height)] * len(mixed_grads),
        out_specs=pl.BlockSpec((total, depth), lambda o: (0, 0)),
        scratch_shapes=[pltpu.VMEM((total, depth), wide)],
        out_shape=jax.ShapeDtypeStruct((total, depth), low),
        compiler_params=pltpu.CompilerParams(vmem_limit_bytes=VMEM_BYTES),
        cost_estimate=pl.CostEstimate(flops=0, bytes_accessed=0, transcendentals=0),
        name="unproject",
    )(normed, *mixed_grads)


def finish_kernel(came_ref, w_ref, part_ref, x_ref, gain_ref, state_ref, out_ref):
    normed_grad = part_ref[...]
    for number in range(came_ref.shape[0]):
        normed_grad += dot_nn(came_ref[number], w_ref[number, 0])
    gain = gain_ref[0:1, :].astype(wide)
    _, unit, factor = rms_parts(x_ref[...].astype(wide), gain)
    out_ref[...] = state_ref[...] + rms_back(normed_grad, unit, factor, gain)


def finish(came, qkv_full, part, tokens, pack, state_grad):
    line, rows, height = came.shape
    pairs, depth = qkv_full.shape[1], qkv_full.shape[3]
    gain_block = pack.shape[0] // GAIN_ROWS - 1
    chunk = rows // 2
    block = pl.BlockSpec((chunk, depth), lambda i: (i, 0))
    return pl.pallas_call(
        finish_kernel,
        grid=(rows // chunk,),
        in_specs=[
            pl.BlockSpec((line, chunk, height), lambda i: (0, i, 0)),
            pl.BlockSpec((line, 1, height, depth), lambda i: (0, pairs - 1, 0, 0)),
            block,
            block,
            pl.BlockSpec((GAIN_ROWS, depth), lambda i: (gain_block, 0)),
            block,
        ],
        out_specs=block,
        out_shape=jax.ShapeDtypeStruct((rows, depth), wide),
        compiler_params=pltpu.CompilerParams(vmem_limit_bytes=VMEM_BYTES),
        cost_estimate=pl.CostEstimate(
            flops=2 * line * rows * height * depth, bytes_accessed=10 << 20, transcendentals=0
        ),
        name="finish",
    )(came, qkv_full, part, tokens, pack, state_grad)


def arrival_order(place):
    ways = jnp.where(place < 2, 1, -1)
    far = jnp.where(place % 2 == 0, 3, 0)
    return jnp.stack([place, place + ways, place + 2 * ways, far]).astype(jnp.int32)


def gather_all(tokens, weights, end, place, chips, use, then, send):
    near = place < 2
    rows, depth = tokens.shape
    width = weights.shape[1]
    cut = rows * depth // width

    def hop(ends):
        return (
            lax.ppermute(ends[0], "head", [(0, 1), (1, 2), (2, 3)]),
            lax.ppermute(ends[1], "head", [(1, 0), (2, 1), (3, 2)]),
        )

    def nearest(hops):
        return jnp.where(near, hops[-1][1], hops[-1][0])

    def farthest(hops):
        return jnp.where(
            place % 3 == 0, nearest(hops), jnp.where(near, hops[0][0], hops[0][1])
        )

    def plane(slot):
        if chips != 4:
            return [lax.all_gather(slot[:end], "chip", axis=1, tiled=True)]
        return [slot[:end]] + [
            lax.ppermute(slot[:end], "chip", [(c, c ^ away) for c in range(chips)])
            for away in range(1, chips)
        ]

    barrier = lax.optimization_barrier
    slots, planes = [weights], []
    token_hops, weight_hops = [], []
    ends = barrier(hop((tokens, tokens)))
    first_block = nearest([ends])
    ends = tuple(join(*ends, weights))
    token_hops.append(tuple(end[:cut] for end in ends))

    ends = hop(ends)
    planes.append(plane(weights))
    used = use(0, tokens, None)
    ends, planes, used = barrier((ends, planes, used))
    token_hops.append(tuple(end[:cut] for end in ends))
    weight_hops.append(tuple(end[cut:] for end in ends))
    slots.append(nearest(weight_hops))
    second_block = nearest(token_hops)

    ends = hop(ends)
    planes.append(plane(slots[1]))
    used = use(1, first_block, used)
    used = use(2, second_block, used)
    ends, planes, used = barrier((ends, planes, used))
    token_hops.append(tuple(end[:cut] for end in ends))
    weight_hops.append(tuple(end[cut:] for end in ends))
    slots.append(nearest(weight_hops))
    used = use(3, farthest(token_hops), used)

    ends = hop(weight_hops[-1])
    planes.append(plane(slots[2]))
    made, used = then(0, used)
    ends, planes, made, used = barrier((ends, planes, made, used))
    sent = [send(made[0])]
    weight_hops.append(ends)
    slots.append(farthest(weight_hops))
    planes.append(plane(slots[3]))
    more, used = then(1, used)
    later = more[0]
    planes, more, sent = barrier((planes, more, sent))
    sent.append(send(barrier((later, sent[0]))[0]))
    planes, sent = barrier((planes, sent))
    return planes, slots, used, [made, more], sent


def exchange(pieces):
    return lax.all_to_all(pieces, "head", split_axis=0, concat_axis=0)


def exchange_turned(pieces, place):
    count = pieces.shape[0]
    came = []
    for j in range(count):
        piece = lax.dynamic_index_in_dim(pieces, (place + j) % count, 0, keepdims=False)
        came.append(
            lax.ppermute(piece, "head", [(k, (k + j) % count) for k in range(count)]) if j else piece
        )
    return came


def other_core(array):
    return lax.ppermute(array, "core", [(0, 1), (1, 0)])


def by_core(core, own, came, axis):
    first = jnp.where(core == 0, own, came)
    second = jnp.where(core == 0, came, own)
    return jnp.concatenate([first, second], axis=axis)


def shards(
    tokens, first_values, mixer_in, mixer_out, gate_up, down_weight, norm_gains, lengths, cotangent
):
    line = lax.axis_size("head")
    chips = lax.axis_size("chip")
    place = lax.axis_index("head")
    core = lax.axis_index("core")
    rows, depth = tokens.shape
    cols = mixer_in.shape[2]
    width = mixer_in.shape[1]
    units = down_weight.shape[0] // 2
    pairs = cols // LANES
    after = lax.optimization_barrier

    def halves(array, axis):
        first, second = jnp.split(array, 2, axis=axis)
        return jnp.where(core == 0, first, second), jnp.where(core == 0, second, first)

    def chip_scatter(grad):
        grad = grad.reshape(*grad.shape[:-1], chips, 2 * width)
        return lax.psum_scatter(jnp.moveaxis(grad, -2, 0), "chip", scatter_dimension=0)

    def before(given, *results):
        return after((given, *results))[0]

    qkv_low = mixer_in.astype(low)
    gain_low = norm_gains.astype(low)
    gain_rows = jnp.pad(gain_low, ((0, GAIN_ROWS - 2), (0, 0)))
    qkv_rows = qkv_low.reshape(3, width, pairs, LANES).transpose(2, 0, 3, 1)
    qkv_rows = qkv_rows.reshape(3 * cols, width)
    pack = lax.all_gather(
        jnp.concatenate([qkv_rows, gain_rows], axis=0), ("chip", "core"), axis=1, tiled=True
    )
    gain_second = pack[3 * cols + 1].astype(wide)

    gates_low = gate_up.astype(low)
    feed_rows = jnp.concatenate(
        [gates_low.transpose(0, 2, 1), down_weight.astype(low)[None]], axis=0
    ).reshape(3, 2, units, width)
    out_low = mixer_out.astype(low).reshape(2, cols // 2, width)

    def half_rows(which):
        return jnp.concatenate([out_low[which], feed_rows[:, which].reshape(3 * units, width)])

    first_rows, second_rows = half_rows(0), half_rows(1)
    own_rows = jnp.where(core == 0, first_rows, second_rows)
    other_rows = jnp.where(core == 0, second_rows, first_rows)
    own_rows = by_core(core, own_rows, other_core(other_rows), -1)
    end = own_rows.shape[0]
    qkv_sides = jnp.concatenate(jnp.split(qkv_rows, pairs), axis=-1)
    weights = jnp.concatenate([own_rows, qkv_sides])

    order = arrival_order(place)
    place_one = place[None].astype(jnp.int32)
    chip = lax.axis_index("chip")
    which = (chip ^ jnp.arange(4) if chips == 4 else jnp.zeros(1)).astype(jnp.int32)
    cosine, sine = rope_tables()

    def use(number, x, made):
        index = order[number : number + 1]
        return project(index, x, pack, first_values, cosine, sine, made or [])

    def then(pair, made):
        return attend(pair, lengths, *made[:3]), made

    def send(result):
        return exchange(result.reshape(line, rows, LANES))

    planes, slots, made, attended_parts, attended_pieces = gather_all(
        tokens, weights, end, place, chips, use, then, send
    )
    query, keys, values, normed_a = made
    cot_other = other_core(cotangent)
    out_half = collect(order, which, planes, cols // 2).reshape(line, 1, cols // 2, depth)
    qkv_sides, out_half = after(([slot[end:] for slot in slots], out_half))
    out_heads = by_core(core, out_half, other_core(out_half), 1)
    out_full = out_heads.reshape(depth, depth)
    lined = chips == 4
    attended_wide = [part[1] for part in attended_parts]
    log_total = [part[2] for part in attended_parts]
    attended = jnp.stack(attended_pieces, axis=1).transpose(2, 0, 1, 3).reshape(rows, depth)

    qkv_line = line_up(order, qkv_sides, pairs)
    qkv_full = lax.all_gather(qkv_line, ("chip", "core"), axis=1, tiled=True)
    qkv_full = qkv_full.reshape(line, pairs, 3 * LANES, depth)

    token_rows = tokens.astype(wide)
    hidden_state = token_rows + dot_nn(attended, out_full)
    normed_b = rms_parts(hidden_state, gain_second)[0].astype(low)
    branch_own, branch_other, grad_own, grad_other, gate_grad, down_grad = feed(
        order, which, planes, units, normed_b, other_core(normed_b), cotangent, cot_other
    )
    facts = jnp.concatenate([lengths, place_one])
    state_grad, branch_grad, *asked = turn(
        facts, grad_own, before(other_core(grad_other), qkv_full), hidden_state, cotangent, pack,
        out_full, line, pairs,
    )
    branch_b = branch_own + other_core(branch_other)
    block_out = (hidden_state + branch_b).astype(low)

    def settle(grad):
        kept, given = halves(grad, -1)
        return by_core(core, kept[..., None, :, :], other_core(given)[..., None, :, :], -3)

    def plane_sum(grad):
        if chips != 4:
            return chip_scatter(grad).astype(wide)
        pieces = [
            lax.dynamic_slice_in_dim(grad, (chip ^ away) * 2 * width, 2 * width, 1)
            for away in range(chips)
        ]
        moved = [
            lax.ppermute(pieces[away], "chip", [(c, c ^ away) for c in range(chips)])
            for away in range(1, chips)
        ]
        return sum(piece.astype(wide) for piece in [pieces[0]] + moved)

    def spread(grad):
        if not lined:
            grad = grad.reshape(line, -1, chips, 2 * width).transpose(2, 0, 1, 3)
        return grad

    down_sum = lax.psum_scatter(spread(down_grad), "chip", scatter_dimension=0)
    def back(pair, came):
        return attend_back(
            pair, lengths, query, keys, values, came.reshape(line * rows, LANES),
            attended_wide[pair], log_total[pair], cosine, sine,
        )

    came = exchange(asked[0])
    kept, given = outer(core[None].astype(jnp.int32), attended_pieces, branch_grad)
    out_grad = (kept.astype(wide) + other_core(given).astype(wide)).astype(low)
    out_grad = jnp.moveaxis(out_grad.reshape(line, cols // 2, chips, 2 * width), 2, 0)
    gate_grad = spread(gate_grad).at[:, :, : cols // 2].set(out_grad)
    came, gate_grad, asked, down_sum, block_out = after(
        (came, gate_grad, asked, down_sum, block_out)
    )

    gate_sum = lax.psum_scatter(gate_grad, "chip", scatter_dimension=0)
    mixed_first = back(0, came)
    came = exchange(asked[1])
    down_came = exchange_turned(down_sum, place)
    came, mixed_first, down_came = after((came, mixed_first, down_came))

    mixed_second = back(1, came)
    mixed_rows = exchange(mixed_first[0].reshape(line, rows, 3 * LANES))
    mixed_rows, mixed_second = after((mixed_rows, mixed_second))

    came = exchange(mixed_second[0].reshape(line, rows, 3 * LANES))
    gate_came = exchange_turned(after(gate_sum), place)
    qkv_grad = unproject(normed_a, [mixed_first[0], mixed_second[0]])
    kept, given = halves(qkv_grad, 0)
    qkv_grad = (kept.astype(wide) + other_core(given).astype(wide)).astype(low)
    came, gate_came, qkv_grad = after((came, gate_came, qkv_grad))

    qkv_sum = settle(plane_sum(qkv_grad)).reshape(pairs, 3, LANES, width)
    mixer_in_grad = qkv_sum.transpose(1, 3, 0, 2).reshape(3, width, cols)
    normed_a_grad = jnp.einsum(
        "ztc,zcd->td", mixed_rows, qkv_full[:, 0], preferred_element_type=wide
    )
    tokens_grad = finish(came, qkv_full, normed_a_grad, tokens, pack, state_grad)
    down_sum = sum(piece.astype(wide) for piece in down_came)
    down_grad = settle(down_sum).reshape(2 * units, width)
    weights_sum = sum(piece.astype(wide) for piece in gate_came)
    mixer_out_grad = settle(weights_sum[: cols // 2]).reshape(cols, width)
    gate_up_grad = settle(weights_sum[cols // 2 :].reshape(2, units, 2 * width))
    gate_up_grad = gate_up_grad.reshape(2, 2 * units, width).transpose(0, 2, 1)

    gain_parts = jnp.stack(
        [
            jnp.sum(qkv_low.astype(wide) * mixer_in_grad, axis=(0, 2)),
            jnp.sum(gates_low.astype(wide) * gate_up_grad, axis=(0, 2)),
        ]
    )
    gains_grad = sum(exchange_turned(jnp.broadcast_to(gain_parts, (line, 2, width)), place))
    gains_grad = gains_grad / gain_low.astype(wide)
    first_grad = jnp.concatenate([mixed_first[1], mixed_second[1]], axis=1)
    return (
        block_out,
        tokens_grad,
        first_grad,
        mixer_in_grad,
        mixer_out_grad,
        gate_up_grad,
        down_grad,
        gains_grad,
    )


def solution(mesh):
    groups, line = mesh.shape["dp"], mesh.shape["head"]
    fine = jax.sharding.Mesh(
        mesh.devices.reshape(groups // 2, 2, line), ("chip", "core", "head")
    )
    dp = ("chip", "core")
    return jax.shard_map(
        shards,
        mesh=fine,
        in_specs=(
            P(("chip", "core", "head"), None),
            P(dp, "head"),
            P(None, dp, "head"),
            P("head", dp),
            P(None, dp, "head"),
            P("head", dp),
            P(None, dp),
            P(dp),
            P(("chip", "core", "head"), None),
        ),
        out_specs=(
            P(("chip", "core", "head"), None),
            P(("chip", "core", "head"), None),
            P(dp, "head"),
            P(None, dp, "head"),
            P("head", dp),
            P(None, dp, "head"),
            P("head", dp),
            P(None, dp),
        ),
        check_vma=False,
    )
```
